32 devices in a mesh: dp: 8 (over y, x, core), img: 4 (over z).
Axes of the slice: x: 2, y: 2, z: 4, core: 2. Of those that a mesh axis runs over, the one named last changes fastest.
Arguments:
- tokens: bfloat16 [256, 64, 768], P(('dp', 'img')), may hold values from -3 to 3
- image_tokens: bfloat16 [256, 256, 768], P('dp', 'img'), may hold values from -4 to 4
- token_counts: int32 [256], P('dp'), may hold values from 1 to 256, 40960 in all
- self_qkv: bfloat16 [768, 2304], P('dp', 'img'), may hold values from -0.21875 to 0.21875
- self_out: bfloat16 [768, 768], P('dp', 'img'), may hold values from -0.4375 to 0.4375
- cross_q: bfloat16 [768, 768], P('dp', 'img'), may hold values from -0.21875 to 0.21875
- cross_kv: bfloat16 [768, 1536], P('dp', 'img'), may hold values from -0.21875 to 0.21875
- cross_out: bfloat16 [768, 768], P('dp', 'img'), may hold values from -0.625 to 0.625
- mlp_in: bfloat16 [768, 3072], P('dp', 'img'), may hold values from -0.21875 to 0.21875
- mlp_out: bfloat16 [3072, 768], P('dp', 'img'), may hold values from -0.109375 to 0.109375
- norm_gains: float32 [3, 768], P(None, 'dp'), may hold values from 0.25 to 1.75
- shifts: float32 [10, 768], P(None, 'dp'), may hold values from -1 to 1
- mlp_bias: float32 [3072], P('dp'), may hold values from -1 to 1
- cotangent: bfloat16 [256, 64, 768], P(('dp', 'img')), may hold values from -8 to 8
Outputs:
- layer_out: bfloat16 [256, 64, 768], P(('dp', 'img'))
- token_grads: bfloat16 [256, 64, 768], P(('dp', 'img'))
- image_grads: bfloat16 [256, 256, 768], P('dp', 'img')
- g_self_qkv: float32 [768, 2304], P('dp', 'img')
- g_self_out: float32 [768, 768], P('dp', 'img')
- g_cross_q: float32 [768, 768], P('dp', 'img')
- g_cross_kv: float32 [768, 1536], P('dp', 'img')
- g_cross_out: float32 [768, 768], P('dp', 'img')
- g_mlp_in: float32 [768, 3072], P('dp', 'img')
- g_mlp_out: float32 [3072, 768], P('dp', 'img')
- g_norm_gains: float32 [3, 768], P(None, 'dp')
- g_shifts: float32 [10, 768], P(None, 'dp')
- g_mlp_bias: float32 [3072], P('dp')
The draws below stay inside these ranges and needn't reach their ends.
Inputs may be any that keep to these rules, and one draw needn't show every extreme that they name: The first token_counts[c] pooled tokens of caption c's image are valid; some image has all 256 valid.
All inputs are finite; a program needn't handle non-finite values. No bound on the sum of `token_counts` on one device may be relied on, other than what follows from the above.
Results may differ from the reference program's by a relative error of at most 0.03.
Values may be sent and summed in bfloat16 or wider, within the bound.
A program may use at most 192 MiB of HBM per device.

```python
import math
import jax
import jax.numpy as jnp
import numpy as np
from jax import lax

MODEL_WIDTH = 768
HEADS = 12
HEAD = 64
FF = 3072
IMG_TOK = 256
SEQ = 64
CAP_DEV = 8
CAPTIONS = 256
N_IMG = 4


def spiked(entries, stream_key, source, target, blocks, factor):
    def block_of(axis_at):
        return (jnp.arange(entries.shape[axis_at]) // (entries.shape[axis_at] // blocks)).reshape((-1,) + (1,) * (entries.ndim - 1 - axis_at))

    one_side = jax.random.permutation(stream_key, blocks)[block_of(target)]
    other_side = (block_of(target) + blocks // 2) % blocks
    return jnp.where((block_of(source) == one_side) | (block_of(source) == other_side), factor * entries, entries)


def levels(stream_key, shape, shards, low, largest):
    factor_of, own = 1.0, jax.random.fold_in(stream_key, 6)
    for axis_at, shards_of in shards:
        steps = jnp.exp(jax.random.uniform(jax.random.fold_in(own, axis_at), (shards_of,), jnp.float32, low / len(shards), largest / len(shards)))
        factor_of = factor_of * jnp.repeat(steps, shape[axis_at] // shards_of).reshape([-1 if axis == axis_at else 1 for axis in range(len(shape))])
    return factor_of


def split_up(count, total, limit, slope):
    weights = [(1 << 20) // math.isqrt(standing ** slope) + 1 for standing in range(2, count + 1)]
    rest, given = total - limit - (count - 1), [1] * (count - 1)
    while rest > 0:
        movable = [i for i in range(count - 1) if given[i] < limit]
        mass, remaining = sum([weights[i] for i in movable]), rest
        for i in movable:
            extra = min(limit - given[i], max(1, remaining * weights[i] // mass), rest)
            given[i] = given[i] + extra
            rest = rest - extra
    return np.array([limit] + given)


def ragged(rng, number_of, total, reach, skew):
    if number_of == 2:
        one = jax.random.randint(rng, (), max(1, total - reach), min(reach, total - 1) + 1)
        return jnp.stack([one, total - one])
    lengths = jnp.asarray(split_up(number_of, total, reach, skew), jnp.int32)
    twos = (number_of - 1) // 2
    donor, receiver = lengths[1:1 + 2 * twos:2], lengths[2:2 + 2 * twos:2]
    slack = jnp.minimum(donor - 1, reach - receiver)
    passed = jax.random.randint(jax.random.fold_in(rng, 1), (twos,), 0, 1 << 20) % (slack + 1)
    lengths = lengths.at[1:1 + 2 * twos:2].set(donor - passed).at[2:2 + 2 * twos:2].set(receiver + passed)
    return lengths[jax.random.permutation(jax.random.fold_in(rng, 2), number_of)]


def scatter_about(stream_key, shape, width, limit, split=(), held_as=jnp.bfloat16):
    values = jax.random.normal(stream_key, shape, jnp.float32) * width
    if len(split) > 0:
        values = levels(stream_key, shape, split, -0.22, 0.18) * values
    return jnp.clip(values, min=-limit, max=limit).astype(held_as)


def noise_with(own_key, extent, width, most, shards, heavy, kind=jnp.bfloat16):
    entries = width * jax.random.normal(own_key, extent, jnp.float32)
    if shards:
        entries = entries * levels(own_key, extent, shards, -0.22, 0.18)
    return jnp.clip(spiked(entries, jax.random.fold_in(own_key, 3), *heavy), -most, most).astype(kind)


def setup_inputs(seed: int = 0) -> dict:
    arg_keys = jax.random.split(jax.random.key(seed), 15)
    tokens = scatter_about(arg_keys[0], (CAPTIONS, SEQ, MODEL_WIDTH), 0.8, 3.0, ((0, 32),))
    image_tokens = scatter_about(arg_keys[1], (CAPTIONS, IMG_TOK, MODEL_WIDTH), 1.0, 4.0, ((0, 8), (1, 4)))
    token_counts = ragged(arg_keys[2], CAPTIONS, 5 * CAPTIONS * IMG_TOK // 8, IMG_TOK, 0).astype(jnp.int32)
    self_qkv = scatter_about(arg_keys[3], (MODEL_WIDTH, 3 * MODEL_WIDTH), MODEL_WIDTH ** -0.5, 0.21875, ((0, 8), (1, 4)))
    self_out = scatter_about(arg_keys[4], (MODEL_WIDTH, MODEL_WIDTH), (MODEL_WIDTH // 4) ** -0.5, 0.4375, ((0, 8), (1, 4)))
    cross_q = scatter_about(arg_keys[5], (MODEL_WIDTH, MODEL_WIDTH), MODEL_WIDTH ** -0.5, 0.21875, ((0, 8), (1, 4)))
    cross_kv = scatter_about(arg_keys[6], (MODEL_WIDTH, 2 * MODEL_WIDTH), MODEL_WIDTH ** -0.5, 0.21875, ((0, 8), (1, 4)))
    cross_out = scatter_about(arg_keys[7], (MODEL_WIDTH, MODEL_WIDTH), (MODEL_WIDTH // 8) ** -0.5, 0.625, ((0, 8), (1, 4)))
    mlp_in = scatter_about(arg_keys[8], (MODEL_WIDTH, FF), MODEL_WIDTH ** -0.5, 0.21875, ((0, 8), (1, 4)))
    mlp_out = scatter_about(arg_keys[9], (FF, MODEL_WIDTH), FF ** -0.5, 0.109375, ((0, 8), (1, 4)))
    norm_gains = jnp.clip(1.0 + 0.15 * jax.random.normal(arg_keys[10], (3, MODEL_WIDTH), jnp.float32), 0.25, 1.75)
    shifts = scatter_about(arg_keys[11], (10, MODEL_WIDTH), 0.2, 1.0, ((1, 8),), jnp.float32)
    mlp_bias = scatter_about(arg_keys[12], (FF,), 0.2, 1.0, ((0, 8),), jnp.float32)
    cotangent = noise_with(arg_keys[13], (CAPTIONS, SEQ, MODEL_WIDTH), 0.7, 8.0, ((0, 32),), (0, 2, 32, 2.75))
    return dict(tokens=tokens, image_tokens=image_tokens, token_counts=token_counts, self_qkv=self_qkv, self_out=self_out, cross_q=cross_q, cross_kv=cross_kv, cross_out=cross_out, mlp_in=mlp_in, mlp_out=mlp_out, norm_gains=norm_gains, shifts=shifts, mlp_bias=mlp_bias, cotangent=cotangent)


@jax.custom_vjp
def low(v):
    return lax.optimization_barrier(v.astype(jnp.bfloat16)).astype(jnp.float32)

@jax.custom_vjp
def low_back(v):
    return v

def low_keep(v):
    return (low(v), None)

def low_pass(kept, grad):
    return (grad,)

def back_keep(v):
    return (v, None)

def back_low(kept, grad):
    return (low(grad),)
low.defvjp(low_keep, low_pass)
low_back.defvjp(back_keep, back_low)
masked_value = -1e+30
norm_epsilon = 1e-05

def product(left_op, right_op):
    return jnp.dot(left_op, right_op, precision=lax.Precision.HIGHEST, preferred_element_type=jnp.float32)

def layer_norm(values, norm_gain, norm_shift):
    average = lax.optimization_barrier(jnp.mean(values, axis=-1, keepdims=True))
    centred = values - average
    spread = lax.optimization_barrier(jnp.mean(centred * centred, axis=-1, keepdims=True))
    return centred * lax.rsqrt(spread + norm_epsilon) * norm_gain + norm_shift

def both_low(values):
    return low(low_back(values))

def attend(queries, key_heads, value_heads, allowed):
    score_scale = HEAD ** (-0.5)
    scores = low_back(jnp.einsum('cqhd,ckhd->chqk', queries, key_heads, precision=lax.Precision.HIGHEST) * score_scale)
    attn_probs = low(jax.nn.softmax(jnp.where(allowed, scores, masked_value), axis=-1))
    mixed_heads = jnp.einsum('chqk,ckhd->cqhd', attn_probs, value_heads, precision=lax.Precision.HIGHEST)
    return both_low(mixed_heads.reshape(-1, MODEL_WIDTH))

def forward(params, text_rows, image_rows, counts):
    qkv_w, sout_w, cq_w, ckv_w, cout_w, in_w, outm_w, gain_rows, shift_rows, inner_bias = params
    captions = text_rows.shape[0]
    rows = text_rows.reshape(-1, MODEL_WIDTH)
    zero_row = jnp.zeros((MODEL_WIDTH,), jnp.float32)
    normed = low(layer_norm(rows, gain_rows[0], shift_rows[0]))
    mixed_qkv = both_low(product(normed, qkv_w) + jnp.concatenate([shift_rows[3], zero_row, shift_rows[4]]))
    queries = mixed_qkv[:, :MODEL_WIDTH].reshape(captions, SEQ, HEADS, HEAD)
    key_heads = mixed_qkv[:, MODEL_WIDTH:2 * MODEL_WIDTH].reshape(captions, SEQ, HEADS, HEAD)
    value_heads = mixed_qkv[:, 2 * MODEL_WIDTH:].reshape(captions, SEQ, HEADS, HEAD)
    places = jnp.arange(SEQ, dtype=jnp.int32)
    causal = (places[None, :] <= places[:, None])[None, None]
    attended = attend(queries, key_heads, value_heads, causal)
    first_sum = rows + low_back(product(attended, sout_w) + shift_rows[5])
    normed = low(layer_norm(first_sum, gain_rows[1], shift_rows[1]))
    cross_queries = both_low(product(normed, cq_w) + shift_rows[6]).reshape(captions, SEQ, HEADS, HEAD)
    image_kv = both_low(product(image_rows.reshape(-1, MODEL_WIDTH), ckv_w) + jnp.concatenate([zero_row, shift_rows[7]]))
    cross_keys = image_kv[:, :MODEL_WIDTH].reshape(captions, IMG_TOK, HEADS, HEAD)
    cross_values = image_kv[:, MODEL_WIDTH:].reshape(captions, IMG_TOK, HEADS, HEAD)
    valid_keys = (jnp.arange(IMG_TOK, dtype=jnp.int32)[None, :] < counts[:, None])[:, None, None, :]
    attended = attend(cross_queries, cross_keys, cross_values, valid_keys)
    second_sum = first_sum + low_back(product(attended, cout_w) + shift_rows[8])
    normed = low(layer_norm(second_sum, gain_rows[2], shift_rows[2]))
    hidden = low_back(product(normed, in_w) + inner_bias)
    activated = low(jax.nn.gelu(hidden, approximate=False))
    result = second_sum + low_back(product(activated, outm_w) + shift_rows[9])
    return result.reshape(captions, SEQ, MODEL_WIDTH)

def reference(tokens, image_tokens, token_counts, self_qkv, self_out, cross_q, cross_kv, cross_out, mlp_in, mlp_out, norm_gains, shifts, mlp_bias, cotangent):
    params = tuple((weight.astype(jnp.float32) for weight in (self_qkv, self_out, cross_q, cross_kv, cross_out, mlp_in, mlp_out, norm_gains, shifts, mlp_bias)))
    group_size = CAP_DEV * N_IMG
    block_count = tokens.shape[0] // group_size
    block_data = (tokens.reshape(block_count, group_size, SEQ, MODEL_WIDTH), image_tokens.reshape(block_count, group_size, IMG_TOK, MODEL_WIDTH), token_counts.reshape(block_count, group_size), cotangent.reshape(block_count, group_size, SEQ, MODEL_WIDTH))

    def one_block(totals, pieces):
        text_rows, image_rows, counts, grad_output = pieces

        def apply_layer(weights, text_in, image_in):
            return forward(weights, text_in, image_in, counts)
        result, pullback = jax.vjp(apply_layer, params, text_rows.astype(jnp.float32), image_rows.astype(jnp.float32))
        grad_params, grad_text, grad_image = pullback(grad_output.astype(jnp.float32))
        totals = jax.tree.map(jnp.add, totals, grad_params)
        return (totals, (result.astype(jnp.bfloat16), grad_text.astype(jnp.bfloat16), grad_image.astype(jnp.bfloat16)))
    zero_grads = jax.tree.map(jnp.zeros_like, params)
    totals, outputs = lax.scan(one_block, zero_grads, block_data)
    layer_out = outputs[0].reshape(tokens.shape)
    token_grads = outputs[1].reshape(tokens.shape)
    image_grads = outputs[2].reshape(image_tokens.shape)
    return (layer_out, token_grads, image_grads, totals[0], totals[1], totals[2], totals[3], totals[4], totals[5], totals[6], totals[7], totals[8], totals[9])
```

```python
import functools

import jax
import jax.numpy as jnp
from jax import lax
from jax.experimental import pallas as pl
from jax.experimental.pallas import tpu as pltpu
from jax.sharding import PartitionSpec as P

MODEL_WIDTH = 768
HEADS = 12
HEAD = 64
SEQ = 64
VEC_ROWS = 16
LANES = 128
MESH = pl.DeviceIdType.MESH
bf16 = jnp.bfloat16
f32 = jnp.float32

masked_value = -1e30
norm_epsilon = 1e-05


def tile_ds(index, size, unit):
    return pl.ds(pl.multiple_of(index * size, unit), size)


def stacked_block(rows, cols):
    return lambda ref, d, i: ref.at[i, tile_ds(d, rows, 16), :]


def grid_block(rows, cols):
    return lambda ref, d, i: ref.at[tile_ds(d, rows, 16), tile_ds(i, cols, LANES)]


def turned_block(rows, cols):
    return lambda ref, d, i: ref.at[tile_ds(i, rows, 16), tile_ds(d, cols, LANES)]


class Group:
    def __init__(self, rows, cols, dtype, full, block):
        self.rows, self.cols, self.dtype, self.full = rows, cols, dtype, full
        self.block = block(rows, cols)


def flip(d, bit):
    return d + bit * (1 - 2 * ((d // bit) % 2))


class Place:
    def __init__(self, n_img):
        self.n_img = n_img
        self.dp, self.im = lax.axis_index("dp"), lax.axis_index("img")
        self.core = self.dp % 2
        self.sib = flip(self.dp, 1)

    def first(self, d):
        return flip(d, 2) * (1 - self.core) + flip(d, 4) * self.core

    def second(self, d):
        return flip(d, 4) * (1 - self.core) + flip(d, 2) * self.core

    def near(self, k):
        value = jnp.int32(0)
        for at in range(self.n_img):
            order = sorted(range(self.n_img), key=lambda other: (abs(other - at), other))
            value = jnp.where(self.im == at, order[k], value)
        return value

    def barrier(self):
        semaphore = pltpu.get_barrier_semaphore()
        peers = [(self.sib, self.im), (self.first(self.dp), self.im), (self.second(self.dp), self.im)]
        peers += [(self.dp, (self.im + k) % self.n_img) for k in range(1, self.n_img)]
        for peer in peers:
            pl.semaphore_signal(semaphore, inc=1, device_id=peer, device_id_type=MESH)
        pl.semaphore_wait(semaphore, len(peers))


class Sends:
    def __init__(self):
        self.started = []

    def send(self, src, dst, send_sem, recv_sem, device, when=None):
        copy = pltpu.make_async_remote_copy(
            src, dst, send_sem, recv_sem, device_id=device, device_id_type=MESH
        )
        self.started.append((when, copy))
        if when is None:
            copy.start()
        else:
            pl.when(when)(copy.start)

    def finish(self):
        for when, copy in self.started:
            if when is None:
                copy.wait_send()
            else:
                pl.when(when)(copy.wait_send)


def gather_kernel(groups, n_img, caps, *refs):
    count = len(groups)
    own, x_ref = refs[:count], refs[count]
    full, xo_ref = refs[count + 1 : 2 * count + 1], refs[2 * count + 1]
    send_sem, recv_sem, local_sem, xs_sem, xr_sem = refs[2 * count + 2 :]
    here = Place(n_img)
    dp, im, sib = here.dp, here.im, here.sib
    near = [here.near(k) for k in range(n_img)]
    sends = Sends()
    used = [0] * count

    locals_ = []
    for g, group in enumerate(groups):
        copy = pltpu.make_async_copy(own[g], group.block(full[g], dp, im), local_sem.at[g])
        copy.start()
        locals_.append(copy)
    copy = pltpu.make_async_copy(
        x_ref.at[pl.ds(im * caps, caps)], xo_ref.at[im], local_sem.at[count]
    )
    copy.start()
    locals_.append(copy)
    here.barrier()

    def forward(g, d, i, src, device, when=None):
        sends.send(
            src,
            groups[g].block(full[g], d, i),
            send_sem.at[g, used[g]],
            recv_sem.at[g, d, i],
            device,
            when,
        )
        used[g] += 1

    def arrived(g, d, i):
        block = groups[g].block(full[g], d, i)
        pltpu.make_async_remote_copy(
            block, block, send_sem.at[g, 0], recv_sem.at[g, d, i], device_id=(sib, im), device_id_type=MESH
        ).wait_recv()
        return block

    for g in range(count):
        forward(g, dp, im, own[g], (dp, im + 1), im < n_img - 1)
        forward(g, dp, im, own[g], (dp, im - 1), im > 0)
        forward(g, dp, im, own[g], (here.first(dp), im))
        forward(g, dp, im, own[g], (here.second(dp), im))
        forward(g, dp, im, own[g], (sib, im))
    x_copies = []
    for k in range(1, n_img):
        target = (im + k) % n_img
        x_copies.append(
            pltpu.make_async_remote_copy(
                x_ref.at[pl.ds(target * caps, caps)],
                xo_ref.at[im],
                xs_sem.at[k],
                xr_sem.at[k],
                device_id=(dp, target),
                device_id_type=MESH,
            )
        )
        x_copies[-1].start()

    def line_step(g, k):
        i = near[k]
        block = arrived(g, dp, i)
        step = jnp.where(i < im, 1, -1)
        forward(g, dp, i, block, (dp, im + step), (im + step >= 0) & (im + step < n_img))
        forward(g, dp, i, block, (here.first(dp), im))
        forward(g, dp, i, block, (here.second(dp), im))
        forward(g, dp, i, block, (sib, im))

    def first_step(g, k):
        d, i = here.first(dp), near[k]
        block = arrived(g, d, i)
        forward(g, d, i, block, (here.second(dp), im))
        forward(g, d, i, block, (sib, im))

    def second_step(g, k):
        for d in (here.second(dp), here.second(here.first(dp))):
            block = arrived(g, d, near[k])
            forward(g, d, near[k], block, (sib, im))

    for t in range(count + 2):
        if t < count:
            for k in range(1, n_img):
                line_step(t, k)
        if 0 <= t - 1 < count:
            for k in range(n_img):
                first_step(t - 1, k)
        if 0 <= t - 2 < count:
            for k in range(n_img):
                second_step(t - 2, k)
    for g in range(count):
        for c in range(4):
            for i in range(n_img):
                arrived(g, 2 * c + 1 - here.core, i)
    for copy in x_copies:
        copy.wait()
    sends.finish()
    for copy in locals_:
        copy.wait()


def gather_all(groups, n_img, owns, image_tokens):
    caps = image_tokens.shape[0] // n_img
    count = len(groups)
    any_spec = pl.BlockSpec(memory_space=pl.ANY)
    outs = [jax.ShapeDtypeStruct(group.full, group.dtype) for group in groups]
    outs.append(jax.ShapeDtypeStruct((n_img, caps) + image_tokens.shape[1:], image_tokens.dtype))
    dma = pltpu.SemaphoreType.DMA
    return pl.pallas_call(
        functools.partial(gather_kernel, groups, n_img, caps),
        out_shape=outs,
        in_specs=[any_spec] * (count + 1),
        out_specs=[any_spec] * (count + 1),
        scratch_shapes=[
            dma((count, 64)),
            dma((count, 8, n_img)),
            dma((count + 1,)),
            dma((n_img,)),
            dma((n_img,)),
        ],
        compiler_params=pltpu.CompilerParams(
            collective_id=1, has_side_effects=True, vmem_limit_bytes=8 << 20
        ),
    )(*owns, image_tokens)


def add_into(dst, src):
    rows = dst.shape[0]

    def body(r, carry):
        part = pl.ds(pl.multiple_of(r * 16, 16), 16)
        dst[part, :] = (dst[part, :].astype(f32) + src[part, :].astype(f32)).astype(dst.dtype)
        return carry

    lax.fori_loop(0, rows // 16, body, 0)


def reduce_kernel(groups, n_img, caps, *refs):
    count = len(groups)
    full, dx_ref = refs[:count], refs[count]
    refs = refs[count + 1 :]
    out, dxo_ref = refs[:count], refs[count]
    refs = refs[count + 1 :]
    acc, r0, r1, r2, zr = [refs[n * count : (n + 1) * count] for n in range(5)]
    (load_sem, s0_sem, r0_sem, s1_sem, r1_sem, s2_sem, r2_sem, sz_sem, rz_sem, xs_sem, xr_sem, x_sem) = refs[
        5 * count :
    ]
    here = Place(n_img)
    dp, im, sib, core = here.dp, here.im, here.sib, here.core
    chip = dp // 2
    first, second = here.first(dp), here.second(dp)
    chip1, chip2 = first // 2, second // 2
    chip12 = here.second(first) // 2
    near = [here.near(k) for k in range(n_img)]
    sends = Sends()

    loads = {}
    for g, group in enumerate(groups):
        for c in range(4):
            for i in range(n_img):
                copy = pltpu.make_async_copy(
                    group.block(full[g], 2 * c + core, i), acc[g].at[c, i], load_sem.at[g, c, i]
                )
                copy.start()
    x_own = pltpu.make_async_copy(dx_ref.at[im], dxo_ref.at[pl.ds(im * caps, caps)], x_sem)
    x_own.start()
    here.barrier()
    for g, group in enumerate(groups):
        for c in (chip1, chip12, chip2, chip):
            for i in range(n_img):
                sends.send(
                    group.block(full[g], 2 * c + 1 - core, i),
                    r0[g].at[c, i],
                    s0_sem.at[g, c, i],
                    r0_sem.at[g, c, i],
                    (sib, im),
                )
    x_copies = []
    for k in range(1, n_img):
        target = (im + k) % n_img
        copy = pltpu.make_async_remote_copy(
            dx_ref.at[target],
            dxo_ref.at[pl.ds(im * caps, caps)],
            xs_sem.at[k],
            xr_sem.at[k],
            device_id=(dp, target),
            device_id_type=MESH,
        )
        copy.start()
        x_copies.append(copy)

    def arrived(buffer, semaphore):
        pltpu.make_async_remote_copy(
            buffer, buffer, s0_sem.at[0, 0, 0], semaphore, device_id=(sib, im), device_id_type=MESH
        ).wait_recv()

    def own_pair(g, c, i):
        block = acc[g].at[c, i]
        pltpu.make_async_copy(block, block, load_sem.at[g, c, i]).wait()
        arrived(r0[g].at[c, i], r0_sem.at[g, c, i])
        add_into(block, r0[g].at[c, i])
        return block

    def take(block, buffer, semaphore):
        arrived(buffer, semaphore)
        add_into(block, buffer)

    def second_step(g):
        for j, c in enumerate((chip2, chip12)):
            for i in range(n_img):
                block = own_pair(g, c, i)
                sends.send(
                    block, r1[g].at[j, i], s1_sem.at[g, j, i], r1_sem.at[g, j, i], (second, im)
                )

    def first_step(g):
        for i in range(n_img):
            block = own_pair(g, chip1, i)
            take(block, r1[g].at[1, i], r1_sem.at[g, 1, i])
            sends.send(block, r2[g].at[i], s2_sem.at[g, i], r2_sem.at[g, i], (first, im))

    def line_step(g):
        for k in reversed(range(1, n_img)):
            i = near[k]
            block = own_pair(g, chip, i)
            take(block, r1[g].at[0, i], r1_sem.at[g, 0, i])
            take(block, r2[g].at[i], r2_sem.at[g, i])
            down = jnp.where(i < im, 1, 0)
            inner = (im > 0) & (im < n_img - 1)

            @pl.when(inner)
            def _():
                take(block, zr[g].at[down, i], rz_sem.at[g, down, i])

            sends.send(
                block,
                zr[g].at[down, i],
                sz_sem.at[g, i],
                rz_sem.at[g, down, i],
                (dp, im + 1 - 2 * down),
            )
        block = own_pair(g, chip, im)
        take(block, r1[g].at[0, im], r1_sem.at[g, 0, im])
        take(block, r2[g].at[im], r2_sem.at[g, im])

    def last_step(g):
        block = acc[g].at[chip, im]
        out[g][...] = block[...].astype(f32)
        for down, has in ((0, im > 0), (1, im < n_img - 1)):

            @pl.when(has)
            def _():
                arrived(zr[g].at[down, im], rz_sem.at[g, down, im])
                out[g][...] += zr[g][down, im].astype(f32)

    for t in range(count + 3):
        if t < count:
            second_step(t)
        if 0 <= t - 1 < count:
            first_step(t - 1)
        if 0 <= t - 2 < count:
            line_step(t - 2)
        if 0 <= t - 3 < count:
            last_step(t - 3)
    for copy in x_copies:
        copy.wait()
    sends.finish()
    x_own.wait()


def reduce_all(groups, n_img, partials, image_grads):
    caps = image_grads.shape[1]
    count = len(groups)
    any_spec = pl.BlockSpec(memory_space=pl.ANY)
    vmem_spec = pl.BlockSpec(memory_space=pltpu.VMEM)
    outs = [jax.ShapeDtypeStruct((group.rows, group.cols), f32) for group in groups]
    outs.append(
        jax.ShapeDtypeStruct((n_img * caps,) + image_grads.shape[2:], image_grads.dtype)
    )
    dma = pltpu.SemaphoreType.DMA

    def buffers(*lead):
        return [pltpu.VMEM(lead + (group.rows, group.cols), group.dtype) for group in groups]

    return pl.pallas_call(
        functools.partial(reduce_kernel, groups, n_img, caps),
        out_shape=outs,
        in_specs=[any_spec] * (count + 1),
        out_specs=[vmem_spec] * count + [any_spec],
        scratch_shapes=buffers(4, n_img)
        + buffers(4, n_img)
        + buffers(2, n_img)
        + buffers(n_img)
        + buffers(2, n_img)
        + [
            dma((count, 4, n_img)),
            dma((count, 4, n_img)),
            dma((count, 4, n_img)),
            dma((count, 2, n_img)),
            dma((count, 2, n_img)),
            dma((count, n_img)),
            dma((count, n_img)),
            dma((count, n_img)),
            dma((count, 2, n_img)),
            dma((n_img,)),
            dma((n_img,)),
            dma(()),
        ],
        compiler_params=pltpu.CompilerParams(
            collective_id=2, has_side_effects=True, vmem_limit_bytes=56 << 20
        ),
    )(*partials, image_grads)


def layer_norm(values, norm_gain, norm_shift):
    average = jnp.mean(values, axis=-1, keepdims=True)
    centred = values - average
    spread = jnp.mean(centred * centred, axis=-1, keepdims=True)
    return centred * lax.rsqrt(spread + norm_epsilon) * norm_gain + norm_shift


def matmul(left_op, right_op):
    return jnp.dot(left_op, right_op, preferred_element_type=f32)


def matmul_tleft(left_op, right_op):
    return lax.dot_general(
        left_op, right_op, (((0,), (0,)), ((), ())), preferred_element_type=f32
    )


def matmul_tright(left_op, right_op):
    return lax.dot_general(
        left_op, right_op, (((1,), (1,)), ((), ())), preferred_element_type=f32
    )


def column_sums(values):
    return jnp.sum(values.astype(f32), axis=0)


def to_heads(values, captions):
    return values.reshape(captions, -1, HEADS, HEAD)


def probabilities(queries, key_heads, allowed):
    scores = jnp.einsum("cqhd,ckhd->chqk", queries, key_heads, preferred_element_type=f32)
    scores = jnp.where(allowed, scores * HEAD ** (-0.5), masked_value)
    return jax.nn.softmax(scores, axis=-1)


def attention(queries, key_heads, value_heads, allowed):
    probs = probabilities(queries, key_heads, allowed).astype(bf16)
    return jnp.einsum("chqk,ckhd->cqhd", probs, value_heads, preferred_element_type=f32)


def attention_backward(queries, key_heads, value_heads, allowed, grad_mixed):
    probs = probabilities(queries, key_heads, allowed)
    grad_probs = jnp.einsum("cqhd,ckhd->chqk", grad_mixed, value_heads, preferred_element_type=f32)
    inner_term = jnp.sum(probs * grad_probs, axis=-1, keepdims=True)
    grad_scores = (probs * (grad_probs - inner_term)).astype(bf16)
    score_scale = HEAD ** (-0.5)
    grad_queries = (
        jnp.einsum("chqk,ckhd->cqhd", grad_scores, key_heads, preferred_element_type=f32)
        * score_scale
    )
    grad_keys = (
        jnp.einsum("chqk,cqhd->ckhd", grad_scores, queries, preferred_element_type=f32)
        * score_scale
    )
    grad_values = jnp.einsum(
        "chqk,cqhd->ckhd", probs.astype(bf16), grad_mixed, preferred_element_type=f32
    )
    return grad_queries.astype(bf16), grad_keys.astype(bf16), grad_values.astype(bf16)


def local(
    n_dp,
    n_img,
    tokens,
    image_tokens,
    token_counts,
    self_qkv,
    self_out,
    cross_q,
    cross_kv,
    cross_out,
    mlp_in,
    mlp_out,
    norm_gains,
    shifts,
    mlp_bias,
    cotangent,
):
    captions = tokens.shape[0]
    rows_all = captions * SEQ
    block_len = image_tokens.shape[1]
    width = self_out.shape[1]
    depth = self_out.shape[0]
    inner_dp = mlp_out.shape[0]
    inner_img = mlp_in.shape[1]
    inner = inner_dp * n_dp
    direct = n_dp == 8 and depth % 16 == 0 and width % 16 == 0
    counts = lax.dynamic_slice_in_dim(token_counts, lax.axis_index("img") * captions, captions)

    mixed = jnp.concatenate([self_qkv, self_out, cross_q, cross_out], axis=1)
    vectors = jnp.concatenate([norm_gains.reshape(-1), shifts.reshape(-1), mlp_bias])
    if direct:
        used = vectors.shape[0]
        vectors = jnp.pad(vectors, (0, VEC_ROWS * LANES - used)).reshape(VEC_ROWS, LANES)
        groups = [
            Group(VEC_ROWS, LANES, f32, (n_img, n_dp * VEC_ROWS, LANES), stacked_block),
            Group(depth, 6 * width, bf16, (n_img, n_dp * depth, 6 * width), stacked_block),
            Group(depth, 2 * width, bf16, (MODEL_WIDTH, 2 * MODEL_WIDTH), grid_block),
            Group(depth, inner_img, bf16, (MODEL_WIDTH, inner), grid_block),
            Group(width, inner_dp, bf16, (MODEL_WIDTH, inner), turned_block),
        ]
        vec_full, mixed_full, ckv_w, in_w, outm_t, image_own = gather_all(
            groups, n_img, (vectors, mixed, cross_kv, mlp_in, mlp_out.T), image_tokens
        )
        vec_full = vec_full[0].reshape(n_dp, VEC_ROWS * LANES)[:, :used]
    else:

        def everything(block, first, then, axes):
            return lax.all_gather(
                lax.all_gather(block, first, axis=axes[0], tiled=True), then, axis=axes[1], tiled=True
            )

        mixed_full = lax.all_gather(
            lax.all_gather(mixed, "dp", axis=0, tiled=True), "img", axis=0, tiled=False
        )
        ckv_w = everything(cross_kv, "img", "dp", (1, 0))
        in_w = everything(mlp_in, "img", "dp", (1, 0))
        outm_t = everything(mlp_out, "img", "dp", (1, 0)).T
        vec_full = lax.all_gather(vectors, "dp", axis=0, tiled=False)
        image_own = lax.all_to_all(
            image_tokens.reshape((n_img, captions) + image_tokens.shape[1:]), "img", 0, 0, tiled=True
        )

    def columns(start, size):
        return (
            mixed_full[:, :, start * width : (start + size) * width]
            .transpose(1, 0, 2)
            .reshape(MODEL_WIDTH, size * MODEL_WIDTH)
        )

    qkv_w, sout_w, cq_w, cout_w = columns(0, 3), columns(3, 1), columns(4, 1), columns(5, 1)
    gain_rows = vec_full[:, : 3 * depth].reshape(n_dp, 3, depth).transpose(1, 0, 2).reshape(3, -1)
    shift_rows = (
        vec_full[:, 3 * depth : 13 * depth]
        .reshape(n_dp, 10, depth)
        .transpose(1, 0, 2)
        .reshape(10, -1)
    )
    inner_bias = vec_full[:, 13 * depth :].reshape(-1)

    zero_row = jnp.zeros((MODEL_WIDTH,), f32)
    rows = tokens.reshape(rows_all, MODEL_WIDTH).astype(f32)
    normed1 = layer_norm(rows, gain_rows[0], shift_rows[0]).astype(bf16)
    mixed_qkv = (
        matmul(normed1, qkv_w) + jnp.concatenate([shift_rows[3], zero_row, shift_rows[4]])
    ).astype(bf16)
    self_queries, self_keys, self_values = [
        to_heads(mixed_qkv[:, n * MODEL_WIDTH : (n + 1) * MODEL_WIDTH], captions) for n in range(3)
    ]
    places = jnp.arange(SEQ, dtype=jnp.int32)
    causal = (places[None, :] <= places[:, None])[None, None]
    self_mixed = attention(self_queries, self_keys, self_values, causal)
    self_mixed = self_mixed.reshape(rows_all, MODEL_WIDTH).astype(bf16)
    first_sum = rows + matmul(self_mixed, sout_w) + shift_rows[5]
    normed2 = layer_norm(first_sum, gain_rows[1], shift_rows[1]).astype(bf16)
    cross_query = (matmul(normed2, cq_w) + shift_rows[6]).astype(bf16)
    cross_queries = to_heads(cross_query, captions)

    image_len = n_img * block_len
    image_rows = image_own.reshape(n_img * captions * block_len, MODEL_WIDTH)
    image_kv = (matmul(image_rows, ckv_w) + jnp.concatenate([zero_row, shift_rows[7]])).astype(bf16)

    def by_caption(values):
        return (
            values.reshape(n_img, captions, block_len, HEADS, HEAD)
            .transpose(1, 0, 2, 3, 4)
            .reshape(captions, image_len, HEADS, HEAD)
        )

    def by_place(values):
        return (
            values.reshape(captions, n_img, block_len, MODEL_WIDTH)
            .transpose(1, 0, 2, 3)
            .reshape(-1, MODEL_WIDTH)
        )

    cross_keys = by_caption(image_kv[:, :MODEL_WIDTH])
    cross_values = by_caption(image_kv[:, MODEL_WIDTH:])
    valid = (jnp.arange(image_len, dtype=jnp.int32)[None, :] < counts[:, None])[:, None, None, :]
    cross_mixed = attention(cross_queries, cross_keys, cross_values, valid)
    cross_mixed = cross_mixed.reshape(rows_all, MODEL_WIDTH).astype(bf16)
    second_sum = first_sum + matmul(cross_mixed, cout_w) + shift_rows[8]
    normed3 = layer_norm(second_sum, gain_rows[2], shift_rows[2]).astype(bf16)
    hidden = matmul(normed3, in_w) + inner_bias
    activated = jax.nn.gelu(hidden, approximate=False).astype(bf16)
    result = second_sum + matmul_tright(activated, outm_t) + shift_rows[9]
    layer_out = result.reshape(tokens.shape).astype(bf16)

    grad_low3 = cotangent.reshape(rows_all, MODEL_WIDTH)
    g_outm_t = matmul_tleft(grad_low3, activated)
    g_shift9 = column_sums(grad_low3)
    grad_act = matmul(grad_low3, outm_t)
    _, gelu_pull = jax.vjp(lambda pre_act: jax.nn.gelu(pre_act, approximate=False), hidden)
    grad_hidden = gelu_pull(grad_act)[0].astype(bf16)
    g_in = matmul_tleft(normed3, grad_hidden)
    g_inner_bias = column_sums(grad_hidden)
    grad_normed3 = matmul_tright(grad_hidden, in_w)
    _, norm_pull3 = jax.vjp(layer_norm, second_sum, gain_rows[2], shift_rows[2])
    grad_second_ln, g_gain2, g_shift2 = norm_pull3(grad_normed3)
    grad_second = grad_low3.astype(f32) + grad_second_ln
    grad_low2 = grad_second.astype(bf16)
    g_cout = matmul_tleft(cross_mixed, grad_low2)
    g_shift8 = column_sums(grad_low2)
    grad_cross_mixed = to_heads(matmul_tright(grad_low2, cout_w).astype(bf16), captions)
    grad_query, grad_ckeys, grad_cvalues = attention_backward(
        cross_queries, cross_keys, cross_values, valid, grad_cross_mixed
    )
    grad_query = grad_query.reshape(rows_all, MODEL_WIDTH)
    g_cq = matmul_tleft(normed2, grad_query)
    g_shift6 = column_sums(grad_query)
    grad_normed2 = matmul_tright(grad_query, cq_w)
    grad_value_rows = by_place(grad_cvalues)
    grad_image_kv = jnp.concatenate([by_place(grad_ckeys), grad_value_rows], axis=1)
    g_ckv = matmul_tleft(image_rows, grad_image_kv)
    g_shift7 = column_sums(grad_value_rows)
    image_grads = matmul_tright(grad_image_kv, ckv_w).astype(bf16).reshape(image_own.shape)
    _, norm_pull2 = jax.vjp(layer_norm, first_sum, gain_rows[1], shift_rows[1])
    grad_first_ln, g_gain1, g_shift1 = norm_pull2(grad_normed2)
    grad_first = grad_second + grad_first_ln
    grad_low1 = grad_first.astype(bf16)
    g_sout = matmul_tleft(self_mixed, grad_low1)
    g_shift5 = column_sums(grad_low1)
    grad_self_mixed = to_heads(matmul_tright(grad_low1, sout_w).astype(bf16), captions)
    grad_qkv = jnp.concatenate(
        [
            part.reshape(rows_all, MODEL_WIDTH)
            for part in attention_backward(
                self_queries, self_keys, self_values, causal, grad_self_mixed
            )
        ],
        axis=1,
    )
    g_qkv = matmul_tleft(normed1, grad_qkv)
    qkv_sums = column_sums(grad_qkv)
    g_shift3, g_shift4 = qkv_sums[:MODEL_WIDTH], qkv_sums[2 * MODEL_WIDTH :]
    grad_normed1 = matmul_tright(grad_qkv, qkv_w)
    _, norm_pull1 = jax.vjp(layer_norm, rows, gain_rows[0], shift_rows[0])
    grad_rows_ln, g_gain0, g_shift0 = norm_pull1(grad_normed1)
    token_grads = (grad_first + grad_rows_ln).reshape(tokens.shape).astype(bf16)
    g_vector_rows = jnp.stack(
        [
            g_gain0,
            g_gain1,
            g_gain2,
            g_shift0,
            g_shift1,
            g_shift2,
            g_shift3,
            g_shift4,
            g_shift5,
            g_shift6,
            g_shift7,
            g_shift8,
            g_shift9,
        ]
    )

    if direct:
        g_vectors = jnp.concatenate(
            [
                g_vector_rows.reshape(13, n_dp, depth).transpose(1, 0, 2).reshape(n_dp, -1),
                g_inner_bias.reshape(n_dp, -1),
            ],
            axis=1,
        )
        g_vectors = jnp.pad(g_vectors, ((0, 0), (0, VEC_ROWS * LANES - used)))
        g_vectors = jnp.broadcast_to(
            g_vectors.reshape(1, n_dp * VEC_ROWS, LANES), (n_img, n_dp * VEC_ROWS, LANES)
        )

        def stacked(grad):
            return (
                grad.astype(bf16).reshape(MODEL_WIDTH, n_img, -1).transpose(1, 0, 2)
            )

        g_mixed = jnp.concatenate([stacked(g) for g in (g_qkv, g_sout, g_cq, g_cout)], axis=2)
        s_vectors, s_mixed, s_ckv, s_in, s_outm_t, image_out = reduce_all(
            groups,
            n_img,
            (g_vectors, g_mixed, g_ckv.astype(bf16), g_in.astype(bf16), g_outm_t.astype(bf16)),
            image_grads,
        )
        s_vectors = s_vectors.reshape(-1)
        s_rows = s_vectors[: 13 * depth].reshape(13, depth)
        s_inner = s_vectors[13 * depth : used]
        s_qkv = s_mixed[:, : 3 * width]
        s_sout, s_cq, s_cout = [s_mixed[:, n * width : (n + 1) * width] for n in (3, 4, 5)]
        s_outm = s_outm_t.T
    else:

        def scattered(grad):
            tall = lax.psum_scatter(grad, "dp", scatter_dimension=0, tiled=True)
            return lax.psum_scatter(tall, "img", scatter_dimension=1, tiled=True)

        s_qkv, s_sout, s_cq, s_ckv, s_cout, s_in, s_outm = [
            scattered(g) for g in (g_qkv, g_sout, g_cq, g_ckv, g_cout, g_in, g_outm_t.T)
        ]
        s_rows, s_inner = lax.psum(
            (
                lax.psum_scatter(g_vector_rows, "dp", scatter_dimension=1, tiled=True),
                lax.psum_scatter(g_inner_bias, "dp", scatter_dimension=0, tiled=True),
            ),
            "img",
        )
        image_out = lax.all_to_all(image_grads, "img", 0, 0, tiled=True).reshape(image_tokens.shape)
    return (
        layer_out,
        token_grads,
        image_out,
        s_qkv,
        s_sout,
        s_cq,
        s_ckv,
        s_cout,
        s_in,
        s_outm,
        s_rows[:3],
        s_rows[3:],
        s_inner,
    )


def solution(mesh):
    caption_rows = P(("dp", "img"), None, None)
    weight = P("dp", "img")
    vector = P(None, "dp")
    in_specs = (caption_rows, P("dp", "img", None), P("dp")) + (weight,) * 7
    in_specs += (vector, vector, P("dp"), caption_rows)
    out_specs = (caption_rows, caption_rows, P("dp", "img", None)) + (weight,) * 7
    out_specs += (vector, vector, P("dp"))
    return jax.shard_map(
        functools.partial(local, mesh.shape["dp"], mesh.shape["img"]),
        mesh=mesh,
        in_specs=in_specs,
        out_specs=out_specs,
        check_vma=False,
    )
```

```python
import functools
from types import SimpleNamespace

import jax
import jax.numpy as jnp
from jax import lax
from jax.experimental import pallas as pl
from jax.experimental.pallas import tpu as pltpu
from jax.sharding import PartitionSpec as P

MODEL_WIDTH = 768
HEADS = 12
HEAD = 64
SEQ = 64
VEC_ROWS = 16
LANES = 128
MESH = pl.DeviceIdType.MESH
bf16 = jnp.bfloat16
f32 = jnp.float32

masked_value = -1e30
norm_epsilon = 1e-05


def tile_ds(index, size, unit):
    return pl.ds(pl.multiple_of(index * size, unit), size)


def stacked_block(rows, cols):
    return lambda ref, d, i: ref.at[i, tile_ds(d, rows, 16), :]


def grid_block(rows, cols):
    return lambda ref, d, i: ref.at[tile_ds(d, rows, 16), tile_ds(i, cols, LANES)]


def turned_block(rows, cols):
    return lambda ref, d, i: ref.at[tile_ds(i, rows, 16), tile_ds(d, cols, LANES)]


def repeated_block(rows, cols):
    return lambda ref, d, i: ref.at[tile_ds(d, rows, 8), :]


class Group:
    def __init__(self, rows, cols, dtype, full, block):
        self.rows, self.cols, self.dtype, self.full = rows, cols, dtype, full
        self.block = block(rows, cols)


def flip(d, bit):
    return d + bit * (1 - 2 * ((d // bit) % 2))


class Place:
    def __init__(self, n_img):
        self.n_img = n_img
        self.dp, self.im = lax.axis_index("dp"), lax.axis_index("img")
        self.core = self.dp % 2
        self.sib = flip(self.dp, 1)

    def first(self, d):
        return flip(d, 2) * (1 - self.core) + flip(d, 4) * self.core

    def second(self, d):
        return flip(d, 4) * (1 - self.core) + flip(d, 2) * self.core

    def near(self, k):
        value = jnp.int32(0)
        for at in range(self.n_img):
            order = sorted(range(self.n_img), key=lambda other: (abs(other - at), other))
            value = jnp.where(self.im == at, order[k], value)
        return value

    def barrier(self):
        semaphore = pltpu.get_barrier_semaphore()
        peers = [(self.sib, self.im), (self.first(self.dp), self.im), (self.second(self.dp), self.im)]
        peers += [(self.dp, (self.im + k) % self.n_img) for k in range(1, self.n_img)]
        for peer in peers:
            pl.semaphore_signal(semaphore, inc=1, device_id=peer, device_id_type=MESH)
        pl.semaphore_wait(semaphore, len(peers))


class Sends:
    def __init__(self):
        self.started = []

    def send(self, src, dst, send_sem, recv_sem, device, when=None):
        copy = pltpu.make_async_remote_copy(
            src, dst, send_sem, recv_sem, device_id=device, device_id_type=MESH
        )
        entry = (when, copy)
        self.started.append(entry)
        if when is None:
            copy.start()
        else:
            pl.when(when)(copy.start)
        return entry

    def send_copy(self, copy):
        self.started.append((None, copy))
        copy.start()

    def wait(self, *entries):
        for entry in entries:
            self.started = [other for other in self.started if other is not entry]
            when, copy = entry
            if when is None:
                copy.wait_send()
            else:
                pl.when(when)(copy.wait_send)

    def finish(self):
        self.wait(*self.started)


def add_into(dst, src):
    rows = dst.shape[0]

    def body(r, carry):
        part = pl.ds(pl.multiple_of(r * 16, 16), 16)
        dst[part, :] = (dst[part, :].astype(f32) + src[part, :].astype(f32)).astype(dst.dtype)
        return carry

    lax.fori_loop(0, rows // 16, body, 0)


def dot(left, right):
    return jnp.dot(left, right, preferred_element_type=f32)


def dot_left(left, right):
    return lax.dot_general(left, right, (((0,), (0,)), ((), ())), preferred_element_type=f32)


def dot_right(left, right):
    return lax.dot_general(left, right, (((1,), (1,)), ((), ())), preferred_element_type=f32)


def for_rows(count, size, body):
    def step(r, carry):
        body(pl.ds(pl.multiple_of(r * size, size), size))
        return carry

    lax.fori_loop(0, count // size, step, 0)


def standard(values):
    average = jnp.mean(values, axis=-1, keepdims=True)
    centred = values - average
    spread = jnp.mean(centred * centred, axis=-1, keepdims=True)
    rate = lax.rsqrt(spread + norm_epsilon)
    return centred * rate, rate


def norm_rows(out, values, gain, shift):
    def body(part):
        unit, _ = standard(values[part, :].astype(f32))
        out[part, :] = (unit * gain + shift).astype(bf16)

    for_rows(out.shape[0], 64, body)


def norm_rows_back(grad, values, gain, add, out, sums, low, gain_row, shift_row, low_row):
    zero = jnp.zeros((1, MODEL_WIDTH), f32)
    sums[gain_row : gain_row + 1, :] = zero
    sums[shift_row : shift_row + 1, :] = zero
    if low_row is not None:
        sums[low_row : low_row + 1, :] = zero

    def body(part):
        unit, rate = standard(values[part, :].astype(f32))
        grad_part = grad[part, :]
        scaled = grad_part * gain
        inner = jnp.mean(scaled, axis=-1, keepdims=True)
        along = jnp.mean(scaled * unit, axis=-1, keepdims=True)
        total = add[part, :].astype(f32) + rate * (scaled - inner - unit * along)
        rounded = total.astype(bf16)
        if out is not None:
            out[part, :] = total
        low[part, :] = rounded
        sums[gain_row : gain_row + 1, :] += jnp.sum(grad_part * unit, axis=0, keepdims=True)
        sums[shift_row : shift_row + 1, :] += jnp.sum(grad_part, axis=0, keepdims=True)
        if low_row is not None:
            sums[low_row : low_row + 1, :] += jnp.sum(rounded.astype(f32), axis=0, keepdims=True)

    for_rows(grad.shape[0], 64, body)


QUAD = 4 * HEAD


def head_mask():
    lane_head = lax.broadcasted_iota(jnp.int32, (4, SEQ, QUAD), 2) // HEAD
    return lane_head == lax.broadcasted_iota(jnp.int32, (4, SEQ, QUAD), 0)


def by_head(values, mask):
    return jnp.where(mask, values.astype(f32)[None], 0.0).reshape(4 * SEQ, QUAD).astype(bf16)


def from_head(values, mask):
    return jnp.sum(jnp.where(mask, values.reshape(4, SEQ, QUAD), 0.0), axis=0)


def weights_of(queries, keys, allowed):
    scores = jnp.where(allowed, dot_right(queries, keys) * HEAD ** (-0.5), masked_value)
    top = jnp.max(scores, axis=-1, keepdims=True)
    weights = jnp.exp(scores - top)
    return weights * (1.0 / jnp.sum(weights, axis=-1, keepdims=True))


def attend(query, keys, values, allowed, mask):
    probs = weights_of(by_head(query, mask), keys, allowed).astype(bf16)
    return from_head(dot(probs, values), mask).astype(bf16)


def attend_back(query, keys, values, allowed, mask, grad_mixed):
    queries, grads = by_head(query, mask), by_head(grad_mixed, mask)
    probs = weights_of(queries, keys, allowed)
    grad_probs = dot_right(grads, values)
    inner = jnp.sum(probs * grad_probs, axis=-1, keepdims=True)
    grad_scores = (probs * (grad_probs - inner)).astype(bf16)
    scale = HEAD ** (-0.5)
    return (
        (from_head(dot(grad_scores, keys), mask) * scale).astype(bf16),
        (dot_left(grad_scores, queries) * scale).astype(bf16),
        dot_left(probs.astype(bf16), grads).astype(bf16),
    )


def causal_mask():
    shape = (4 * SEQ, SEQ)
    query = lax.broadcasted_iota(jnp.int32, shape, 0) % SEQ
    return lax.broadcasted_iota(jnp.int32, shape, 1) <= query


def unpack_vectors(blocks, vec, bias, n_dp, depth, inner_dp):
    for d in range(n_dp):
        row = d * VEC_ROWS
        vec[0:13, d * depth : (d + 1) * depth] = blocks[row : row + 13, 0:depth]
        for j in range(inner_dp // LANES):
            at, col = divmod(d * inner_dp + j * LANES, bias.shape[1])
            bias[at : at + 1, col : col + LANES] = blocks[row + 13 + j : row + 14 + j, :]


def pack_vectors(vec, bias, blocks, n_dp, depth, inner_dp):
    blocks[...] = jnp.zeros_like(blocks)
    for d in range(n_dp):
        row = d * VEC_ROWS
        blocks[row : row + 13, 0:depth] = vec[0:13, d * depth : (d + 1) * depth]
        for j in range(inner_dp // LANES):
            at, col = divmod(d * inner_dp + j * LANES, bias.shape[1])
            blocks[row + 13 + j : row + 14 + j, :] = bias[at : at + 1, col : col + LANES]


class Copies:
    def __init__(self, semaphores):
        self.semaphores, self.used, self.open = semaphores, 0, []

    def start(self, src, dst):
        copy = pltpu.make_async_copy(src, dst, self.semaphores.at[self.used])
        self.used += 1
        copy.start()
        self.open.append(copy)
        return copy

    def wait(self, *copies):
        for copy in copies:
            self.open = [other for other in self.open if other is not copy]
            copy.wait()

    def finish(self):
        self.wait(*self.open)


def kept_shapes(dims):
    n_dp, n_img, caps, depth, width, inner_dp, block_len = dims
    rows, wide, inner = caps * SEQ, MODEL_WIDTH, n_dp * inner_dp
    low, high = ((rows, wide), bf16), ((rows, wide), f32)
    return dict(
        weights=((wide, 6 * wide), bf16),
        normed1=low,
        qkv=((rows, 3 * wide), bf16),
        self_mixed=low,
        first_sum=high,
        normed2=low,
        query=low,
        kv=((n_img, caps, block_len, 2 * wide), bf16),
        mixed=low,
        second_sum=high,
        vec=((16, wide), f32),
        bias=((n_img, inner // n_img), f32),
        images=((n_img, caps, block_len, wide), bf16),
        ckv=((wide, 2 * wide), bf16),
    )


class Forward:
    def __init__(self, dims, counts, raw, tokens, kept):
        self.n_img, self.width = dims[1], dims[4]
        self.counts, self.raw, self.tokens, self.kept = counts, raw, tokens, kept

    def gain(self, k):
        return self.kept.vec[k : k + 1, :]

    def shift(self, k):
        return self.kept.vec[3 + k : 4 + k, :]

    def first_norm(self):
        norm_rows(self.kept.normed1, self.tokens, self.gain(0), self.shift(0))

    def assemble(self, i):
        weights, w, wide = self.kept.weights, self.width, MODEL_WIDTH
        weights[:, i * 3 * w : (i + 1) * 3 * w] = self.raw[i, :, 0 : 3 * w]
        for n in range(3):
            at = (3 + n) * wide + i * w
            weights[:, at : at + w] = self.raw[i, :, (3 + n) * w : (4 + n) * w]

    def image_kv(self, i):
        wide = MODEL_WIDTH
        kv = self.kept.kv
        block = self.kept.images[i]
        rows = block.shape[0] * block.shape[1]
        block = block.reshape(rows, wide)
        for n in range(2):
            value = dot(block, self.kept.ckv[:, n * wide : (n + 1) * wide])
            if n == 1:
                value = value + self.shift(7)
            kv[i, :, :, n * wide : (n + 1) * wide] = value.astype(bf16).reshape(kv.shape[1:3] + (wide,))

    def project(self):
        wide, qkv = MODEL_WIDTH, self.kept.qkv
        for n, shift in enumerate((3, None, 4)):
            value = dot(self.kept.normed1[...], self.kept.weights[:, n * wide : (n + 1) * wide])
            if shift is not None:
                value = value + self.shift(shift)
            qkv[:, n * wide : (n + 1) * wide] = value.astype(bf16)

    def self_attention(self, start, stop):
        qkv, out, wide = self.kept.qkv, self.kept.self_mixed, MODEL_WIDTH
        allowed, mask = causal_mask(), head_mask()

        def caption(c, carry):
            part = pl.ds(pl.multiple_of(c * SEQ, SEQ), SEQ)
            for t in range(wide // QUAD):
                at = t * QUAD
                out[part, at : at + QUAD] = attend(
                    qkv[part, at : at + QUAD],
                    qkv[part, wide + at : wide + at + QUAD],
                    qkv[part, 2 * wide + at : 2 * wide + at + QUAD],
                    allowed,
                    mask,
                )
            return carry

        lax.fori_loop(start, stop, caption, 0)

    def add_product(self, left, n, shift, base, out):
        wide = MODEL_WIDTH
        out[...] = dot(left[...], self.kept.weights[:, n * wide : (n + 1) * wide])
        row = self.shift(shift)

        def body(part):
            out[part, :] = base[part, :].astype(f32) + (out[part, :] + row)

        for_rows(out.shape[0], 64, body)

    def first_residual(self):
        wide = MODEL_WIDTH
        self.add_product(self.kept.self_mixed, 3, 5, self.tokens, self.kept.first_sum)
        norm_rows(self.kept.normed2, self.kept.first_sum, self.gain(1), self.shift(1))
        value = dot(self.kept.normed2[...], self.kept.weights[:, 4 * wide : 5 * wide])
        self.kept.query[...] = (value + self.shift(6)).astype(bf16)

    def valid_keys(self, c):
        shape = (4 * SEQ, self.n_img * self.kept.kv.shape[2])
        return lax.broadcasted_iota(jnp.int32, shape, 1) < self.counts[c]

    def cross_attention(self, start, stop):
        query, kv, out, wide = self.kept.query, self.kept.kv, self.kept.mixed, MODEL_WIDTH
        mask = head_mask()
        length = self.n_img * kv.shape[2]

        def caption(c, carry):
            part = pl.ds(pl.multiple_of(c * SEQ, SEQ), SEQ)
            allowed = self.valid_keys(c)
            for t in range(wide // QUAD):
                at = t * QUAD
                out[part, at : at + QUAD] = attend(
                    query[part, at : at + QUAD],
                    kv[:, c, :, at : at + QUAD].reshape(length, QUAD),
                    kv[:, c, :, wide + at : wide + at + QUAD].reshape(length, QUAD),
                    allowed,
                    mask,
                )
            return carry

        lax.fori_loop(start, stop, caption, 0)

    def second_residual(self):
        self.add_product(self.kept.mixed, 5, 8, self.kept.first_sum, self.kept.second_sum)


class Gatherer:
    def __init__(self, here, groups, own, full, send_sem, recv_sem):
        self.here, self.groups, self.own, self.full = here, groups, own, full
        self.send_sem, self.recv_sem = send_sem, recv_sem
        self.sends, self.used = Sends(), [0] * len(groups)

    def forward(self, g, d, i, src, device, when=None):
        self.sends.send(
            src,
            self.groups[g].block(self.full[g], d, i),
            self.send_sem.at[g, self.used[g]],
            self.recv_sem.at[g, d, i],
            device,
            when,
        )
        self.used[g] += 1

    def arrived(self, g, d, i):
        block, here = self.groups[g].block(self.full[g], d, i), self.here
        pltpu.make_async_remote_copy(
            block,
            block,
            self.send_sem.at[g, 0],
            self.recv_sem.at[g, d, i],
            device_id=(here.sib, here.im),
            device_id_type=MESH,
        ).wait_recv()
        return block

    def to_planes(self, g, d, i, block):
        here = self.here
        self.forward(g, d, i, block, (here.first(here.dp), here.im))
        self.forward(g, d, i, block, (here.second(here.dp), here.im))
        self.forward(g, d, i, block, (here.sib, here.im))

    def start(self, g):
        here = self.here
        dp, im = here.dp, here.im
        self.forward(g, dp, im, self.own[g], (dp, im + 1), im < here.n_img - 1)
        self.forward(g, dp, im, self.own[g], (dp, im - 1), im > 0)
        self.to_planes(g, dp, im, self.own[g])

    def line(self, g, k):
        here = self.here
        dp, im, i = here.dp, here.im, here.near(k)
        block = self.arrived(g, dp, i)
        after = im + jnp.where(i < im, 1, -1)
        self.forward(g, dp, i, block, (dp, after), (after >= 0) & (after < here.n_img))
        self.to_planes(g, dp, i, block)

    def first(self, g, k):
        here = self.here
        d, i = here.first(here.dp), here.near(k)
        block = self.arrived(g, d, i)
        self.forward(g, d, i, block, (here.second(here.dp), here.im))
        self.forward(g, d, i, block, (here.sib, here.im))

    def second(self, g, k):
        here = self.here
        i = here.near(k)
        for d in (here.second(here.dp), here.second(here.first(here.dp))):
            block = self.arrived(g, d, i)
            self.forward(g, d, i, block, (here.sib, here.im))

    def complete(self, g):
        for c in range(4):
            for i in range(self.here.n_img):
                self.arrived(g, 2 * c + 1 - self.here.core, i)


X_PARTS = 4
LAGS = (6, 12)
X_EVERY = 4


def entry_groups(dims):
    n_dp, n_img, caps, depth, width, inner_dp, block_len = dims
    wide, inner = MODEL_WIDTH, n_dp * inner_dp
    return [
        Group(VEC_ROWS, LANES, f32, (n_img, n_dp * VEC_ROWS, LANES), stacked_block),
        Group(depth, 2 * width, bf16, (wide, 2 * wide), grid_block),
        Group(depth, 6 * width, bf16, (n_img, wide, 6 * width), stacked_block),
        Group(depth, inner // n_img, bf16, (wide, inner), grid_block),
        Group(width, inner_dp, bf16, (wide, inner), turned_block),
    ]


def entry_kernel(dims, *refs):
    n_dp, n_img, caps, depth, width, inner_dp, block_len = dims
    groups, shapes = entry_groups(dims), kept_shapes(dims)
    count = len(groups)
    counts, own, (x_ref, tokens_hbm) = refs[0], refs[1 : 1 + count], refs[1 + count : 3 + count]
    refs = refs[3 + count :]
    outs, (in_w, out_t) = bag(shapes, refs), refs[len(shapes) : len(shapes) + 2]
    refs = refs[len(shapes) + 2 :]
    kept, refs = bag(shapes, refs), refs[len(shapes) :]
    vec_full, raw, tokens, send_sem, recv_sem, xs_sem, xr_sem, local_sem = refs
    here = Place(n_img)
    dp, im = here.dp, here.im
    copies = Copies(local_sem)
    full = (vec_full, kept.ckv, raw, in_w, out_t)
    gather = Gatherer(here, groups, own, full, send_sem, recv_sem)
    local_blocks = [
        copies.start(own[g], groups[g].block(full[g], dp, im)) for g in range(count)
    ]
    own_images = copies.start(x_ref.at[pl.ds(im * caps, caps)], kept.images.at[im])
    token_load = copies.start(tokens_hbm, tokens)
    here.barrier()
    for g in range(count):
        gather.start(g)
    part_caps = caps // X_PARTS

    def x_copy(k, p, target, source):
        return pltpu.make_async_remote_copy(
            x_ref.at[pl.ds(target * caps + p * part_caps, part_caps)],
            kept.images.at[source, pl.ds(p * part_caps, part_caps)],
            xs_sem.at[k, p],
            xr_sem.at[k, p],
            device_id=(dp, target),
            device_id_type=MESH,
        )

    waiting = [(k, p) for p in range(X_PARTS) for k in range(1, n_img)][::-1]
    ticks = [0]

    def tick():
        ticks[0] += 1
        if ticks[0] % X_EVERY == 0 and waiting:
            k, p = waiting.pop()
            gather.sends.send_copy(x_copy(k, p, (im + k) % n_img, im))

    units = [(g, k) for g in range(count) for k in range(n_img)]

    def exchange(t):
        if t < len(units):
            g, k = units[t]
            if k > 0:
                gather.line(g, k)
                tick()
        if 0 <= t - LAGS[0] < len(units):
            gather.first(*units[t - LAGS[0]])
            tick()
        if 0 <= t - LAGS[1] < len(units):
            gather.second(*units[t - LAGS[1]])
            tick()

    def images_from(k):
        source = (im + n_img - k) % n_img
        if k > 0:
            for p in range(X_PARTS):
                x_copy(k, p, source, source).wait_recv()
        copies.start(kept.images.at[source], outs.images.at[source])
        step.image_kv(source)
        copies.start(kept.kv.at[source], outs.kv.at[source])

    step = Forward(dims, counts, raw, tokens, kept)
    done = LAGS[1] + n_img
    for t in range(len(units) + LAGS[1]):
        exchange(t)
        if t == done:
            gather.complete(0)
            copies.wait(local_blocks[0], token_load)
            unpack_vectors(vec_full.at[0], kept.vec, kept.bias, n_dp, depth, inner_dp)
            step.first_norm()
        if t == done + n_img:
            gather.complete(1)
            copies.wait(local_blocks[1], own_images)
            images_from(0)
        if t == done + 2 * n_img:
            gather.complete(2)
            copies.wait(local_blocks[2])
            for i in range(n_img):
                step.assemble(i)
            step.project()
        if t == done + 2 * n_img + 2:
            step.self_attention(0, caps // 2)
        if t == done + 2 * n_img + 4:
            step.self_attention(caps // 2, caps)
    copies.start(kept.vec, outs.vec)
    copies.start(kept.bias, outs.bias)
    copies.start(kept.ckv, outs.ckv)
    copies.start(kept.weights, outs.weights)
    copies.start(kept.normed1, outs.normed1)
    copies.start(kept.qkv, outs.qkv)
    copies.start(kept.self_mixed, outs.self_mixed)
    step.first_residual()
    copies.start(kept.first_sum, outs.first_sum)
    copies.start(kept.normed2, outs.normed2)
    copies.start(kept.query, outs.query)
    for k in (1, n_img - 1) + tuple(range(2, n_img - 1)):
        images_from(k)
    step.cross_attention(0, caps)
    copies.start(kept.mixed, outs.mixed)
    step.second_residual()
    copies.start(kept.second_sum, outs.second_sum)
    for g in range(3, count):
        gather.complete(g)
    gather.sends.finish()
    copies.finish()


def entry_pass(dims, counts, owns, image_tokens, tokens):
    n_dp, n_img, caps, depth, width, inner_dp, block_len = dims
    groups, shapes = entry_groups(dims), kept_shapes(dims)
    count = len(groups)
    dma = pltpu.SemaphoreType.DMA
    any_spec = pl.BlockSpec(memory_space=pl.ANY)
    outs = pl.pallas_call(
        functools.partial(entry_kernel, dims),
        out_shape=structs_of(shapes) + [jax.ShapeDtypeStruct(g.full, g.dtype) for g in groups[3:]],
        in_specs=[pl.BlockSpec(memory_space=pltpu.SMEM)] + [any_spec] * (count + 2),
        out_specs=[any_spec] * (len(shapes) + 2),
        scratch_shapes=[pltpu.VMEM(*shape) for shape in shapes.values()]
        + [pltpu.VMEM(groups[0].full, f32), pltpu.VMEM(groups[2].full, bf16), pltpu.VMEM(tokens.shape, bf16)]
        + [
            dma((count, 64)),
            dma((count, n_dp, n_img)),
            dma((n_img, X_PARTS)),
            dma((n_img, X_PARTS)),
            dma((48,)),
        ],
        compiler_params=pltpu.CompilerParams(
            collective_id=1, has_side_effects=True, vmem_limit_bytes=62 << 20
        ),
    )(counts, *owns, image_tokens, tokens)
    kept = dict(zip(shapes, outs))
    kept.update(in_w=outs[-2], out_t=outs[-1])
    return kept


class Backward:
    def __init__(self, dims, counts, refs):
        self.dims, self.counts, self.refs = dims, counts, refs

    def __getattr__(self, name):
        return getattr(self.refs, name)

    def gain(self, k):
        return self.vec[k : k + 1, :]

    def weight(self, n):
        return self.weights[n][...]

    def sum_row(self, k, values):
        self.sums[3 + k : 4 + k, :] = jnp.sum(values.astype(f32), axis=0, keepdims=True)

    def begin(self):
        wide = MODEL_WIDTH
        norm_rows(self.normed3, self.second_sum, self.gain(2), self.vec[5:6, :])
        self.sum_row(9, self.cot[...])
        self.turned[0:wide, :] = self.normed3[...].astype(f32).T.astype(bf16)
        self.turned[wide : 2 * wide, :] = self.cot[...].astype(f32).T.astype(bf16)
        row = self.vec[12:13, :]

        def body(part):
            self.result[part, :] = self.second_sum[part, :] + row
            self.grad[part, :] = jnp.zeros((64, wide), f32)

        for_rows(self.result.shape[0], 64, body)

    def feed_forward(self, bias, in_w, out_t):
        rows = self.normed3.shape[0]
        self.hidden[...] = dot(self.normed3[...], in_w[...])
        self.grad_act[...] = dot(self.cot[...], out_t[...])
        self.hidden_sums[...] = jnp.zeros_like(self.hidden_sums)

        def body(part):
            pre = self.hidden[part, :] + bias
            below = 0.5 * (1.0 + lax.erf(pre * 2**-0.5))
            self.activated[part, :] = (pre * below).astype(bf16)
            slope = below + pre * (jnp.exp(-0.5 * pre * pre) * (2 * jnp.pi) ** -0.5)
            grad = (self.grad_act[part, :] * slope).astype(bf16)
            self.grad_hidden[part, :] = grad
            self.hidden_sums[...] += jnp.sum(grad.astype(f32), axis=0, keepdims=True)

        for_rows(rows, 32, body)
        self.result[...] += dot_right(self.activated[...], out_t[...])
        self.grad[...] += dot_right(self.grad_hidden[...], in_w[...])

    def third_norm_back(self):
        norm_rows_back(
            self.grad, self.second_sum, self.gain(2), self.cot, self.grad_sum, self.sums, self.low, 2, 5, 11
        )

    def cross_grad(self):
        self.grad_mixed[...] = dot_right(self.low[...], self.weight(5)).astype(bf16)

    def cross_caption(self, c, kv, grad_kv):
        wide = MODEL_WIDTH
        n_img, block_len = kv.shape[:2]
        length = n_img * block_len
        part = pl.ds(pl.multiple_of(c * SEQ, SEQ), SEQ)
        allowed = lax.broadcasted_iota(jnp.int32, (4 * SEQ, length), 1) < self.counts[c]
        mask = head_mask()
        for t in range(wide // QUAD):
            own, other = slice(t * QUAD, (t + 1) * QUAD), slice(wide + t * QUAD, wide + (t + 1) * QUAD)
            grad_query, grad_keys, grad_values = attend_back(
                self.query[part, own],
                kv[:, :, own].reshape(length, QUAD),
                kv[:, :, other].reshape(length, QUAD),
                allowed,
                mask,
                self.grad_mixed[part, own],
            )
            self.grad_query[part, own] = grad_query
            grad_kv[:, :, own] = grad_keys.reshape(n_img, block_len, QUAD)
            grad_kv[:, :, other] = grad_values.reshape(n_img, block_len, QUAD)
            self.sums[10:11, own] += jnp.sum(grad_values.astype(f32), axis=0, keepdims=True)

    def second_norm_back(self):
        self.sum_row(6, self.grad_query[...])
        self.grad[...] = dot_right(self.grad_query[...], self.weight(4))
        norm_rows_back(
            self.grad, self.first_sum, self.gain(1), self.grad_sum, self.grad_sum, self.sums, self.low, 1, 4, 8
        )

    def self_grad(self):
        self.grad_mixed[...] = dot_right(self.low[...], self.weight(3)).astype(bf16)

    def self_attention(self, start, stop):
        wide = MODEL_WIDTH
        allowed, mask = causal_mask(), head_mask()

        def caption(c, carry):
            part = pl.ds(pl.multiple_of(c * SEQ, SEQ), SEQ)
            for t in range(wide // QUAD):
                cols = [slice(n * wide + t * QUAD, n * wide + (t + 1) * QUAD) for n in range(3)]
                grads = attend_back(
                    self.qkv[part, cols[0]],
                    self.qkv[part, cols[1]],
                    self.qkv[part, cols[2]],
                    allowed,
                    mask,
                    self.grad_mixed[part, cols[0]],
                )
                for at, value in zip(cols, grads):
                    self.grad_qkv[part, at] = value
            return carry

        lax.fori_loop(start, stop, caption, 0)

    def first_norm_back(self):
        wide = MODEL_WIDTH
        self.sum_row(3, self.grad_qkv[:, 0:wide])
        self.sum_row(4, self.grad_qkv[:, 2 * wide : 3 * wide])
        self.grad[...] = dot_right(self.grad_qkv[...], self.weights_all[:, 0 : 3 * wide])
        norm_rows_back(
            self.grad, self.tokens, self.gain(0), self.grad_sum, None, self.sums, self.token_grads, 0, 3, None
        )


class Reducer:
    def __init__(self, here, groups, buffers, semaphores):
        self.here, self.groups, self.n_img = here, groups, here.n_img
        count = len(groups)
        self.acc, self.r0, self.r1, self.r2, self.zr = [
            buffers[n * count : (n + 1) * count] for n in range(5)
        ]
        (self.load_sem, self.s0, self.r0_sem, self.s1, self.r1_sem, self.s2, self.r2_sem, self.sz, self.rz) = semaphores
        self.sends = Sends()
        dp = here.dp
        self.chip = dp // 2
        self.chip1, self.chip2 = here.first(dp) // 2, here.second(dp) // 2
        self.chip12 = here.second(here.first(dp)) // 2

    @staticmethod
    def scratch(groups, n_img):
        count, dma = len(groups), pltpu.SemaphoreType.DMA
        leads = ((4, n_img), (4, n_img), (2, n_img), (n_img,), (2, n_img))
        buffers = [
            pltpu.VMEM(lead + (group.rows, group.cols), group.dtype) for lead in leads for group in groups
        ]
        sizes = [(4, n_img)] * 3 + [(2, n_img)] * 2 + [(n_img,)] * 3 + [(2, n_img)]
        return buffers, [dma((count,) + size) for size in sizes]

    def give(self, g, c, i, own, other):
        here = self.here
        copy = pltpu.make_async_copy(own, self.acc[g].at[c, i], self.load_sem.at[g, c, i])
        copy.start()
        sent = self.sends.send(
            other, self.r0[g].at[c, i], self.s0.at[g, c, i], self.r0_sem.at[g, c, i], (here.sib, here.im)
        )
        return copy, sent

    def give_from(self, g, full, chips):
        core, block = self.here.core, self.groups[g].block
        for c in chips:
            for i in range(self.n_img):
                self.give(g, c, i, block(full, 2 * c + core, i), block(full, 2 * c + 1 - core, i))

    def arrived(self, buffer, semaphore):
        here = self.here
        pltpu.make_async_remote_copy(
            buffer, buffer, self.s0.at[0, 0, 0], semaphore, device_id=(here.sib, here.im), device_id_type=MESH
        ).wait_recv()

    def take(self, block, buffer, semaphore):
        self.arrived(buffer, semaphore)
        add_into(block, buffer)

    def pair(self, g, c, i, loaded):
        block = self.acc[g].at[c, i]
        if not loaded:
            pltpu.make_async_copy(block, block, self.load_sem.at[g, c, i]).wait()
        self.take(block, self.r0[g].at[c, i], self.r0_sem.at[g, c, i])
        return block

    def second(self, g, j, i, loaded=False):
        here = self.here
        block = self.pair(g, self.chip12 if j else self.chip2, i, loaded)
        self.sends.send(
            block,
            self.r1[g].at[j, i],
            self.s1.at[g, j, i],
            self.r1_sem.at[g, j, i],
            (here.second(here.dp), here.im),
        )

    def first(self, g, i, loaded=False):
        here = self.here
        block = self.pair(g, self.chip1, i, loaded)
        self.take(block, self.r1[g].at[1, i], self.r1_sem.at[g, 1, i])
        self.sends.send(
            block, self.r2[g].at[i], self.s2.at[g, i], self.r2_sem.at[g, i], (here.first(here.dp), here.im)
        )

    def plane(self, g, i, loaded):
        block = self.pair(g, self.chip, i, loaded)
        self.take(block, self.r1[g].at[0, i], self.r1_sem.at[g, 0, i])
        self.take(block, self.r2[g].at[i], self.r2_sem.at[g, i])
        return block

    def line(self, g, k, loaded=False):
        here, im = self.here, self.here.im
        i = here.near(k)
        block = self.plane(g, i, loaded)
        if k > 0:
            down = jnp.where(i < im, 1, 0)

            @pl.when((im > 0) & (im < self.n_img - 1))
            def _():
                self.take(block, self.zr[g].at[down, i], self.rz.at[g, down, i])

            self.sends.send(
                block,
                self.zr[g].at[down, i],
                self.sz.at[g, i],
                self.rz.at[g, down, i],
                (here.dp, im + 1 - 2 * down),
            )

    def last(self, g, out):
        im = self.here.im
        out[...] = self.acc[g][self.chip, im].astype(f32)
        for down, has in ((0, im > 0), (1, im < self.n_img - 1)):

            @pl.when(has)
            def _():
                self.arrived(self.zr[g].at[down, im], self.rz.at[g, down, im])
                out[...] += self.zr[g][down, im].astype(f32)


def turned_gradient(out, values, grads, size=256):
    for n in range(grads.shape[-1] // size):
        cols = slice(n * size, (n + 1) * size)
        out[:, cols] = dot_left(values[...], grads[:, cols]).astype(bf16)


def bag(shapes, refs):
    return SimpleNamespace(**dict(zip(shapes, refs)))


def outer_inputs(dims):
    n_dp, n_img, caps, depth, width, inner_dp, block_len = dims
    wide, rows, inner = MODEL_WIDTH, caps * SEQ, n_dp * inner_dp
    low, high = ((rows, wide), bf16), ((rows, wide), f32)
    return dict(
        vec=((16, wide), f32),
        bias=((n_img, inner // n_img), f32),
        cot=low,
        second_sum=high,
        in_w=((wide, inner), bf16),
        out_t=((wide, inner), bf16),
        weights=((wide, 6 * wide), bf16),
        mixed=low,
        query=low,
        kv=((n_img, caps, block_len, 2 * wide), bf16),
        images=((n_img, caps, block_len, wide), bf16),
        ckv=((wide, 2 * wide), bf16),
        first_sum=high,
        normed2=low,
    )


def outer_outputs(dims):
    n_dp, n_img, caps, depth, width, inner_dp, block_len = dims
    wide, rows, inner = MODEL_WIDTH, caps * SEQ, n_dp * inner_dp
    return dict(
        layer_out=((rows, wide), bf16),
        g_cross=((n_img, wide, 2 * width), bf16),
        g_ckv=((wide, 2 * wide), bf16),
        dx_rest=((n_img, caps - caps // 2, block_len, wide), bf16),
        grad_sum=((rows, wide), f32),
        low=((rows, wide), bf16),
        sums=((16, wide), f32),
        bias_sums=((n_img, inner // n_img), f32),
        image_half=((n_img, caps // 2, block_len, wide), bf16),
        s_out=((width, inner_dp), f32),
        s_in=((depth, inner // n_img), f32),
    )


def outer_scratch(dims):
    n_dp, n_img, caps, depth, width, inner_dp, block_len = dims
    wide, rows, inner = MODEL_WIDTH, caps * SEQ, n_dp * inner_dp
    tile = inner // n_img
    low, high = ((rows, wide), bf16), ((rows, wide), f32)
    return dict(
        vec=((16, wide), f32),
        bias=((n_img, tile), f32),
        sums=((16, wide), f32),
        bias_sums=((n_img, tile), f32),
        hidden_sums=((1, tile), f32),
        cot=low,
        second_sum=high,
        normed3=low,
        turned=((2 * wide, rows), bf16),
        result=high,
        grad=high,
        hidden=((rows, tile), f32),
        grad_act=((rows, tile), f32),
        activated=((rows, tile), bf16),
        grad_hidden=((rows, tile), bf16),
        in_tile=((2, wide, tile), bf16),
        out_tile=((2, wide, tile), bf16),
        stage_in=((wide, tile), bf16),
        stage_out=((wide, tile), bf16),
        low=low,
        mixed=low,
        query=low,
        normed2=low,
        kv=((n_img, caps, block_len, 2 * wide), bf16),
        images=((n_img, caps, block_len, wide), bf16),
        images_out=((n_img, caps, block_len, wide), bf16),
        stage_cross=((n_img, wide, 2 * width), bf16),
        stage_ckv=((wide, 2 * wide), bf16),
    )


def outer_groups(dims):
    n_dp, n_img, caps, depth, width, inner_dp, block_len = dims
    wide, inner = MODEL_WIDTH, n_dp * inner_dp
    return [
        Group(width, inner_dp, bf16, (wide, inner), turned_block),
        Group(depth, inner // n_img, bf16, (wide, inner), grid_block),
    ]


def outer_kernel(dims, *refs):
    n_dp, n_img, caps, depth, width, inner_dp, block_len = dims
    wide, rows, inner = MODEL_WIDTH, caps * SEQ, n_dp * inner_dp
    tile, half = inner // n_img, caps // 2
    inputs, outputs, scratch = outer_inputs(dims), outer_outputs(dims), outer_scratch(dims)
    counts, refs = refs[0], refs[1:]
    hbm, refs = bag(inputs, refs), refs[len(inputs) :]
    outs, refs = bag(outputs, refs), refs[len(outputs) :]
    s, refs = bag(scratch, refs), refs[len(scratch) :]
    groups = outer_groups(dims)
    buffers, refs = refs[: 5 * len(groups)], refs[5 * len(groups) :]
    here = Place(n_img)
    dp, im, core = here.dp, here.im, here.core
    red = Reducer(here, groups, buffers, refs[:9])
    copies = Copies(refs[9])
    dx_send, dx_recv = refs[10:]
    first_loads = [
        copies.start(getattr(hbm, name), getattr(s, name)) for name in list(inputs)[:4]
    ]
    def load_tile(t):
        cols = pl.ds(t * tile, tile)
        return [
            copies.start(hbm.in_w.at[:, cols], s.in_tile.at[t % 2]),
            copies.start(hbm.out_t.at[:, cols], s.out_tile.at[t % 2]),
        ]

    tiles = [load_tile(0), load_tile(1)]
    attention_loads = [
        copies.start(getattr(hbm, name), getattr(s, name))
        for name in inputs
        if name in ("mixed", "query", "kv", "images", "normed2")
    ]
    here.barrier()
    copies.wait(*first_loads)
    s.sums[...] = jnp.zeros_like(s.sums)
    step = Backward(dims, counts, s)
    step.begin()
    given = []
    for t in range(n_img):
        copies.wait(*tiles[t])
        step.feed_forward(s.bias[t : t + 1, :], s.in_tile.at[t % 2], s.out_tile.at[t % 2])
        s.bias_sums[t : t + 1, :] = s.hidden_sums[...]
        if t + 2 < n_img:
            tiles.append(load_tile(t + 2))
        for copy, sent in given:
            copy.wait()
            red.sends.wait(sent)
        s.stage_in[...] = dot(s.turned[0:wide, :], s.grad_hidden[...]).astype(bf16)
        given = []
        for c in (red.chip12, red.chip2, red.chip1, red.chip):
            own, other = tile_ds(2 * c + core, depth, 16), tile_ds(2 * c + 1 - core, depth, 16)
            given.append(red.give(1, c, t, s.stage_in.at[own, :], s.stage_in.at[other, :]))
        s.stage_out[...] = dot(s.turned[wide : 2 * wide, :], s.activated[...]).astype(bf16)
        for i in range(n_img):
            part = pl.ds(i * width, width)
            own, other = tile_ds(core, inner_dp, LANES), tile_ds(1 - core, inner_dp, LANES)
            given.append(red.give(0, t, i, s.stage_out.at[part, own], s.stage_out.at[part, other]))
        if t >= 1:
            for j in (1, 0):
                red.second(1, j, t - 1, True)
        if t >= 2:
            red.first(1, t - 2, True)
    for copy, sent in given:
        copy.wait()
        red.sends.wait(sent)
    square = [
        copies.start(hbm.weights.at[:, pl.ds((4 + n) * wide, wide)], s.in_tile.at[n]) for n in range(2)
    ]
    ckv = [copies.start(hbm.ckv.at[:, pl.ds(n * wide, wide)], s.out_tile.at[n]) for n in range(2)]
    first_sum = copies.start(hbm.first_sum, s.grad_act)
    for j in (1, 0):
        red.second(1, j, n_img - 1, True)
    for j in (1, 0):
        for i in range(n_img):
            red.second(0, j, i, True)
    red.first(1, n_img - 2, True)
    red.first(1, n_img - 1, True)

    def body(part):
        s.activated[part, :] = s.result[part, :].astype(bf16)

    for_rows(rows, 64, body)
    layer_out = copies.start(s.activated, outs.layer_out)
    s.grad_sum, s.grad_query, s.first_sum = s.hidden, s.grad_hidden, s.grad_act
    step.third_norm_back()
    copies.wait(*attention_loads)

    def spread(values, grads, n):
        for m in range(wide // 256):
            cols = slice(m * 256, (m + 1) * 256)
            s.stage_in[:, cols] = dot_left(values[...], grads[:, cols]).astype(bf16)
        for i in range(n_img):
            s.stage_cross[i, :, n * width : (n + 1) * width] = s.stage_in[:, i * width : (i + 1) * width]

    spread(s.mixed, s.low, 0)
    for i in range(n_img):
        red.first(0, i, True)
    copies.wait(layer_out, *square)
    s.grad_mixed, s.weights = s.activated, (None,) * 4 + (s.in_tile.at[0], s.in_tile.at[1])
    step.cross_grad()

    def caption(c, carry):
        step.cross_caption(c, s.kv.at[:, c], s.kv.at[:, c])
        return carry

    lax.fori_loop(0, half, caption, 0)
    for k in reversed(range(n_img)):
        red.line(1, k, True)
    lax.fori_loop(half, caps, caption, 0)
    for k in reversed(range(n_img)):
        red.line(0, k, True)
    copies.wait(*ckv)
    length = caps * block_len
    for k in (2, 1, 3, 0):
        target = (im + k) % n_img
        value = dot_right(s.kv[target, :, :, 0:wide].reshape(length, wide), s.out_tile[0])
        value = value + dot_right(s.kv[target, :, :, wide : 2 * wide].reshape(length, wide), s.out_tile[1])
        s.images_out[k] = value.astype(bf16).reshape(caps, block_len, wide)
        near, far = s.images_out.at[k, pl.ds(0, half)], s.images_out.at[k, pl.ds(half, caps - half)]
        if k == 0:
            copies.start(near, outs.image_half.at[im])
        else:
            red.sends.send(near, outs.image_half.at[im], dx_send.at[k], dx_recv.at[k], (dp, target))
        copies.start(far, outs.dx_rest.at[target])
    flat = n_img * length
    for n in range(2 * wide // 256):
        cols = slice(n * 256, (n + 1) * 256)
        part = s.kv[:, :, :, cols].reshape(flat, 256)
        s.stage_ckv[:, cols] = dot_left(s.images[...].reshape(flat, wide), part).astype(bf16)
    copies.start(s.stage_ckv, outs.g_ckv)
    copies.wait(first_sum)
    step.second_norm_back()
    spread(s.normed2, s.grad_query, 1)
    copies.start(s.stage_cross, outs.g_cross)
    copies.start(s.grad_sum, outs.grad_sum)
    copies.start(s.low, outs.low)
    copies.start(s.sums, outs.sums)
    copies.start(s.bias_sums, outs.bias_sums)
    red.last(0, outs.s_out)
    red.last(1, outs.s_in)
    for k in range(1, n_img):
        source = (im + n_img - k) % n_img
        block = outs.image_half.at[source]
        pltpu.make_async_remote_copy(
            block, block, dx_send.at[k], dx_recv.at[k], device_id=(dp, source), device_id_type=MESH
        ).wait_recv()
    red.sends.finish()
    copies.finish()


def specs_of(shapes, in_vmem=()):
    return [
        pl.BlockSpec(memory_space=pltpu.VMEM if name in in_vmem else pl.ANY) for name in shapes
    ]


def structs_of(shapes):
    return [jax.ShapeDtypeStruct(*shape) for shape in shapes.values()]


def outer_pass(dims, counts, values):
    inputs, outputs, scratch = outer_inputs(dims), outer_outputs(dims), outer_scratch(dims)
    n_img = dims[1]
    buffers, semaphores = Reducer.scratch(outer_groups(dims), n_img)
    dma = pltpu.SemaphoreType.DMA
    outs = pl.pallas_call(
        functools.partial(outer_kernel, dims),
        out_shape=structs_of(outputs),
        in_specs=[pl.BlockSpec(memory_space=pltpu.SMEM)] + specs_of(inputs),
        out_specs=specs_of(outputs, ("s_out", "s_in")),
        scratch_shapes=[pltpu.VMEM(*shape) for shape in scratch.values()]
        + buffers
        + semaphores
        + [dma((64,)), dma((n_img,)), dma((n_img,))],
        compiler_params=pltpu.CompilerParams(
            collective_id=2, has_side_effects=True, vmem_limit_bytes=62 << 20
        ),
    )(counts, *[values[name] for name in inputs])
    return dict(zip(outputs, outs))


def inner_inputs(dims):
    n_dp, n_img, caps, depth, width, inner_dp, block_len = dims
    wide, rows, inner = MODEL_WIDTH, caps * SEQ, n_dp * inner_dp
    low, high = ((rows, wide), bf16), ((rows, wide), f32)
    return dict(
        low=low,
        weights=((wide, 6 * wide), bf16),
        qkv=((rows, 3 * wide), bf16),
        self_mixed=low,
        normed1=low,
        vec=((16, wide), f32),
        sums=((16, wide), f32),
        bias_sums=((n_img, inner // n_img), f32),
        tokens=low,
        grad_sum=high,
        g_cross=((n_img, wide, 2 * width), bf16),
        g_ckv=((wide, 2 * wide), bf16),
        dx_rest=((n_img, caps - caps // 2, block_len, wide), bf16),
    )


def inner_outputs(dims):
    n_dp, n_img, caps, depth, width, inner_dp, block_len = dims
    return dict(
        token_grads=((caps * SEQ, MODEL_WIDTH), bf16),
        image_rest=((n_img, caps - caps // 2, block_len, MODEL_WIDTH), bf16),
        s_cross=((depth, 2 * width), f32),
        s_ckv=((depth, 2 * width), f32),
        s_self=((depth, 4 * width), f32),
        s_vec=((VEC_ROWS, LANES), f32),
    )


def inner_scratch(dims):
    n_dp, n_img, caps, depth, width, inner_dp, block_len = dims
    wide, rows, inner = MODEL_WIDTH, caps * SEQ, n_dp * inner_dp
    low, high = ((rows, wide), bf16), ((rows, wide), f32)
    return dict(
        low=low,
        weights=((wide, 4 * wide), bf16),
        qkv=((rows, 3 * wide), bf16),
        self_mixed=low,
        normed1=low,
        vec=((16, wide), f32),
        sums=((16, wide), f32),
        bias_sums=((n_img, inner // n_img), f32),
        tokens=low,
        grad_sum=high,
        grad=high,
        grad_mixed=low,
        grad_qkv=((rows, 3 * wide), bf16),
        token_grads=low,
        g_wide=((wide, 3 * wide), bf16),
        stage_self=((n_img, wide, 4 * width), bf16),
        vectors=((n_dp * VEC_ROWS, LANES), f32),
    )


def inner_groups(dims):
    n_dp, n_img, caps, depth, width, inner_dp, block_len = dims
    wide = MODEL_WIDTH
    return [
        Group(depth, 2 * width, bf16, (n_img, wide, 2 * width), stacked_block),
        Group(depth, 2 * width, bf16, (wide, 2 * wide), grid_block),
        Group(depth, 4 * width, bf16, (n_img, wide, 4 * width), stacked_block),
        Group(VEC_ROWS, LANES, f32, (n_dp * VEC_ROWS, LANES), repeated_block),
    ]


def inner_kernel(dims, *refs):
    n_dp, n_img, caps, depth, width, inner_dp, block_len = dims
    wide, rows = MODEL_WIDTH, caps * SEQ
    inputs, outputs, scratch = inner_inputs(dims), inner_outputs(dims), inner_scratch(dims)
    hbm, refs = bag(inputs, refs), refs[len(inputs) :]
    outs, refs = bag(outputs, refs), refs[len(outputs) :]
    s, refs = bag(scratch, refs), refs[len(scratch) :]
    groups = inner_groups(dims)
    buffers, refs = refs[: 5 * len(groups)], refs[5 * len(groups) :]
    here = Place(n_img)
    dp, im = here.dp, here.im
    red = Reducer(here, groups, buffers, refs[:9])
    copies = Copies(refs[9])
    dx_send, dx_recv = refs[10:]
    loads = []
    for name in list(inputs)[:10]:
        src = getattr(hbm, name)
        if name == "weights":
            src = src.at[:, pl.ds(0, 4 * wide)]
        loads.append(copies.start(src, getattr(s, name)))
    copies.start(hbm.dx_rest.at[im], outs.image_rest.at[im])
    here.barrier()
    chips = (red.chip12, red.chip2, red.chip1, red.chip)
    for g, full in enumerate((hbm.g_cross, hbm.g_ckv)):
        red.give_from(g, full, chips)
    for k in (2, 1, 3):
        target = (im + k) % n_img
        red.sends.send(
            hbm.dx_rest.at[target], outs.image_rest.at[im], dx_send.at[k], dx_recv.at[k], (dp, target)
        )
    copies.wait(*loads[:3])
    s.weights_all, s.weights = s.weights, tuple(s.weights.at[:, pl.ds(n * wide, wide)] for n in range(4))
    step = Backward(dims, None, s)
    step.self_grad()
    for g in range(2):
        for j in (1, 0):
            for i in range(n_img):
                red.second(g, j, i)
    step.self_attention(0, caps // 2)
    for i in range(n_img):
        red.first(0, i)
    step.self_attention(caps // 2, caps)
    for i in range(n_img):
        red.first(1, i)
    copies.wait(*loads[3:])
    turned_gradient(s.g_wide, s.normed1, s.grad_qkv)
    for i in range(n_img):
        s.stage_self[i, :, 0 : 3 * width] = s.g_wide[:, i * 3 * width : (i + 1) * 3 * width]
    turned_gradient(s.g_wide, s.self_mixed, s.low)
    for i in range(n_img):
        s.stage_self[i, :, 3 * width :] = s.g_wide[:, i * width : (i + 1) * width]
    red.give_from(2, s.stage_self, chips)
    step.first_norm_back()
    for j in (1, 0):
        for i in range(n_img):
            red.second(2, j, i)
    pack_vectors(s.sums, s.bias_sums, s.vectors, n_dp, depth, inner_dp)
    red.give_from(3, s.vectors, chips)
    copies.start(s.token_grads, outs.token_grads)
    for g in (0, 1):
        for k in reversed(range(1, n_img)):
            red.line(g, k)
        red.line(g, 0)
    for j in (1, 0):
        for i in range(n_img):
            red.second(3, j, i)
    for g in (2, 3):
        for i in range(n_img):
            red.first(g, i)
    for k in reversed(range(n_img)):
        for g in (2, 3):
            red.line(g, k)
    red.last(0, outs.s_cross)
    red.last(1, outs.s_ckv)
    red.last(2, outs.s_self)
    red.last(3, outs.s_vec)
    for k in range(1, n_img):
        source = (im + n_img - k) % n_img
        block = outs.image_rest.at[source]
        pltpu.make_async_remote_copy(
            block, block, dx_send.at[k], dx_recv.at[k], device_id=(dp, source), device_id_type=MESH
        ).wait_recv()
    red.sends.finish()
    copies.finish()


def inner_pass(dims, values):
    inputs, outputs, scratch = inner_inputs(dims), inner_outputs(dims), inner_scratch(dims)
    n_img = dims[1]
    buffers, semaphores = Reducer.scratch(inner_groups(dims), n_img)
    dma = pltpu.SemaphoreType.DMA
    outs = pl.pallas_call(
        functools.partial(inner_kernel, dims),
        out_shape=structs_of(outputs),
        in_specs=specs_of(inputs),
        out_specs=specs_of(outputs, ("s_cross", "s_ckv", "s_self", "s_vec")),
        scratch_shapes=[pltpu.VMEM(*shape) for shape in scratch.values()]
        + buffers
        + semaphores
        + [dma((64,)), dma((n_img,)), dma((n_img,))],
        compiler_params=pltpu.CompilerParams(
            collective_id=3, has_side_effects=True, vmem_limit_bytes=62 << 20
        ),
    )(*[values[name] for name in inputs])
    return dict(zip(outputs, outs))


def layer_norm(values, norm_gain, norm_shift):
    average = jnp.mean(values, axis=-1, keepdims=True)
    centred = values - average
    spread = jnp.mean(centred * centred, axis=-1, keepdims=True)
    return centred * lax.rsqrt(spread + norm_epsilon) * norm_gain + norm_shift


def matmul(left_op, right_op):
    return jnp.dot(left_op, right_op, preferred_element_type=f32)


def matmul_tleft(left_op, right_op):
    return lax.dot_general(
        left_op, right_op, (((0,), (0,)), ((), ())), preferred_element_type=f32
    )


def matmul_tright(left_op, right_op):
    return lax.dot_general(
        left_op, right_op, (((1,), (1,)), ((), ())), preferred_element_type=f32
    )


def column_sums(values):
    return jnp.sum(values.astype(f32), axis=0)


def to_heads(values, captions):
    return values.reshape(captions, -1, HEADS, HEAD)


def probabilities(queries, key_heads, allowed):
    scores = jnp.einsum("cqhd,ckhd->chqk", queries, key_heads, preferred_element_type=f32)
    scores = jnp.where(allowed, scores * HEAD ** (-0.5), masked_value)
    return jax.nn.softmax(scores, axis=-1)


def attention(queries, key_heads, value_heads, allowed):
    probs = probabilities(queries, key_heads, allowed).astype(bf16)
    return jnp.einsum("chqk,ckhd->cqhd", probs, value_heads, preferred_element_type=f32)


def attention_backward(queries, key_heads, value_heads, allowed, grad_mixed):
    probs = probabilities(queries, key_heads, allowed)
    grad_probs = jnp.einsum("cqhd,ckhd->chqk", grad_mixed, value_heads, preferred_element_type=f32)
    inner_term = jnp.sum(probs * grad_probs, axis=-1, keepdims=True)
    grad_scores = (probs * (grad_probs - inner_term)).astype(bf16)
    score_scale = HEAD ** (-0.5)
    grad_queries = (
        jnp.einsum("chqk,ckhd->cqhd", grad_scores, key_heads, preferred_element_type=f32)
        * score_scale
    )
    grad_keys = (
        jnp.einsum("chqk,cqhd->ckhd", grad_scores, queries, preferred_element_type=f32)
        * score_scale
    )
    grad_values = jnp.einsum(
        "chqk,cqhd->ckhd", probs.astype(bf16), grad_mixed, preferred_element_type=f32
    )
    return grad_queries.astype(bf16), grad_keys.astype(bf16), grad_values.astype(bf16)


def local_direct(
    n_dp,
    n_img,
    tokens,
    image_tokens,
    counts,
    mixed,
    cross_kv,
    mlp_in,
    mlp_out,
    norm_gains,
    shifts,
    mlp_bias,
    cotangent,
):
    captions = tokens.shape[0]
    depth = mixed.shape[0]
    width = mlp_out.shape[1]
    inner_dp = mlp_out.shape[0]
    rows_all = captions * SEQ
    dims = (n_dp, n_img, captions, depth, width, inner_dp, image_tokens.shape[1])
    narrow = jnp.pad(jnp.concatenate([norm_gains, shifts]), ((0, 0), (0, LANES - depth)))
    vectors = jnp.concatenate([narrow, mlp_bias.reshape(-1, LANES)])
    token_rows = tokens.reshape(rows_all, MODEL_WIDTH)
    values = entry_pass(
        dims, counts, (vectors, cross_kv, mixed, mlp_in, mlp_out.T), image_tokens, token_rows
    )
    values.update(cot=cotangent.reshape(rows_all, MODEL_WIDTH), tokens=token_rows)
    values.update(outer_pass(dims, counts, values))
    values.update(inner_pass(dims, values))
    get = SimpleNamespace(**values)
    image_out = jnp.concatenate([get.image_half, get.image_rest], axis=1).reshape(image_tokens.shape)
    return (
        get.layer_out.reshape(tokens.shape),
        get.token_grads.reshape(tokens.shape),
        image_out,
        get.s_self[:, : 3 * width],
        get.s_self[:, 3 * width :],
        get.s_cross[:, width:],
        get.s_ckv,
        get.s_cross[:, :width],
        get.s_in,
        get.s_out.T,
        get.s_vec[:3, :depth],
        get.s_vec[3:13, :depth],
        get.s_vec[13:].reshape(-1),
    )


def local(
    n_dp,
    n_img,
    tokens,
    image_tokens,
    token_counts,
    self_qkv,
    self_out,
    cross_q,
    cross_kv,
    cross_out,
    mlp_in,
    mlp_out,
    norm_gains,
    shifts,
    mlp_bias,
    cotangent,
):
    captions = tokens.shape[0]
    rows_all = captions * SEQ
    block_len = image_tokens.shape[1]
    width = self_out.shape[1]
    depth = self_out.shape[0]
    inner_dp = mlp_out.shape[0]
    direct = n_dp == 8 and depth % 16 == 0 and captions * n_img == image_tokens.shape[0]
    counts = lax.dynamic_slice_in_dim(token_counts, lax.axis_index("img") * captions, captions)

    mixed = jnp.concatenate([self_qkv, self_out, cross_q, cross_out], axis=1)
    if direct:
        return local_direct(
            n_dp,
            n_img,
            tokens,
            image_tokens,
            counts,
            mixed,
            cross_kv,
            mlp_in,
            mlp_out,
            norm_gains,
            shifts,
            mlp_bias,
            cotangent,
        )
    vectors = jnp.concatenate([norm_gains.reshape(-1), shifts.reshape(-1), mlp_bias])

    def everything(block, first, then, axes):
        return lax.all_gather(
            lax.all_gather(block, first, axis=axes[0], tiled=True), then, axis=axes[1], tiled=True
        )

    mixed_full = lax.all_gather(
        lax.all_gather(mixed, "dp", axis=0, tiled=True), "img", axis=0, tiled=False
    )
    ckv_w = everything(cross_kv, "img", "dp", (1, 0))
    in_w = everything(mlp_in, "img", "dp", (1, 0))
    outm_t = everything(mlp_out, "img", "dp", (1, 0)).T
    vec_full = lax.all_gather(vectors, "dp", axis=0, tiled=False)
    image_own = lax.all_to_all(
        image_tokens.reshape((n_img, captions) + image_tokens.shape[1:]), "img", 0, 0, tiled=True
    )

    def columns(start, size):
        return (
            mixed_full[:, :, start * width : (start + size) * width]
            .transpose(1, 0, 2)
            .reshape(MODEL_WIDTH, size * MODEL_WIDTH)
        )

    qkv_w, sout_w, cq_w, cout_w = columns(0, 3), columns(3, 1), columns(4, 1), columns(5, 1)
    gain_rows = vec_full[:, : 3 * depth].reshape(n_dp, 3, depth).transpose(1, 0, 2).reshape(3, -1)
    shift_rows = (
        vec_full[:, 3 * depth : 13 * depth]
        .reshape(n_dp, 10, depth)
        .transpose(1, 0, 2)
        .reshape(10, -1)
    )
    inner_bias = vec_full[:, 13 * depth :].reshape(-1)

    zero_row = jnp.zeros((MODEL_WIDTH,), f32)
    rows = tokens.reshape(rows_all, MODEL_WIDTH).astype(f32)
    normed1 = layer_norm(rows, gain_rows[0], shift_rows[0]).astype(bf16)
    mixed_qkv = (
        matmul(normed1, qkv_w) + jnp.concatenate([shift_rows[3], zero_row, shift_rows[4]])
    ).astype(bf16)
    self_queries, self_keys, self_values = [
        to_heads(mixed_qkv[:, n * MODEL_WIDTH : (n + 1) * MODEL_WIDTH], captions) for n in range(3)
    ]
    places = jnp.arange(SEQ, dtype=jnp.int32)
    causal = (places[None, :] <= places[:, None])[None, None]
    self_mixed = attention(self_queries, self_keys, self_values, causal)
    self_mixed = self_mixed.reshape(rows_all, MODEL_WIDTH).astype(bf16)
    first_sum = rows + matmul(self_mixed, sout_w) + shift_rows[5]
    normed2 = layer_norm(first_sum, gain_rows[1], shift_rows[1]).astype(bf16)
    cross_query = (matmul(normed2, cq_w) + shift_rows[6]).astype(bf16)
    cross_queries = to_heads(cross_query, captions)

    image_len = n_img * block_len
    image_rows = image_own.reshape(n_img * captions * block_len, MODEL_WIDTH)
    image_kv = (matmul(image_rows, ckv_w) + jnp.concatenate([zero_row, shift_rows[7]])).astype(bf16)

    def by_caption(values):
        return (
            values.reshape(n_img, captions, block_len, HEADS, HEAD)
            .transpose(1, 0, 2, 3, 4)
            .reshape(captions, image_len, HEADS, HEAD)
        )

    def by_place(values):
        return (
            values.reshape(captions, n_img, block_len, MODEL_WIDTH)
            .transpose(1, 0, 2, 3)
            .reshape(-1, MODEL_WIDTH)
        )

    cross_keys = by_caption(image_kv[:, :MODEL_WIDTH])
    cross_values = by_caption(image_kv[:, MODEL_WIDTH:])
    valid = (jnp.arange(image_len, dtype=jnp.int32)[None, :] < counts[:, None])[:, None, None, :]
    cross_mixed = attention(cross_queries, cross_keys, cross_values, valid)
    cross_mixed = cross_mixed.reshape(rows_all, MODEL_WIDTH).astype(bf16)
    second_sum = first_sum + matmul(cross_mixed, cout_w) + shift_rows[8]
    normed3 = layer_norm(second_sum, gain_rows[2], shift_rows[2]).astype(bf16)
    hidden = matmul(normed3, in_w) + inner_bias
    activated = jax.nn.gelu(hidden, approximate=False).astype(bf16)
    result = second_sum + matmul_tright(activated, outm_t) + shift_rows[9]
    layer_out = result.reshape(tokens.shape).astype(bf16)

    grad_low3 = cotangent.reshape(rows_all, MODEL_WIDTH)
    g_outm_t = matmul_tleft(grad_low3, activated)
    g_shift9 = column_sums(grad_low3)
    grad_act = matmul(grad_low3, outm_t)
    _, gelu_pull = jax.vjp(lambda pre_act: jax.nn.gelu(pre_act, approximate=False), hidden)
    grad_hidden = gelu_pull(grad_act)[0].astype(bf16)
    g_in = matmul_tleft(normed3, grad_hidden)
    g_inner_bias = column_sums(grad_hidden)
    grad_normed3 = matmul_tright(grad_hidden, in_w)
    _, norm_pull3 = jax.vjp(layer_norm, second_sum, gain_rows[2], shift_rows[2])
    grad_second_ln, g_gain2, g_shift2 = norm_pull3(grad_normed3)
    grad_second = grad_low3.astype(f32) + grad_second_ln
    grad_low2 = grad_second.astype(bf16)
    g_cout = matmul_tleft(cross_mixed, grad_low2)
    g_shift8 = column_sums(grad_low2)
    grad_cross_mixed = to_heads(matmul_tright(grad_low2, cout_w).astype(bf16), captions)
    grad_query, grad_ckeys, grad_cvalues = attention_backward(
        cross_queries, cross_keys, cross_values, valid, grad_cross_mixed
    )
    grad_query = grad_query.reshape(rows_all, MODEL_WIDTH)
    g_cq = matmul_tleft(normed2, grad_query)
    g_shift6 = column_sums(grad_query)
    grad_normed2 = matmul_tright(grad_query, cq_w)
    grad_value_rows = by_place(grad_cvalues)
    grad_image_kv = jnp.concatenate([by_place(grad_ckeys), grad_value_rows], axis=1)
    g_ckv = matmul_tleft(image_rows, grad_image_kv)
    g_shift7 = column_sums(grad_value_rows)
    image_grads = matmul_tright(grad_image_kv, ckv_w).astype(bf16).reshape(image_own.shape)
    _, norm_pull2 = jax.vjp(layer_norm, first_sum, gain_rows[1], shift_rows[1])
    grad_first_ln, g_gain1, g_shift1 = norm_pull2(grad_normed2)
    grad_first = grad_second + grad_first_ln
    grad_low1 = grad_first.astype(bf16)
    g_sout = matmul_tleft(self_mixed, grad_low1)
    g_shift5 = column_sums(grad_low1)
    grad_self_mixed = to_heads(matmul_tright(grad_low1, sout_w).astype(bf16), captions)
    grad_qkv = jnp.concatenate(
        [
            part.reshape(rows_all, MODEL_WIDTH)
            for part in attention_backward(
                self_queries, self_keys, self_values, causal, grad_self_mixed
            )
        ],
        axis=1,
    )
    g_qkv = matmul_tleft(normed1, grad_qkv)
    qkv_sums = column_sums(grad_qkv)
    g_shift3, g_shift4 = qkv_sums[:MODEL_WIDTH], qkv_sums[2 * MODEL_WIDTH :]
    grad_normed1 = matmul_tright(grad_qkv, qkv_w)
    _, norm_pull1 = jax.vjp(layer_norm, rows, gain_rows[0], shift_rows[0])
    grad_rows_ln, g_gain0, g_shift0 = norm_pull1(grad_normed1)
    token_grads = (grad_first + grad_rows_ln).reshape(tokens.shape).astype(bf16)
    g_vector_rows = jnp.stack(
        [
            g_gain0,
            g_gain1,
            g_gain2,
            g_shift0,
            g_shift1,
            g_shift2,
            g_shift3,
            g_shift4,
            g_shift5,
            g_shift6,
            g_shift7,
            g_shift8,
            g_shift9,
        ]
    )

    def scattered(grad):
        tall = lax.psum_scatter(grad, "dp", scatter_dimension=0, tiled=True)
        return lax.psum_scatter(tall, "img", scatter_dimension=1, tiled=True)

    s_qkv, s_sout, s_cq, s_ckv, s_cout, s_in, s_outm = [
        scattered(g) for g in (g_qkv, g_sout, g_cq, g_ckv, g_cout, g_in, g_outm_t.T)
    ]
    s_rows, s_inner = lax.psum(
        (
            lax.psum_scatter(g_vector_rows, "dp", scatter_dimension=1, tiled=True),
            lax.psum_scatter(g_inner_bias, "dp", scatter_dimension=0, tiled=True),
        ),
        "img",
    )
    image_out = lax.all_to_all(image_grads, "img", 0, 0, tiled=True).reshape(image_tokens.shape)
    return (
        layer_out,
        token_grads,
        image_out,
        s_qkv,
        s_sout,
        s_cq,
        s_ckv,
        s_cout,
        s_in,
        s_outm,
        s_rows[:3],
        s_rows[3:],
        s_inner,
    )


def solution(mesh):
    caption_rows = P(("dp", "img"), None, None)
    weight = P("dp", "img")
    vector = P(None, "dp")
    in_specs = (caption_rows, P("dp", "img", None), P("dp")) + (weight,) * 7
    in_specs += (vector, vector, P("dp"), caption_rows)
    out_specs = (caption_rows, caption_rows, P("dp", "img", None)) + (weight,) * 7
    out_specs += (vector, vector, P("dp"))
    return jax.shard_map(
        functools.partial(local, mesh.shape["dp"], mesh.shape["img"]),
        mesh=mesh,
        in_specs=in_specs,
        out_specs=out_specs,
        check_vma=False,
    )
```

```python
import functools
from types import SimpleNamespace

import jax
import jax.numpy as jnp
from jax import lax
from jax.experimental import pallas as pl
from jax.experimental.pallas import tpu as pltpu
from jax.sharding import PartitionSpec as P

MODEL_WIDTH = 768
HEADS = 12
HEAD = 64
SEQ = 64
VEC_ROWS = 16
LANES = 128
MESH = pl.DeviceIdType.MESH
bf16 = jnp.bfloat16
f32 = jnp.float32

masked_value = -1e30
norm_epsilon = 1e-05


def tile_ds(index, size, unit):
    return pl.ds(pl.multiple_of(index * size, unit), size)


def stacked_block(rows, cols):
    return lambda ref, d, i: ref.at[i, tile_ds(d, rows, 16), :]


def grid_block(rows, cols):
    return lambda ref, d, i: ref.at[tile_ds(d, rows, 16), tile_ds(i, cols, LANES)]


def turned_block(rows, cols):
    return lambda ref, d, i: ref.at[tile_ds(i, rows, 16), tile_ds(d, cols, LANES)]


def repeated_block(rows, cols):
    return lambda ref, d, i: ref.at[tile_ds(d, rows, 8), :]


class Group:
    def __init__(self, rows, cols, dtype, full, block):
        self.rows, self.cols, self.dtype, self.full = rows, cols, dtype, full
        self.block = block(rows, cols)


def flip(d, bit):
    return d + bit * (1 - 2 * ((d // bit) % 2))


class Place:
    def __init__(self, n_img):
        self.n_img = n_img
        self.dp, self.im = lax.axis_index("dp"), lax.axis_index("img")
        self.core = self.dp % 2
        self.sib = flip(self.dp, 1)

    def first(self, d):
        return flip(d, 2) * (1 - self.core) + flip(d, 4) * self.core

    def second(self, d):
        return flip(d, 4) * (1 - self.core) + flip(d, 2) * self.core

    def near(self, k):
        value = jnp.int32(0)
        for at in range(self.n_img):
            order = sorted(range(self.n_img), key=lambda other: (abs(other - at), other))
            value = jnp.where(self.im == at, order[k], value)
        return value

    def barrier(self):
        semaphore = pltpu.get_barrier_semaphore()
        peers = [(self.sib, self.im), (self.first(self.dp), self.im), (self.second(self.dp), self.im)]
        peers += [(self.dp, (self.im + k) % self.n_img) for k in range(1, self.n_img)]
        for peer in peers:
            pl.semaphore_signal(semaphore, inc=1, device_id=peer, device_id_type=MESH)
        pl.semaphore_wait(semaphore, len(peers))


class Sends:
    def __init__(self):
        self.started = []

    def send(self, src, dst, send_sem, recv_sem, device, when=None):
        copy = pltpu.make_async_remote_copy(
            src, dst, send_sem, recv_sem, device_id=device, device_id_type=MESH
        )
        entry = (when, copy)
        self.started.append(entry)
        if when is None:
            copy.start()
        else:
            pl.when(when)(copy.start)
        return entry

    def send_copy(self, copy):
        self.started.append((None, copy))
        copy.start()

    def wait(self, *entries):
        for entry in entries:
            self.started = [other for other in self.started if other is not entry]
            when, copy = entry
            if when is None:
                copy.wait_send()
            else:
                pl.when(when)(copy.wait_send)

    def finish(self):
        self.wait(*self.started)


def dot(left, right):
    return jnp.dot(left, right, preferred_element_type=f32)


def dot_left(left, right):
    return lax.dot_general(left, right, (((0,), (0,)), ((), ())), preferred_element_type=f32)


def dot_right(left, right):
    return lax.dot_general(left, right, (((1,), (1,)), ((), ())), preferred_element_type=f32)


def for_rows(count, size, body):
    def step(r, carry):
        body(pl.ds(pl.multiple_of(r * size, size), size))
        return carry

    lax.fori_loop(0, count // size, step, 0)


def standard(values):
    average = jnp.mean(values, axis=-1, keepdims=True)
    centred = values - average
    spread = jnp.mean(centred * centred, axis=-1, keepdims=True)
    rate = lax.rsqrt(spread + norm_epsilon)
    return centred * rate, rate


def add_into(dst, src):
    dst[...] = (dst[...].astype(f32) + src[...].astype(f32)).astype(dst.dtype)


def norm_rows(out, values, gain, shift):
    def body(part):
        unit, _ = standard(values[part, :].astype(f32))
        out[part, :] = (unit * gain + shift).astype(bf16)

    for_rows(out.shape[0], 64, body)


def norm_rows_back(grad, values, gain, add, out, sums, low, gain_row, shift_row, low_row):
    zero = jnp.zeros((1, MODEL_WIDTH), f32)
    sums[gain_row : gain_row + 1, :] = zero
    sums[shift_row : shift_row + 1, :] = zero
    if low_row is not None:
        sums[low_row : low_row + 1, :] = zero

    def body(part):
        unit, rate = standard(values[part, :].astype(f32))
        grad_part = grad[part, :]
        scaled = grad_part * gain
        inner = jnp.mean(scaled, axis=-1, keepdims=True)
        along = jnp.mean(scaled * unit, axis=-1, keepdims=True)
        total = add[part, :].astype(f32) + rate * (scaled - inner - unit * along)
        rounded = total.astype(bf16)
        if out is not None:
            out[part, :] = total
        low[part, :] = rounded
        sums[gain_row : gain_row + 1, :] += jnp.sum(grad_part * unit, axis=0, keepdims=True)
        sums[shift_row : shift_row + 1, :] += jnp.sum(grad_part, axis=0, keepdims=True)
        if low_row is not None:
            sums[low_row : low_row + 1, :] += jnp.sum(rounded.astype(f32), axis=0, keepdims=True)

    for_rows(grad.shape[0], 64, body)


QUAD = 4 * HEAD


def head_mask():
    lane_head = lax.broadcasted_iota(jnp.int32, (4, SEQ, QUAD), 2) // HEAD
    return lane_head == lax.broadcasted_iota(jnp.int32, (4, SEQ, QUAD), 0)


def by_head(values, mask):
    return jnp.where(mask, values.astype(f32)[None], 0.0).reshape(4 * SEQ, QUAD).astype(bf16)


def from_head(values, mask):
    return jnp.sum(jnp.where(mask, values.reshape(4, SEQ, QUAD), 0.0), axis=0)


def weights_of(queries, keys, allowed):
    scores = jnp.where(allowed, dot_right(queries, keys) * HEAD ** (-0.5), masked_value)
    top = jnp.max(scores, axis=-1, keepdims=True)
    weights = jnp.exp(scores - top)
    return weights * (1.0 / jnp.sum(weights, axis=-1, keepdims=True))


def attend(query, keys, values, allowed, mask):
    probs = weights_of(by_head(query, mask), keys, allowed).astype(bf16)
    return from_head(dot(probs, values), mask).astype(bf16)


def attend_back(query, keys, values, allowed, mask, grad_mixed):
    queries, grads = by_head(query, mask), by_head(grad_mixed, mask)
    probs = weights_of(queries, keys, allowed)
    grad_probs = dot_right(grads, values)
    inner = jnp.sum(probs * grad_probs, axis=-1, keepdims=True)
    grad_scores = (probs * (grad_probs - inner)).astype(bf16)
    scale = HEAD ** (-0.5)
    return (
        (from_head(dot(grad_scores, keys), mask) * scale).astype(bf16),
        (dot_left(grad_scores, queries) * scale).astype(bf16),
        dot_left(probs.astype(bf16), grads).astype(bf16),
    )


def causal_mask():
    shape = (4 * SEQ, SEQ)
    query = lax.broadcasted_iota(jnp.int32, shape, 0) % SEQ
    return lax.broadcasted_iota(jnp.int32, shape, 1) <= query


def unpack_vectors(blocks, vec, bias, n_dp, depth, inner_dp):
    for d in range(n_dp):
        row = d * VEC_ROWS
        vec[0:13, d * depth : (d + 1) * depth] = blocks[row : row + 13, 0:depth]
        for j in range(inner_dp // LANES):
            at, col = divmod(d * inner_dp + j * LANES, bias.shape[1])
            bias[at : at + 1, col : col + LANES] = blocks[row + 13 + j : row + 14 + j, :]


def pack_vectors(vec, bias, blocks, n_dp, depth, inner_dp):
    blocks[...] = jnp.zeros_like(blocks)
    for d in range(n_dp):
        row = d * VEC_ROWS
        blocks[row : row + 13, 0:depth] = vec[0:13, d * depth : (d + 1) * depth]
        for j in range(inner_dp // LANES):
            at, col = divmod(d * inner_dp + j * LANES, bias.shape[1])
            blocks[row + 13 + j : row + 14 + j, :] = bias[at : at + 1, col : col + LANES]


class Copies:
    def __init__(self, semaphores):
        self.semaphores, self.used, self.open = semaphores, 0, []

    def start(self, src, dst):
        copy = pltpu.make_async_copy(src, dst, self.semaphores.at[self.used])
        self.used += 1
        copy.start()
        self.open.append(copy)
        return copy

    def wait(self, *copies):
        for copy in copies:
            self.open = [other for other in self.open if other is not copy]
            copy.wait()

    def finish(self):
        self.wait(*self.open)


def kept_shapes(dims):
    n_dp, n_img, caps, depth, width, inner_dp, block_len = dims
    rows, wide, inner = caps * SEQ, MODEL_WIDTH, n_dp * inner_dp
    low, high = ((rows, wide), bf16), ((rows, wide), f32)
    return dict(
        weights=((wide, 6 * wide), bf16),
        normed1=low,
        qkv=((rows, 3 * wide), bf16),
        self_mixed=low,
        first_sum=high,
        normed2=low,
        query=low,
        kv=((n_img, caps, block_len, 2 * wide), bf16),
        mixed=low,
        second_sum=high,
        vec=((16, wide), f32),
        bias=((n_img, inner // n_img), f32),
        images=((n_img, caps, block_len, wide), bf16),
        ckv=((wide, 2 * wide), bf16),
    )


class Forward:
    def __init__(self, dims, counts, raw, tokens, kept):
        self.n_img, self.width = dims[1], dims[4]
        self.counts, self.raw, self.tokens, self.kept = counts, raw, tokens, kept

    def gain(self, k):
        return self.kept.vec[k : k + 1, :]

    def shift(self, k):
        return self.kept.vec[3 + k : 4 + k, :]

    def first_norm(self):
        norm_rows(self.kept.normed1, self.tokens, self.gain(0), self.shift(0))

    def assemble(self, i):
        weights, w, wide = self.kept.weights, self.width, MODEL_WIDTH
        weights[:, i * 3 * w : (i + 1) * 3 * w] = self.raw[i, :, 0 : 3 * w]
        for n in range(3):
            at = (3 + n) * wide + i * w
            weights[:, at : at + w] = self.raw[i, :, (3 + n) * w : (4 + n) * w]

    def image_kv(self, i):
        wide = MODEL_WIDTH
        kv = self.kept.kv
        block = self.kept.images[i]
        rows = block.shape[0] * block.shape[1]
        block = block.reshape(rows, wide)
        for n in range(2):
            value = dot(block, self.kept.ckv[:, n * wide : (n + 1) * wide])
            if n == 1:
                value = value + self.shift(7)
            kv[i, :, :, n * wide : (n + 1) * wide] = value.astype(bf16).reshape(kv.shape[1:3] + (wide,))

    def project(self):
        wide, qkv = MODEL_WIDTH, self.kept.qkv
        for n, shift in enumerate((3, None, 4)):
            value = dot(self.kept.normed1[...], self.kept.weights[:, n * wide : (n + 1) * wide])
            if shift is not None:
                value = value + self.shift(shift)
            qkv[:, n * wide : (n + 1) * wide] = value.astype(bf16)

    def self_attention(self, start, stop):
        qkv, out, wide = self.kept.qkv, self.kept.self_mixed, MODEL_WIDTH
        allowed, mask = causal_mask(), head_mask()

        def caption(c, carry):
            part = pl.ds(pl.multiple_of(c * SEQ, SEQ), SEQ)
            for t in range(wide // QUAD):
                at = t * QUAD
                out[part, at : at + QUAD] = attend(
                    qkv[part, at : at + QUAD],
                    qkv[part, wide + at : wide + at + QUAD],
                    qkv[part, 2 * wide + at : 2 * wide + at + QUAD],
                    allowed,
                    mask,
                )
            return carry

        lax.fori_loop(start, stop, caption, 0)

    def add_product(self, left, n, shift, base, out):
        wide = MODEL_WIDTH
        out[...] = dot(left[...], self.kept.weights[:, n * wide : (n + 1) * wide])
        row = self.shift(shift)

        def body(part):
            out[part, :] = base[part, :].astype(f32) + (out[part, :] + row)

        for_rows(out.shape[0], 64, body)

    def first_residual(self):
        wide = MODEL_WIDTH
        self.add_product(self.kept.self_mixed, 3, 5, self.tokens, self.kept.first_sum)
        norm_rows(self.kept.normed2, self.kept.first_sum, self.gain(1), self.shift(1))
        value = dot(self.kept.normed2[...], self.kept.weights[:, 4 * wide : 5 * wide])
        self.kept.query[...] = (value + self.shift(6)).astype(bf16)

    def valid_keys(self, c):
        shape = (4 * SEQ, self.n_img * self.kept.kv.shape[2])
        return lax.broadcasted_iota(jnp.int32, shape, 1) < self.counts[c]

    def cross_attention(self, start, stop):
        query, kv, out, wide = self.kept.query, self.kept.kv, self.kept.mixed, MODEL_WIDTH
        mask = head_mask()
        length = self.n_img * kv.shape[2]

        def caption(c, carry):
            part = pl.ds(pl.multiple_of(c * SEQ, SEQ), SEQ)
            allowed = self.valid_keys(c)
            for t in range(wide // QUAD):
                at = t * QUAD
                out[part, at : at + QUAD] = attend(
                    query[part, at : at + QUAD],
                    kv[:, c, :, at : at + QUAD].reshape(length, QUAD),
                    kv[:, c, :, wide + at : wide + at + QUAD].reshape(length, QUAD),
                    allowed,
                    mask,
                )
            return carry

        lax.fori_loop(start, stop, caption, 0)

    def second_residual(self):
        self.add_product(self.kept.mixed, 5, 8, self.kept.first_sum, self.kept.second_sum)


class Gatherer:
    def __init__(self, here, groups, own, full, send_sem, recv_sem):
        self.here, self.groups, self.own, self.full = here, groups, own, full
        self.send_sem, self.recv_sem = send_sem, recv_sem
        self.sends, self.used = Sends(), [0] * len(groups)

    def forward(self, g, d, i, src, device, when=None):
        self.sends.send(
            src,
            self.groups[g].block(self.full[g], d, i),
            self.send_sem.at[g, self.used[g]],
            self.recv_sem.at[g, d, i],
            device,
            when,
        )
        self.used[g] += 1

    def arrived(self, g, d, i):
        block, here = self.groups[g].block(self.full[g], d, i), self.here
        pltpu.make_async_remote_copy(
            block,
            block,
            self.send_sem.at[g, 0],
            self.recv_sem.at[g, d, i],
            device_id=(here.sib, here.im),
            device_id_type=MESH,
        ).wait_recv()
        return block

    def to_planes(self, g, d, i, block):
        here = self.here
        self.forward(g, d, i, block, (here.first(here.dp), here.im))
        self.forward(g, d, i, block, (here.second(here.dp), here.im))
        self.forward(g, d, i, block, (here.sib, here.im))

    def start(self, g):
        here = self.here
        dp, im = here.dp, here.im
        self.forward(g, dp, im, self.own[g], (dp, im + 1), im < here.n_img - 1)
        self.forward(g, dp, im, self.own[g], (dp, im - 1), im > 0)
        self.to_planes(g, dp, im, self.own[g])

    def line(self, g, k):
        here = self.here
        dp, im, i = here.dp, here.im, here.near(k)
        block = self.arrived(g, dp, i)
        after = im + jnp.where(i < im, 1, -1)
        self.forward(g, dp, i, block, (dp, after), (after >= 0) & (after < here.n_img))
        self.to_planes(g, dp, i, block)

    def first(self, g, k):
        here = self.here
        d, i = here.first(here.dp), here.near(k)
        block = self.arrived(g, d, i)
        self.forward(g, d, i, block, (here.second(here.dp), here.im))
        self.forward(g, d, i, block, (here.sib, here.im))

    def second(self, g, k):
        here = self.here
        i = here.near(k)
        for d in (here.second(here.dp), here.second(here.first(here.dp))):
            block = self.arrived(g, d, i)
            self.forward(g, d, i, block, (here.sib, here.im))

    def complete(self, g):
        for c in range(4):
            for i in range(self.here.n_img):
                self.arrived(g, 2 * c + 1 - self.here.core, i)


X_PARTS = 4
LAGS = (6, 12)
X_EVERY = 4


def entry_groups(dims):
    n_dp, n_img, caps, depth, width, inner_dp, block_len = dims
    wide, inner = MODEL_WIDTH, n_dp * inner_dp
    return [
        Group(VEC_ROWS, LANES, f32, (n_img, n_dp * VEC_ROWS, LANES), stacked_block),
        Group(depth, 2 * width, bf16, (wide, 2 * wide), grid_block),
        Group(depth, 6 * width, bf16, (n_img, wide, 6 * width), stacked_block),
        Group(depth, inner // n_img, bf16, (wide, inner), grid_block),
        Group(width, inner_dp, bf16, (wide, inner), turned_block),
    ]


def entry_kernel(dims, *refs):
    n_dp, n_img, caps, depth, width, inner_dp, block_len = dims
    groups, shapes = entry_groups(dims), kept_shapes(dims)
    count = len(groups)
    counts, own, (x_ref, tokens_hbm) = refs[0], refs[1 : 1 + count], refs[1 + count : 3 + count]
    refs = refs[3 + count :]
    outs, (in_w, out_t) = bag(shapes, refs), refs[len(shapes) : len(shapes) + 2]
    refs = refs[len(shapes) + 2 :]
    kept, refs = bag(shapes, refs), refs[len(shapes) :]
    vec_full, raw, tokens, send_sem, recv_sem, xs_sem, xr_sem, local_sem = refs
    here = Place(n_img)
    dp, im = here.dp, here.im
    copies = Copies(local_sem)
    full = (vec_full, kept.ckv, raw, in_w, out_t)
    gather = Gatherer(here, groups, own, full, send_sem, recv_sem)
    local_blocks = [
        copies.start(own[g], groups[g].block(full[g], dp, im)) for g in range(count)
    ]
    own_images = copies.start(x_ref.at[pl.ds(im * caps, caps)], kept.images.at[im])
    token_load = copies.start(tokens_hbm, tokens)
    here.barrier()
    for g in range(count):
        gather.start(g)
    part_caps = caps // X_PARTS

    def x_copy(k, p, target, source):
        return pltpu.make_async_remote_copy(
            x_ref.at[pl.ds(target * caps + p * part_caps, part_caps)],
            kept.images.at[source, pl.ds(p * part_caps, part_caps)],
            xs_sem.at[k, p],
            xr_sem.at[k, p],
            device_id=(dp, target),
            device_id_type=MESH,
        )

    waiting = [(k, p) for p in range(X_PARTS) for k in range(1, n_img)][::-1]
    ticks = [0]

    def tick():
        ticks[0] += 1
        if ticks[0] % X_EVERY == 0 and waiting:
            k, p = waiting.pop()
            gather.sends.send_copy(x_copy(k, p, (im + k) % n_img, im))

    units = [(g, k) for g in range(count) for k in range(n_img)]

    def exchange(t):
        if t < len(units):
            g, k = units[t]
            if k > 0:
                gather.line(g, k)
                tick()
        if 0 <= t - LAGS[0] < len(units):
            gather.first(*units[t - LAGS[0]])
            tick()
        if 0 <= t - LAGS[1] < len(units):
            gather.second(*units[t - LAGS[1]])
            tick()

    def images_from(k):
        source = (im + n_img - k) % n_img
        if k > 0:
            for p in range(X_PARTS):
                x_copy(k, p, source, source).wait_recv()
        copies.start(kept.images.at[source], outs.images.at[source])
        step.image_kv(source)
        copies.start(kept.kv.at[source], outs.kv.at[source])

    step = Forward(dims, counts, raw, tokens, kept)
    done = LAGS[1] + n_img
    for t in range(len(units) + LAGS[1]):
        exchange(t)
        if t == done:
            gather.complete(0)
            copies.wait(local_blocks[0], token_load)
            unpack_vectors(vec_full.at[0], kept.vec, kept.bias, n_dp, depth, inner_dp)
            step.first_norm()
        if t == done + n_img:
            gather.complete(1)
            copies.wait(local_blocks[1], own_images)
            images_from(0)
        if t == done + 2 * n_img:
            gather.complete(2)
            copies.wait(local_blocks[2])
            for i in range(n_img):
                step.assemble(i)
            step.project()
        if t == done + 2 * n_img + 2:
            step.self_attention(0, caps // 2)
        if t == done + 2 * n_img + 4:
            step.self_attention(caps // 2, caps)
    copies.start(kept.vec, outs.vec)
    copies.start(kept.bias, outs.bias)
    copies.start(kept.ckv, outs.ckv)
    copies.start(kept.weights, outs.weights)
    copies.start(kept.normed1, outs.normed1)
    copies.start(kept.qkv, outs.qkv)
    copies.start(kept.self_mixed, outs.self_mixed)
    step.first_residual()
    copies.start(kept.first_sum, outs.first_sum)
    copies.start(kept.normed2, outs.normed2)
    copies.start(kept.query, outs.query)
    for k in (1, n_img - 1) + tuple(range(2, n_img - 1)):
        images_from(k)
    step.cross_attention(0, caps)
    copies.start(kept.mixed, outs.mixed)
    step.second_residual()
    copies.start(kept.second_sum, outs.second_sum)
    for g in range(3, count):
        gather.complete(g)
    gather.sends.finish()
    copies.finish()


def entry_pass(dims, counts, owns, image_tokens, tokens):
    n_dp, n_img, caps, depth, width, inner_dp, block_len = dims
    groups, shapes = entry_groups(dims), kept_shapes(dims)
    count = len(groups)
    dma = pltpu.SemaphoreType.DMA
    any_spec = pl.BlockSpec(memory_space=pl.ANY)
    outs = pl.pallas_call(
        functools.partial(entry_kernel, dims),
        out_shape=structs_of(shapes) + [jax.ShapeDtypeStruct(g.full, g.dtype) for g in groups[3:]],
        in_specs=[pl.BlockSpec(memory_space=pltpu.SMEM)] + [any_spec] * (count + 2),
        out_specs=[any_spec] * (len(shapes) + 2),
        scratch_shapes=[pltpu.VMEM(*shape) for shape in shapes.values()]
        + [pltpu.VMEM(groups[0].full, f32), pltpu.VMEM(groups[2].full, bf16), pltpu.VMEM(tokens.shape, bf16)]
        + [
            dma((count, 64)),
            dma((count, n_dp, n_img)),
            dma((n_img, X_PARTS)),
            dma((n_img, X_PARTS)),
            dma((48,)),
        ],
        compiler_params=pltpu.CompilerParams(
            collective_id=1, has_side_effects=True, vmem_limit_bytes=62 << 20
        ),
    )(counts, *owns, image_tokens, tokens)
    kept = dict(zip(shapes, outs))
    kept.update(in_w=outs[-2], out_t=outs[-1])
    return kept


class Backward:
    def __init__(self, dims, counts, refs):
        self.dims, self.counts, self.refs = dims, counts, refs

    def __getattr__(self, name):
        return getattr(self.refs, name)

    def gain(self, k):
        return self.vec[k : k + 1, :]

    def weight(self, n):
        return self.weights[n][...]

    def sum_row(self, k, values):
        self.sums[3 + k : 4 + k, :] = jnp.sum(values.astype(f32), axis=0, keepdims=True)

    def begin(self):
        wide = MODEL_WIDTH
        norm_rows(self.normed3, self.second_sum, self.gain(2), self.vec[5:6, :])
        self.sum_row(9, self.cot[...])
        self.turned[0:wide, :] = self.normed3[...].astype(f32).T.astype(bf16)
        self.turned[wide : 2 * wide, :] = self.cot[...].astype(f32).T.astype(bf16)
        row = self.vec[12:13, :]

        def body(part):
            self.result[part, :] = self.second_sum[part, :] + row
            self.grad[part, :] = jnp.zeros((64, wide), f32)

        for_rows(self.result.shape[0], 64, body)

    def feed_forward(self, bias, in_w, out_t):
        rows = self.normed3.shape[0]
        self.hidden[...] = dot(self.normed3[...], in_w[...])
        self.grad_act[...] = dot(self.cot[...], out_t[...])
        self.hidden_sums[...] = jnp.zeros_like(self.hidden_sums)

        def body(part):
            pre = self.hidden[part, :] + bias
            below = 0.5 * (1.0 + lax.erf(pre * 2**-0.5))
            self.activated[part, :] = (pre * below).astype(bf16)
            slope = below + pre * (jnp.exp(-0.5 * pre * pre) * (2 * jnp.pi) ** -0.5)
            grad = (self.grad_act[part, :] * slope).astype(bf16)
            self.grad_hidden[part, :] = grad
            self.hidden_sums[...] += jnp.sum(grad.astype(f32), axis=0, keepdims=True)

        for_rows(rows, 32, body)
        self.result[...] += dot_right(self.activated[...], out_t[...])
        self.grad[...] += dot_right(self.grad_hidden[...], in_w[...])

    def third_norm_back(self):
        norm_rows_back(
            self.grad, self.second_sum, self.gain(2), self.cot, self.grad_sum, self.sums, self.low, 2, 5, 11
        )

    def cross_grad(self):
        self.grad_mixed[...] = dot_right(self.low[...], self.weight(5)).astype(bf16)

    def cross_caption(self, c, kv, grad_kv):
        wide = MODEL_WIDTH
        n_img, block_len = kv.shape[:2]
        length = n_img * block_len
        part = pl.ds(pl.multiple_of(c * SEQ, SEQ), SEQ)
        allowed = lax.broadcasted_iota(jnp.int32, (4 * SEQ, length), 1) < self.counts[c]
        mask = head_mask()
        for t in range(wide // QUAD):
            own, other = slice(t * QUAD, (t + 1) * QUAD), slice(wide + t * QUAD, wide + (t + 1) * QUAD)
            grad_query, grad_keys, grad_values = attend_back(
                self.query[part, own],
                kv[:, :, own].reshape(length, QUAD),
                kv[:, :, other].reshape(length, QUAD),
                allowed,
                mask,
                self.grad_mixed[part, own],
            )
            self.grad_query[part, own] = grad_query
            grad_kv[:, :, own] = grad_keys.reshape(n_img, block_len, QUAD)
            grad_kv[:, :, other] = grad_values.reshape(n_img, block_len, QUAD)
            self.sums[10:11, own] += jnp.sum(grad_values.astype(f32), axis=0, keepdims=True)

    def second_norm_back(self):
        self.sum_row(6, self.grad_query[...])
        self.grad[...] = dot_right(self.grad_query[...], self.weight(4))
        norm_rows_back(
            self.grad, self.first_sum, self.gain(1), self.grad_sum, self.grad_sum, self.sums, self.low, 1, 4, 8
        )

    def self_grad(self):
        self.grad_mixed[...] = dot_right(self.low[...], self.weight(3)).astype(bf16)

    def self_attention(self, start, stop):
        wide = MODEL_WIDTH
        allowed, mask = causal_mask(), head_mask()

        def caption(c, carry):
            part = pl.ds(pl.multiple_of(c * SEQ, SEQ), SEQ)
            for t in range(wide // QUAD):
                own, other = slice(t * QUAD, (t + 1) * QUAD), slice(wide + t * QUAD, wide + (t + 1) * QUAD)
                grads = attend_back(
                    self.kv[0, c, :, own],
                    self.kv[0, c, :, other],
                    self.kv[1, c, :, own],
                    allowed,
                    mask,
                    self.grad_mixed[part, own],
                )
                self.kv[2, c, :, own] = grads[0]
                self.kv[2, c, :, other] = grads[1]
                self.kv[3, c, :, own] = grads[2]
            return carry

        lax.fori_loop(start, stop, caption, 0)

    def grad_qkv(self, place, start, stop):
        rows = self.kv.shape[1] * SEQ
        return self.kv[2 + place, :, :, start:stop].reshape(rows, stop - start)

    def qkv_grads(self, pair, stage):
        wide, block = MODEL_WIDTH, 3 * MODEL_WIDTH // 4
        unit = self.normed1[...]
        if pair == 0:
            both = dot_left(unit, self.grad_qkv(0, 0, 2 * block)).astype(bf16)
            stage[0, :, 0:block] = both[:, 0:block]
            stage[1, :, 0:block] = both[:, block : 2 * block]
        else:
            keys = dot_left(unit, self.grad_qkv(0, 2 * block, 2 * wide)).astype(bf16)
            values = dot_left(unit, self.grad_qkv(1, 0, wide)).astype(bf16)
            cut = 3 * block - 2 * wide
            stage[0, :, 0 : 2 * wide - 2 * block] = keys
            stage[0, :, 2 * wide - 2 * block : block] = values[:, 0:cut]
            stage[1, :, 0:block] = values[:, cut:]

    def first_norm_back(self, weights):
        wide = MODEL_WIDTH
        parts = [self.grad_qkv(0, 0, wide), self.grad_qkv(0, wide, 2 * wide), self.grad_qkv(1, 0, wide)]
        self.sum_row(3, parts[0])
        self.sum_row(4, parts[2])
        self.grad[...] = dot_right(parts[0], weights[0][...])
        for part, weight in zip(parts[1:], weights[1:]):
            self.grad[...] += dot_right(part, weight[...])
        norm_rows_back(
            self.grad, self.tokens, self.gain(0), self.grad_sum, None, self.sums, self.low, 0, 3, None
        )


class Reducer:
    def __init__(self, here, groups, places, buffers, semaphores, credits):
        self.here, self.groups, self.places, self.n_img = here, groups, places, here.n_img
        self.acc, self.r0, self.r1, self.r2, self.zr = buffers
        (self.load_sem, self.s0, self.r0_sem, self.s1, self.r1_sem, self.s2, self.r2_sem, self.sz, self.rz) = semaphores
        self.credits = credits
        self.sends = Sends()
        self.sent = {}
        dp = here.dp
        self.chip = dp // 2
        self.chip1, self.chip2 = here.first(dp) // 2, here.second(dp) // 2
        self.chip12 = here.second(here.first(dp)) // 2

    @staticmethod
    def leads(n_img):
        return (4, n_img), (4, n_img), (2, n_img), (n_img,), (n_img + 1,)

    @staticmethod
    def semaphores(count, n_img):
        dma = pltpu.SemaphoreType.DMA
        sizes = [(4, n_img)] * 3 + [(2, n_img)] * 2 + [(n_img,)] * 3 + [(n_img + 1,)]
        return [dma((count,) + size) for size in sizes]

    def view(self, buffers, g, *index):
        own, shared, start = self.places[g]
        store = own if buffers is self.acc else shared
        return buffers[store].at[index + (pl.ds(start, self.groups[g].rows), slice(None))]

    def send(self, g, src, dst, send_sem, recv_sem, device, when=None):
        entry = self.sends.send(src, dst, send_sem, recv_sem, device, when)
        self.sent.setdefault(g, []).append(entry)
        return entry

    def settle(self, g):
        self.sends.wait(*self.sent.pop(g))

    def give(self, g, c, i, own, other):
        here = self.here
        copy = pltpu.make_async_copy(own, self.view(self.acc, g, c, i), self.load_sem.at[g, c, i])
        copy.start()
        sent = self.sends.send(
            other,
            self.view(self.r0, g, c, i),
            self.s0.at[g, c, i],
            self.r0_sem.at[g, c, i],
            (here.sib, here.im),
        )
        return copy, sent

    def given(self, pieces):
        for copy, sent in pieces:
            copy.wait()
            self.sends.wait(sent)

    def chips(self):
        return self.chip12, self.chip2, self.chip1, self.chip

    def arrived(self, buffer, semaphore):
        here = self.here
        pltpu.make_async_remote_copy(
            buffer, buffer, self.s0.at[0, 0, 0], semaphore, device_id=(here.sib, here.im), device_id_type=MESH
        ).wait_recv()

    def take(self, block, buffer, semaphore):
        self.arrived(buffer, semaphore)
        add_into(block, buffer)

    def pair(self, g, c, i):
        block = self.view(self.acc, g, c, i)
        self.take(block, self.view(self.r0, g, c, i), self.r0_sem.at[g, c, i])
        return block

    def second_send(self, g, j, c, i, when=None):
        here = self.here
        self.send(
            g,
            self.view(self.acc, g, c, i),
            self.view(self.r1, g, j, i),
            self.s1.at[g, j, i],
            self.r1_sem.at[g, j, i],
            (here.second(here.dp), here.im),
            when,
        )

    def second(self, g, images):
        for j, c in ((1, self.chip12), (0, self.chip2)):
            for i in images:
                self.pair(g, c, i)
                self.second_send(g, j, c, i)

    def second_if(self, g, c):
        far = jnp.where(self.chip12 == c, 1, 0)
        when = (self.chip12 == c) | (self.chip2 == c)
        for i in range(self.n_img):

            @pl.when(when)
            def _():
                self.pair(g, c, i)

            self.second_send(g, far, c, i, when)

    def first(self, g, images):
        here = self.here
        for i in images:
            block = self.pair(g, self.chip1, i)
            self.take(block, self.view(self.r1, g, 1, i), self.r1_sem.at[g, 1, i])
            self.send(
                g,
                block,
                self.view(self.r2, g, i),
                self.s2.at[g, i],
                self.r2_sem.at[g, i],
                (here.first(here.dp), here.im),
            )

    def plane(self, g, images):
        for i in images:
            block = self.pair(g, self.chip, i)
            self.take(block, self.view(self.r1, g, 0, i), self.r1_sem.at[g, 0, i])
            self.take(block, self.view(self.r2, g, i), self.r2_sem.at[g, i])

    def line(self, g, k):
        here, im, n_img = self.here, self.here.im, self.n_img
        i = here.near(k)
        block = self.view(self.acc, g, self.chip, i)
        down = jnp.where(i < im, 1, 0)

        @pl.when((im > 0) & (im < n_img - 1))
        def _():
            self.take(block, self.view(self.zr, g, i), self.rz.at[g, i])

        target = im + 1 - 2 * down
        slot = jnp.where((down == 1) & (i == target), n_img, i)
        self.send(
            g, block, self.view(self.zr, g, slot), self.sz.at[g, i], self.rz.at[g, slot], (here.dp, target)
        )

    def last(self, g, out):
        im, n_img = self.here.im, self.n_img
        out[...] = self.view(self.acc, g, self.chip, im)[...].astype(f32)
        for slot, has in ((im, im > 0), (n_img, im < n_img - 1)):

            @pl.when(has)
            def _():
                buffer = self.view(self.zr, g, slot)
                self.arrived(buffer, self.rz.at[g, slot])
                out[...] += buffer[...].astype(f32)

    def neighbours(self):
        here = self.here
        im = here.im
        return ((here.dp, im - 1), im > 0, 3), ((here.dp, im + 1), im < self.n_img - 1, 4)

    def free_partner(self, n):
        here = self.here
        partner = (here.sib, here.second(here.dp), here.first(here.dp))[n]
        pl.semaphore_signal(self.credits.at[n], inc=1, device_id=(partner, here.im), device_id_type=MESH)

    def await_partner(self, n):
        pl.semaphore_wait(self.credits.at[n], 1)

    def free_line(self):
        for device, has, n in self.neighbours():
            mine = 7 - n

            @pl.when(has)
            def _():
                pl.semaphore_signal(self.credits.at[mine], inc=1, device_id=device, device_id_type=MESH)

    def await_line(self):
        for device, has, n in self.neighbours():

            @pl.when(has)
            def _():
                pl.semaphore_wait(self.credits.at[n], 1)


def bag(shapes, refs):
    return SimpleNamespace(**dict(zip(shapes, refs)))


def structs_of(shapes):
    return [jax.ShapeDtypeStruct(*shape) for shape in shapes.values()]


def back_inputs(dims):
    n_dp, n_img, caps, depth, width, inner_dp, block_len = dims
    wide, rows, inner = MODEL_WIDTH, caps * SEQ, n_dp * inner_dp
    low, high = ((rows, wide), bf16), ((rows, wide), f32)
    return dict(
        vec=((16, wide), f32),
        bias=((n_img, inner // n_img), f32),
        second_sum=high,
        cot=low,
        mixed=low,
        query=low,
        kv=((n_img, caps, block_len, 2 * wide), bf16),
        images=((n_img, caps, block_len, wide), bf16),
        normed2=low,
        in_w=((wide, inner), bf16),
        out_t=((wide, inner), bf16),
        weights=((wide, 6 * wide), bf16),
        ckv=((wide, 2 * wide), bf16),
        first_sum=high,
        qkv=((caps, SEQ, 3 * wide), bf16),
        self_mixed=low,
        normed1=low,
        tokens=low,
    )


def back_outputs(dims):
    n_dp, n_img, caps, depth, width, inner_dp, block_len = dims
    wide, rows, inner = MODEL_WIDTH, caps * SEQ, n_dp * inner_dp
    return dict(
        layer_out=((rows, wide), bf16),
        token_grads=((rows, wide), bf16),
        image_out=((n_img, caps, block_len, wide), bf16),
        s_out=((width, inner_dp), f32),
        s_in=((depth, inner // n_img), f32),
        s_cross=((depth, 2 * width), f32),
        s_ckv=((depth, 2 * width), f32),
        s_self=((depth, 4 * width), f32),
        s_vec=((VEC_ROWS, LANES), f32),
    )


def back_scratch(dims):
    n_dp, n_img, caps, depth, width, inner_dp, block_len = dims
    wide, rows, inner = MODEL_WIDTH, caps * SEQ, n_dp * inner_dp
    tile = inner // n_img
    low, high = ((rows, wide), bf16), ((rows, wide), f32)
    return dict(
        vec=((16, wide), f32),
        bias=((n_img, tile), f32),
        sums=((16, wide), f32),
        bias_sums=((n_img, tile), f32),
        hidden_sums=((1, tile), f32),
        vectors=((n_dp * VEC_ROWS, LANES), f32),
        cot=low,
        second_sum=high,
        normed3=low,
        turned=((2 * wide, rows), bf16),
        result=high,
        grad=high,
        hidden=((rows, tile), f32),
        grad_act=((rows, tile), f32),
        activated=((rows, tile), bf16),
        grad_hidden=((rows, tile), bf16),
        in_tile=((2, wide, tile), bf16),
        out_tile=((2, wide, tile), bf16),
        stage_in=((wide, tile), bf16),
        stage_out=((wide, tile), bf16),
        low=low,
        mixed=low,
        query=low,
        normed2=low,
        kv=((n_img, caps, block_len, 2 * wide), bf16),
        images=((n_img, caps, block_len, wide), bf16),
        images_out=((n_img, caps, block_len, wide), bf16),
        stage_cross=((n_img, wide, 2 * width), bf16),
        stage_self=((2, wide, 4 * width), bf16),
    )


OUT, IN, CROSS, CKV, SELF, VEC = range(6)
PLACES = ((0, 0, 0), (1, 1, 0), (2, 0, 0), (2, 0, 1), (1, 1, 0), (3, 2, 0))


def back_groups(dims):
    n_dp, n_img, caps, depth, width, inner_dp, block_len = dims
    wide, inner = MODEL_WIDTH, n_dp * inner_dp
    return [
        Group(width, inner_dp, bf16, (wide, inner), turned_block),
        Group(depth, inner // n_img, bf16, (wide, inner), grid_block),
        Group(depth, 2 * width, bf16, (n_img, wide, 2 * width), stacked_block),
        Group(depth, 2 * width, bf16, (wide, 2 * wide), grid_block),
        Group(depth, 4 * width, bf16, (n_img, wide, 4 * width), stacked_block),
        Group(VEC_ROWS, LANES, f32, (n_dp * VEC_ROWS, LANES), repeated_block),
    ]


def back_buffers(dims):
    groups = back_groups(dims)
    out, inside, vec = [(g.rows, g.cols, g.dtype) for g in (groups[OUT], groups[IN], groups[VEC])]
    stores = [[out, inside, out, vec]] + [[out, inside, vec]] * 4
    return [
        [pltpu.VMEM(lead + store[:2], store[2]) for store in these]
        for lead, these in zip(Reducer.leads(dims[1]), stores)
    ]


def back_kernel(dims, *refs):
    n_dp, n_img, caps, depth, width, inner_dp, block_len = dims
    wide, rows, inner = MODEL_WIDTH, caps * SEQ, n_dp * inner_dp
    tile = inner // n_img
    inputs, outputs, scratch = back_inputs(dims), back_outputs(dims), back_scratch(dims)
    counts, refs = refs[0], refs[1:]
    hbm, refs = bag(inputs, refs), refs[len(inputs) :]
    outs, refs = bag(outputs, refs), refs[len(outputs) :]
    s, refs = bag(scratch, refs), refs[len(scratch) :]
    groups = back_groups(dims)
    buffers = []
    for these in back_buffers(dims):
        buffers.append(refs[: len(these)])
        refs = refs[len(these) :]
    places = [(own, shared, start * depth) for own, shared, start in PLACES]
    here = Place(n_img)
    dp, im, core = here.dp, here.im, here.core
    red = Reducer(here, groups, places, buffers, refs[:9], refs[9])
    copies = Copies(refs[10])
    dx_send, dx_recv = refs[11:]
    every = range(n_img)
    names = list(inputs)

    def load(*wanted):
        return [copies.start(getattr(hbm, name), getattr(s, name)) for name in wanted]

    first_loads = load(*names[:4])

    def load_tile(t):
        cols = pl.ds(t * tile, tile)
        return [
            copies.start(hbm.in_w.at[:, cols], s.in_tile.at[t % 2]),
            copies.start(hbm.out_t.at[:, cols], s.out_tile.at[t % 2]),
        ]

    def load_square(n, dst):
        return copies.start(hbm.weights.at[:, pl.ds(n * wide, wide)], dst)

    tiles = [load_tile(0), load_tile(1)]
    middle_loads = load(*names[4:9])
    here.barrier()
    copies.wait(*first_loads)
    s.sums[...] = jnp.zeros_like(s.sums)
    step = Backward(dims, counts, s)
    step.begin()
    given = []
    own, other = tile_ds(core, inner_dp, LANES), tile_ds(1 - core, inner_dp, LANES)
    for t in every:
        copies.wait(*tiles[t])
        step.feed_forward(s.bias[t : t + 1, :], s.in_tile.at[t % 2], s.out_tile.at[t % 2])
        s.bias_sums[t : t + 1, :] = s.hidden_sums[...]
        if t + 2 < n_img:
            tiles.append(load_tile(t + 2))
        red.given(given)
        s.stage_in[...] = dot(s.turned[0:wide, :], s.grad_hidden[...]).astype(bf16)
        given = [
            red.give(
                IN,
                c,
                t,
                s.stage_in.at[tile_ds(2 * c + core, depth, 16), :],
                s.stage_in.at[tile_ds(2 * c + 1 - core, depth, 16), :],
            )
            for c in red.chips()
        ]
        s.stage_out[...] = dot(s.turned[wide : 2 * wide, :], s.activated[...]).astype(bf16)
        for i in every:
            part = pl.ds(i * width, width)
            given.append(red.give(OUT, t, i, s.stage_out.at[part, own], s.stage_out.at[part, other]))
        if t >= 1:
            red.second(IN, [t - 1])
            red.second_if(OUT, t - 1)
        if t >= 2:
            red.first(IN, [t - 2])
    red.given(given)
    cross_loads = [load_square(4 + n, s.in_tile.at[n]) for n in range(2)]
    cross_loads += [copies.start(hbm.ckv.at[:, pl.ds(n * wide, wide)], s.out_tile.at[n]) for n in range(2)]
    first_sum = copies.start(hbm.first_sum, s.grad_act)
    red.second(IN, [n_img - 1])
    red.second_if(OUT, n_img - 1)

    def body(part):
        s.activated[part, :] = s.result[part, :].astype(bf16)

    for_rows(rows, 64, body)
    layer_out = copies.start(s.activated, outs.layer_out)
    s.grad_sum, s.grad_query, s.first_sum = s.hidden, s.grad_hidden, s.grad_act
    step.third_norm_back()
    copies.wait(layer_out, *cross_loads)
    s.grad_mixed, s.weights = s.activated, (None,) * 4 + (s.in_tile.at[0], s.in_tile.at[1])
    step.cross_grad()
    sout_load = load_square(3, s.in_tile.at[1])
    copies.wait(*middle_loads)

    pending = []

    def pace(count=1):
        for _ in range(count):
            if pending:
                k, p = pending.pop(0)
                target = (im + k) % n_img
                part = pl.ds(2 * p, 2)
                red.sends.send(
                    s.images_out.at[target, part],
                    outs.image_out.at[im, part],
                    dx_send.at[k, p],
                    dx_recv.at[k, p],
                    (dp, target),
                )

    def caption(c, carry):
        step.cross_caption(c, s.kv.at[:, c], s.kv.at[:, c])
        return carry

    def images_back(p):
        part = slice(2 * p, 2 * p + 2)
        length = n_img * 2 * block_len
        value = dot_right(s.kv[:, part, :, 0:wide].reshape(length, wide), s.out_tile[0])
        value = value + dot_right(s.kv[:, part, :, wide : 2 * wide].reshape(length, wide), s.out_tile[1])
        s.images_out[:, part] = value.astype(bf16).reshape(n_img, 2, block_len, wide)
        pending.extend([(k, p) for k in (2, 1, 3)])

    for p in range(caps // 2):
        lax.fori_loop(2 * p, 2 * p + 2, caption, 0)
        images_back(p)
        pace()
        if p == 0:
            red.first(IN, [n_img - 2, n_img - 1])
        if p == 1:
            red.plane(IN, every)
            red.first(OUT, every)
            pace()
        if p == 2:
            red.line(IN, n_img - 1)
            red.plane(OUT, every)
            for n in range(3):
                red.free_partner(n)
            red.line(OUT, n_img - 1)
            pace()
        if p == 3:
            red.line(IN, n_img - 2)
            red.line(OUT, n_img - 2)
    copies.start(s.images_out.at[im], outs.image_out.at[im])
    tokens = copies.start(hbm.tokens, s.query)

    def square_grad(values, grads, store):
        for m in range(wide // 256):
            cols = slice(m * 256, (m + 1) * 256)
            s.stage_in[:, cols] = dot_left(values[...], grads[:, cols]).astype(bf16)
        for i in every:
            store(i, s.stage_in[:, i * width : (i + 1) * width])

    def to_cross(n):
        def store(i, value):
            s.stage_cross[i, :, n * width : (n + 1) * width] = value

        return store

    square_grad(s.mixed, s.low, to_cross(0))
    self_mixed = copies.start(hbm.self_mixed, s.mixed)
    pace()
    flat = n_img * caps * block_len
    for n in range(2 * wide // 256):
        at, col = divmod(n * 256, wide)
        part = s.kv[:, :, :, n * 256 : (n + 1) * 256].reshape(flat, 256)
        s.out_tile[at, :, col : col + 256] = dot_left(s.images[...].reshape(flat, wide), part).astype(bf16)
    for k in range(1, n_img - 2):
        red.line(IN, k)
        red.line(OUT, k)
    pace()
    qkv_loads = [
        copies.start(hbm.qkv.at[:, :, pl.ds(0, 2 * wide)], s.kv.at[0]),
        copies.start(hbm.qkv.at[:, :, pl.ds(2 * wide, wide)], s.kv.at[1, :, :, pl.ds(0, wide)]),
    ]
    red.await_partner(0)
    ckv_given = []
    for c in red.chips():
        for i in every:
            at, col = divmod(i * 2 * width, wide)
            half = s.out_tile.at[at, :, pl.ds(col, 2 * width)]
            ckv_given.append(
                red.give(
                    CKV,
                    c,
                    i,
                    half.at[tile_ds(2 * c + core, depth, 16), :],
                    half.at[tile_ds(2 * c + 1 - core, depth, 16), :],
                )
            )
    copies.wait(first_sum)
    step.second_norm_back()
    square_grad(s.normed2, s.grad_query, to_cross(1))
    normed1 = copies.start(hbm.normed1, s.normed2)
    cross_given = []
    for c in red.chips():
        for i in every:
            block = groups[CROSS].block
            cross_given.append(
                red.give(
                    CROSS,
                    c,
                    i,
                    block(s.stage_cross, 2 * c + core, i),
                    block(s.stage_cross, 2 * c + 1 - core, i),
                )
            )
    pace()
    copies.wait(sout_load)
    s.weights = (None,) * 3 + (s.in_tile.at[1],)
    step.self_grad()
    red.given(ckv_given)
    weight_loads = [load_square(0, s.out_tile.at[0]), load_square(1, s.out_tile.at[1]), load_square(2, s.in_tile.at[0])]
    red.await_partner(1)
    red.second(CKV, every)
    red.last(IN, outs.s_in)
    red.last(OUT, outs.s_out)
    red.free_line()
    red.given(cross_given)
    red.second(CROSS, every)
    copies.wait(*qkv_loads)
    step.self_attention(0, caps // 2)
    pace()
    red.await_partner(2)
    red.first(CKV, every)
    step.self_attention(caps // 2, caps)
    pace()
    red.first(CROSS, every)
    red.settle(IN)
    copies.wait(self_mixed, normed1, tokens)
    s.self_mixed, s.normed1, s.tokens = s.mixed, s.normed2, s.query
    for m in range(wide // 256):
        cols = slice(m * 256, (m + 1) * 256)
        s.stage_in[:, cols] = dot_left(s.self_mixed[...], s.low[:, cols]).astype(bf16)
    given = []
    for pair in range(2):
        red.given(given)
        step.qkv_grads(pair, s.stage_self)
        for n in range(2):
            i = 2 * pair + n
            s.stage_self[n, :, 3 * width :] = s.stage_in[:, i * width : (i + 1) * width]
        given = [
            red.give(
                SELF,
                c,
                2 * pair + n,
                s.stage_self.at[n, tile_ds(2 * c + core, depth, 16), :],
                s.stage_self.at[n, tile_ds(2 * c + 1 - core, depth, 16), :],
            )
            for n in range(2)
            for c in red.chips()
        ]
        if pair == 1:
            red.second(SELF, (0, 1))
    pace()
    red.plane(CKV, every)
    red.given(given)
    red.second(SELF, (2, 3))
    copies.wait(*weight_loads)
    step.first_norm_back((s.out_tile.at[0], s.out_tile.at[1], s.in_tile.at[0]))
    copies.start(s.low, outs.token_grads)
    pack_vectors(s.sums, s.bias_sums, s.vectors, n_dp, depth, inner_dp)
    vec_given = []
    for c in red.chips():
        for i in every:
            block = groups[VEC].block
            vec_given.append(
                red.give(VEC, c, i, block(s.vectors, 2 * c + core, i), block(s.vectors, 2 * c + 1 - core, i))
            )
    pace(len(pending))
    red.await_line()
    red.line(CKV, n_img - 1)
    red.plane(CROSS, every)
    red.given(vec_given)
    red.second(VEC, every)
    red.line(CROSS, n_img - 1)
    red.line(CKV, n_img - 2)
    red.first(SELF, every)
    red.line(CROSS, n_img - 2)
    red.first(VEC, every)
    for k in range(1, n_img - 2):
        red.line(CKV, k)
        red.line(CROSS, k)
    red.plane(SELF, every)
    red.plane(VEC, every)
    for k in reversed(range(1, n_img)):
        red.line(SELF, k)
        red.line(VEC, k)
    red.last(CKV, outs.s_ckv)
    red.last(CROSS, outs.s_cross)
    red.last(SELF, outs.s_self)
    red.last(VEC, outs.s_vec)
    for p in range(caps // 2):
        for k in range(1, n_img):
            source = (im + n_img - k) % n_img
            block = outs.image_out.at[source, pl.ds(2 * p, 2)]
            pltpu.make_async_remote_copy(
                block, block, dx_send.at[k, p], dx_recv.at[k, p], device_id=(dp, source), device_id_type=MESH
            ).wait_recv()
    red.sends.finish()
    copies.finish()


def back_pass(dims, counts, values):
    inputs, outputs, scratch = back_inputs(dims), back_outputs(dims), back_scratch(dims)
    n_img, caps = dims[1], dims[2]
    dma = pltpu.SemaphoreType.DMA
    any_spec, vmem_spec = pl.BlockSpec(memory_space=pl.ANY), pl.BlockSpec(memory_space=pltpu.VMEM)
    outs = pl.pallas_call(
        functools.partial(back_kernel, dims),
        out_shape=structs_of(outputs),
        in_specs=[pl.BlockSpec(memory_space=pltpu.SMEM)] + [any_spec] * len(inputs),
        out_specs=[any_spec] * 3 + [vmem_spec] * (len(outputs) - 3),
        scratch_shapes=[pltpu.VMEM(*shape) for shape in scratch.values()]
        + [buffer for these in back_buffers(dims) for buffer in these]
        + Reducer.semaphores(len(back_groups(dims)), n_img)
        + [
            pltpu.SemaphoreType.REGULAR((5,)),
            dma((48,)),
            dma((n_img, caps // 2)),
            dma((n_img, caps // 2)),
        ],
        compiler_params=pltpu.CompilerParams(
            collective_id=2, has_side_effects=True, vmem_limit_bytes=63 << 20
        ),
    )(counts, *[values[name] for name in inputs])
    return dict(zip(outputs, outs))


def layer_norm(values, norm_gain, norm_shift):
    average = jnp.mean(values, axis=-1, keepdims=True)
    centred = values - average
    spread = jnp.mean(centred * centred, axis=-1, keepdims=True)
    return centred * lax.rsqrt(spread + norm_epsilon) * norm_gain + norm_shift


def matmul(left_op, right_op):
    return jnp.dot(left_op, right_op, preferred_element_type=f32)


def matmul_tleft(left_op, right_op):
    return lax.dot_general(
        left_op, right_op, (((0,), (0,)), ((), ())), preferred_element_type=f32
    )


def matmul_tright(left_op, right_op):
    return lax.dot_general(
        left_op, right_op, (((1,), (1,)), ((), ())), preferred_element_type=f32
    )


def column_sums(values):
    return jnp.sum(values.astype(f32), axis=0)


def to_heads(values, captions):
    return values.reshape(captions, -1, HEADS, HEAD)


def probabilities(queries, key_heads, allowed):
    scores = jnp.einsum("cqhd,ckhd->chqk", queries, key_heads, preferred_element_type=f32)
    scores = jnp.where(allowed, scores * HEAD ** (-0.5), masked_value)
    return jax.nn.softmax(scores, axis=-1)


def attention(queries, key_heads, value_heads, allowed):
    probs = probabilities(queries, key_heads, allowed).astype(bf16)
    return jnp.einsum("chqk,ckhd->cqhd", probs, value_heads, preferred_element_type=f32)


def attention_backward(queries, key_heads, value_heads, allowed, grad_mixed):
    probs = probabilities(queries, key_heads, allowed)
    grad_probs = jnp.einsum("cqhd,ckhd->chqk", grad_mixed, value_heads, preferred_element_type=f32)
    inner_term = jnp.sum(probs * grad_probs, axis=-1, keepdims=True)
    grad_scores = (probs * (grad_probs - inner_term)).astype(bf16)
    score_scale = HEAD ** (-0.5)
    grad_queries = (
        jnp.einsum("chqk,ckhd->cqhd", grad_scores, key_heads, preferred_element_type=f32)
        * score_scale
    )
    grad_keys = (
        jnp.einsum("chqk,cqhd->ckhd", grad_scores, queries, preferred_element_type=f32)
        * score_scale
    )
    grad_values = jnp.einsum(
        "chqk,cqhd->ckhd", probs.astype(bf16), grad_mixed, preferred_element_type=f32
    )
    return grad_queries.astype(bf16), grad_keys.astype(bf16), grad_values.astype(bf16)


def local_direct(
    n_dp,
    n_img,
    tokens,
    image_tokens,
    counts,
    mixed,
    cross_kv,
    mlp_in,
    mlp_out,
    norm_gains,
    shifts,
    mlp_bias,
    cotangent,
):
    captions = tokens.shape[0]
    depth = mixed.shape[0]
    width = mlp_out.shape[1]
    inner_dp = mlp_out.shape[0]
    rows_all = captions * SEQ
    dims = (n_dp, n_img, captions, depth, width, inner_dp, image_tokens.shape[1])
    narrow = jnp.pad(jnp.concatenate([norm_gains, shifts]), ((0, 0), (0, LANES - depth)))
    vectors = jnp.concatenate([narrow, mlp_bias.reshape(-1, LANES)])
    token_rows = tokens.reshape(rows_all, MODEL_WIDTH)
    values = entry_pass(
        dims, counts, (vectors, cross_kv, mixed, mlp_in, mlp_out.T), image_tokens, token_rows
    )
    values.update(cot=cotangent.reshape(rows_all, MODEL_WIDTH), tokens=token_rows)
    values.update(qkv=values.pop("qkv").reshape(captions, SEQ, 3 * MODEL_WIDTH))
    get = SimpleNamespace(**back_pass(dims, counts, values))
    image_out = get.image_out.reshape(image_tokens.shape)
    return (
        get.layer_out.reshape(tokens.shape),
        get.token_grads.reshape(tokens.shape),
        image_out,
        get.s_self[:, : 3 * width],
        get.s_self[:, 3 * width :],
        get.s_cross[:, width:],
        get.s_ckv,
        get.s_cross[:, :width],
        get.s_in,
        get.s_out.T,
        get.s_vec[:3, :depth],
        get.s_vec[3:13, :depth],
        get.s_vec[13:].reshape(-1),
    )


def local(
    n_dp,
    n_img,
    tokens,
    image_tokens,
    token_counts,
    self_qkv,
    self_out,
    cross_q,
    cross_kv,
    cross_out,
    mlp_in,
    mlp_out,
    norm_gains,
    shifts,
    mlp_bias,
    cotangent,
):
    captions = tokens.shape[0]
    rows_all = captions * SEQ
    block_len = image_tokens.shape[1]
    width = self_out.shape[1]
    depth = self_out.shape[0]
    inner_dp = mlp_out.shape[0]
    direct = n_dp == 8 and depth % 16 == 0 and captions * n_img == image_tokens.shape[0]
    counts = lax.dynamic_slice_in_dim(token_counts, lax.axis_index("img") * captions, captions)

    mixed = jnp.concatenate([self_qkv, self_out, cross_q, cross_out], axis=1)
    if direct:
        return local_direct(
            n_dp,
            n_img,
            tokens,
            image_tokens,
            counts,
            mixed,
            cross_kv,
            mlp_in,
            mlp_out,
            norm_gains,
            shifts,
            mlp_bias,
            cotangent,
        )
    vectors = jnp.concatenate([norm_gains.reshape(-1), shifts.reshape(-1), mlp_bias])

    def everything(block, first, then, axes):
        return lax.all_gather(
            lax.all_gather(block, first, axis=axes[0], tiled=True), then, axis=axes[1], tiled=True
        )

    mixed_full = lax.all_gather(
        lax.all_gather(mixed, "dp", axis=0, tiled=True), "img", axis=0, tiled=False
    )
    ckv_w = everything(cross_kv, "img", "dp", (1, 0))
    in_w = everything(mlp_in, "img", "dp", (1, 0))
    outm_t = everything(mlp_out, "img", "dp", (1, 0)).T
    vec_full = lax.all_gather(vectors, "dp", axis=0, tiled=False)
    image_own = lax.all_to_all(
        image_tokens.reshape((n_img, captions) + image_tokens.shape[1:]), "img", 0, 0, tiled=True
    )

    def columns(start, size):
        return (
            mixed_full[:, :, start * width : (start + size) * width]
            .transpose(1, 0, 2)
            .reshape(MODEL_WIDTH, size * MODEL_WIDTH)
        )

    qkv_w, sout_w, cq_w, cout_w = columns(0, 3), columns(3, 1), columns(4, 1), columns(5, 1)
    gain_rows = vec_full[:, : 3 * depth].reshape(n_dp, 3, depth).transpose(1, 0, 2).reshape(3, -1)
    shift_rows = (
        vec_full[:, 3 * depth : 13 * depth]
        .reshape(n_dp, 10, depth)
        .transpose(1, 0, 2)
        .reshape(10, -1)
    )
    inner_bias = vec_full[:, 13 * depth :].reshape(-1)

    zero_row = jnp.zeros((MODEL_WIDTH,), f32)
    rows = tokens.reshape(rows_all, MODEL_WIDTH).astype(f32)
    normed1 = layer_norm(rows, gain_rows[0], shift_rows[0]).astype(bf16)
    mixed_qkv = (
        matmul(normed1, qkv_w) + jnp.concatenate([shift_rows[3], zero_row, shift_rows[4]])
    ).astype(bf16)
    self_queries, self_keys, self_values = [
        to_heads(mixed_qkv[:, n * MODEL_WIDTH : (n + 1) * MODEL_WIDTH], captions) for n in range(3)
    ]
    places = jnp.arange(SEQ, dtype=jnp.int32)
    causal = (places[None, :] <= places[:, None])[None, None]
    self_mixed = attention(self_queries, self_keys, self_values, causal)
    self_mixed = self_mixed.reshape(rows_all, MODEL_WIDTH).astype(bf16)
    first_sum = rows + matmul(self_mixed, sout_w) + shift_rows[5]
    normed2 = layer_norm(first_sum, gain_rows[1], shift_rows[1]).astype(bf16)
    cross_query = (matmul(normed2, cq_w) + shift_rows[6]).astype(bf16)
    cross_queries = to_heads(cross_query, captions)

    image_len = n_img * block_len
    image_rows = image_own.reshape(n_img * captions * block_len, MODEL_WIDTH)
    image_kv = (matmul(image_rows, ckv_w) + jnp.concatenate([zero_row, shift_rows[7]])).astype(bf16)

    def by_caption(values):
        return (
            values.reshape(n_img, captions, block_len, HEADS, HEAD)
            .transpose(1, 0, 2, 3, 4)
            .reshape(captions, image_len, HEADS, HEAD)
        )

    def by_place(values):
        return (
            values.reshape(captions, n_img, block_len, MODEL_WIDTH)
            .transpose(1, 0, 2, 3)
            .reshape(-1, MODEL_WIDTH)
        )

    cross_keys = by_caption(image_kv[:, :MODEL_WIDTH])
    cross_values = by_caption(image_kv[:, MODEL_WIDTH:])
    valid = (jnp.arange(image_len, dtype=jnp.int32)[None, :] < counts[:, None])[:, None, None, :]
    cross_mixed = attention(cross_queries, cross_keys, cross_values, valid)
    cross_mixed = cross_mixed.reshape(rows_all, MODEL_WIDTH).astype(bf16)
    second_sum = first_sum + matmul(cross_mixed, cout_w) + shift_rows[8]
    normed3 = layer_norm(second_sum, gain_rows[2], shift_rows[2]).astype(bf16)
    hidden = matmul(normed3, in_w) + inner_bias
    activated = jax.nn.gelu(hidden, approximate=False).astype(bf16)
    result = second_sum + matmul_tright(activated, outm_t) + shift_rows[9]
    layer_out = result.reshape(tokens.shape).astype(bf16)

    grad_low3 = cotangent.reshape(rows_all, MODEL_WIDTH)
    g_outm_t = matmul_tleft(grad_low3, activated)
    g_shift9 = column_sums(grad_low3)
    grad_act = matmul(grad_low3, outm_t)
    _, gelu_pull = jax.vjp(lambda pre_act: jax.nn.gelu(pre_act, approximate=False), hidden)
    grad_hidden = gelu_pull(grad_act)[0].astype(bf16)
    g_in = matmul_tleft(normed3, grad_hidden)
    g_inner_bias = column_sums(grad_hidden)
    grad_normed3 = matmul_tright(grad_hidden, in_w)
    _, norm_pull3 = jax.vjp(layer_norm, second_sum, gain_rows[2], shift_rows[2])
    grad_second_ln, g_gain2, g_shift2 = norm_pull3(grad_normed3)
    grad_second = grad_low3.astype(f32) + grad_second_ln
    grad_low2 = grad_second.astype(bf16)
    g_cout = matmul_tleft(cross_mixed, grad_low2)
    g_shift8 = column_sums(grad_low2)
    grad_cross_mixed = to_heads(matmul_tright(grad_low2, cout_w).astype(bf16), captions)
    grad_query, grad_ckeys, grad_cvalues = attention_backward(
        cross_queries, cross_keys, cross_values, valid, grad_cross_mixed
    )
    grad_query = grad_query.reshape(rows_all, MODEL_WIDTH)
    g_cq = matmul_tleft(normed2, grad_query)
    g_shift6 = column_sums(grad_query)
    grad_normed2 = matmul_tright(grad_query, cq_w)
    grad_value_rows = by_place(grad_cvalues)
    grad_image_kv = jnp.concatenate([by_place(grad_ckeys), grad_value_rows], axis=1)
    g_ckv = matmul_tleft(image_rows, grad_image_kv)
    g_shift7 = column_sums(grad_value_rows)
    image_grads = matmul_tright(grad_image_kv, ckv_w).astype(bf16).reshape(image_own.shape)
    _, norm_pull2 = jax.vjp(layer_norm, first_sum, gain_rows[1], shift_rows[1])
    grad_first_ln, g_gain1, g_shift1 = norm_pull2(grad_normed2)
    grad_first = grad_second + grad_first_ln
    grad_low1 = grad_first.astype(bf16)
    g_sout = matmul_tleft(self_mixed, grad_low1)
    g_shift5 = column_sums(grad_low1)
    grad_self_mixed = to_heads(matmul_tright(grad_low1, sout_w).astype(bf16), captions)
    grad_qkv = jnp.concatenate(
        [
            part.reshape(rows_all, MODEL_WIDTH)
            for part in attention_backward(
                self_queries, self_keys, self_values, causal, grad_self_mixed
            )
        ],
        axis=1,
    )
    g_qkv = matmul_tleft(normed1, grad_qkv)
    qkv_sums = column_sums(grad_qkv)
    g_shift3, g_shift4 = qkv_sums[:MODEL_WIDTH], qkv_sums[2 * MODEL_WIDTH :]
    grad_normed1 = matmul_tright(grad_qkv, qkv_w)
    _, norm_pull1 = jax.vjp(layer_norm, rows, gain_rows[0], shift_rows[0])
    grad_rows_ln, g_gain0, g_shift0 = norm_pull1(grad_normed1)
    token_grads = (grad_first + grad_rows_ln).reshape(tokens.shape).astype(bf16)
    g_vector_rows = jnp.stack(
        [
            g_gain0,
            g_gain1,
            g_gain2,
            g_shift0,
            g_shift1,
            g_shift2,
            g_shift3,
            g_shift4,
            g_shift5,
            g_shift6,
            g_shift7,
            g_shift8,
            g_shift9,
        ]
    )

    def scattered(grad):
        tall = lax.psum_scatter(grad, "dp", scatter_dimension=0, tiled=True)
        return lax.psum_scatter(tall, "img", scatter_dimension=1, tiled=True)

    s_qkv, s_sout, s_cq, s_ckv, s_cout, s_in, s_outm = [
        scattered(g) for g in (g_qkv, g_sout, g_cq, g_ckv, g_cout, g_in, g_outm_t.T)
    ]
    s_rows, s_inner = lax.psum(
        (
            lax.psum_scatter(g_vector_rows, "dp", scatter_dimension=1, tiled=True),
            lax.psum_scatter(g_inner_bias, "dp", scatter_dimension=0, tiled=True),
        ),
        "img",
    )
    image_out = lax.all_to_all(image_grads, "img", 0, 0, tiled=True).reshape(image_tokens.shape)
    return (
        layer_out,
        token_grads,
        image_out,
        s_qkv,
        s_sout,
        s_cq,
        s_ckv,
        s_cout,
        s_in,
        s_outm,
        s_rows[:3],
        s_rows[3:],
        s_inner,
    )


def solution(mesh):
    caption_rows = P(("dp", "img"), None, None)
    weight = P("dp", "img")
    vector = P(None, "dp")
    in_specs = (caption_rows, P("dp", "img", None), P("dp")) + (weight,) * 7
    in_specs += (vector, vector, P("dp"), caption_rows)
    out_specs = (caption_rows, caption_rows, P("dp", "img", None)) + (weight,) * 7
    out_specs += (vector, vector, P("dp"))
    return jax.shard_map(
        functools.partial(local, mesh.shape["dp"], mesh.shape["img"]),
        mesh=mesh,
        in_specs=in_specs,
        out_specs=out_specs,
        check_vma=False,
    )
```

```python
import functools
from types import SimpleNamespace

import jax
import jax.numpy as jnp
from jax import lax
from jax.experimental import pallas as pl
from jax.experimental.pallas import tpu as pltpu
from jax.sharding import PartitionSpec as P

MODEL_WIDTH = 768
HEADS = 12
HEAD = 64
SEQ = 64
VEC_ROWS = 16
LANES = 128
MESH = pl.DeviceIdType.MESH
bf16 = jnp.bfloat16
f32 = jnp.float32

masked_value = -1e30
norm_epsilon = 1e-05


def tile_ds(index, size, unit):
    return pl.ds(pl.multiple_of(index * size, unit), size)


def stacked_block(rows, cols):
    return lambda ref, d, i: ref.at[i, tile_ds(d, rows, 16), :]


def grid_block(rows, cols):
    return lambda ref, d, i: ref.at[tile_ds(d, rows, 16), tile_ds(i, cols, LANES)]


def turned_block(rows, cols):
    return lambda ref, d, i: ref.at[tile_ds(i, rows, 16), tile_ds(d, cols, LANES)]


def repeated_block(rows, cols):
    return lambda ref, d, i: ref.at[tile_ds(d, rows, 8), :]


class Group:
    def __init__(self, rows, cols, dtype, full, block):
        self.rows, self.cols, self.dtype, self.full = rows, cols, dtype, full
        self.block = block(rows, cols)


def flip(d, bit):
    return d + bit * (1 - 2 * ((d // bit) % 2))


class Place:
    def __init__(self, n_img):
        self.n_img = n_img
        self.dp, self.im = lax.axis_index("dp"), lax.axis_index("img")
        self.core = self.dp % 2
        self.sib = flip(self.dp, 1)

    def first(self, d):
        return flip(d, 2) * (1 - self.core) + flip(d, 4) * self.core

    def second(self, d):
        return flip(d, 4) * (1 - self.core) + flip(d, 2) * self.core

    def near(self, k):
        value = jnp.int32(0)
        for at in range(self.n_img):
            order = sorted(range(self.n_img), key=lambda other: (abs(other - at), other))
            value = jnp.where(self.im == at, order[k], value)
        return value

    def barrier(self):
        semaphore = pltpu.get_barrier_semaphore()
        peers = [(self.sib, self.im), (self.first(self.dp), self.im), (self.second(self.dp), self.im)]
        peers += [(self.dp, (self.im + k) % self.n_img) for k in range(1, self.n_img)]
        for peer in peers:
            pl.semaphore_signal(semaphore, inc=1, device_id=peer, device_id_type=MESH)
        pl.semaphore_wait(semaphore, len(peers))


class Sends:
    def __init__(self):
        self.started = []

    def send(self, src, dst, send_sem, recv_sem, device, when=None):
        copy = pltpu.make_async_remote_copy(
            src, dst, send_sem, recv_sem, device_id=device, device_id_type=MESH
        )
        entry = (when, copy)
        self.started.append(entry)
        if when is None:
            copy.start()
        else:
            pl.when(when)(copy.start)
        return entry

    def send_copy(self, copy):
        self.started.append((None, copy))
        copy.start()

    def wait(self, *entries):
        for entry in entries:
            self.started = [other for other in self.started if other is not entry]
            when, copy = entry
            if when is None:
                copy.wait_send()
            else:
                pl.when(when)(copy.wait_send)

    def finish(self):
        self.wait(*self.started)


def dot(left, right):
    return jnp.dot(left, right, preferred_element_type=f32)


def dot_left(left, right):
    return lax.dot_general(left, right, (((0,), (0,)), ((), ())), preferred_element_type=f32)


def dot_right(left, right):
    return lax.dot_general(left, right, (((1,), (1,)), ((), ())), preferred_element_type=f32)


def for_rows(count, size, body):
    def step(r, carry):
        body(pl.ds(pl.multiple_of(r * size, size), size))
        return carry

    lax.fori_loop(0, count // size, step, 0)


def standard(values):
    average = jnp.mean(values, axis=-1, keepdims=True)
    centred = values - average
    spread = jnp.mean(centred * centred, axis=-1, keepdims=True)
    rate = lax.rsqrt(spread + norm_epsilon)
    return centred * rate, rate


def add_into(dst, src):
    dst[...] = (dst[...].astype(f32) + src[...].astype(f32)).astype(dst.dtype)


def norm_rows(out, values, gain, shift):
    def body(part):
        unit, _ = standard(values[part, :].astype(f32))
        out[part, :] = (unit * gain + shift).astype(bf16)

    for_rows(out.shape[0], 64, body)


def norm_rows_back(grad, values, gain, add, out, sums, low, gain_row, shift_row, low_row):
    zero = jnp.zeros((1, MODEL_WIDTH), f32)
    sums[gain_row : gain_row + 1, :] = zero
    sums[shift_row : shift_row + 1, :] = zero
    if low_row is not None:
        sums[low_row : low_row + 1, :] = zero

    def body(part):
        unit, rate = standard(values[part, :].astype(f32))
        grad_part = grad[part, :]
        scaled = grad_part * gain
        inner = jnp.mean(scaled, axis=-1, keepdims=True)
        along = jnp.mean(scaled * unit, axis=-1, keepdims=True)
        total = add[part, :].astype(f32) + rate * (scaled - inner - unit * along)
        rounded = total.astype(bf16)
        if out is not None:
            out[part, :] = total
        low[part, :] = rounded
        sums[gain_row : gain_row + 1, :] += jnp.sum(grad_part * unit, axis=0, keepdims=True)
        sums[shift_row : shift_row + 1, :] += jnp.sum(grad_part, axis=0, keepdims=True)
        if low_row is not None:
            sums[low_row : low_row + 1, :] += jnp.sum(rounded.astype(f32), axis=0, keepdims=True)

    for_rows(grad.shape[0], 64, body)


QUAD = 4 * HEAD


def head_mask():
    lane_head = lax.broadcasted_iota(jnp.int32, (4, SEQ, QUAD), 2) // HEAD
    return lane_head == lax.broadcasted_iota(jnp.int32, (4, SEQ, QUAD), 0)


def by_head(values, mask):
    return jnp.where(mask, values.astype(f32)[None], 0.0).reshape(4 * SEQ, QUAD).astype(bf16)


def from_head(values, mask):
    return jnp.sum(jnp.where(mask, values.reshape(4, SEQ, QUAD), 0.0), axis=0)


def weights_of(queries, keys, allowed):
    scores = jnp.where(allowed, dot_right(keys, queries) * HEAD ** (-0.5), masked_value)
    weights = jnp.exp(scores - jnp.max(scores, axis=0, keepdims=True))
    return weights * (1.0 / jnp.sum(weights, axis=0, keepdims=True))


def attend(query, keys, values, allowed, mask):
    probs = weights_of(by_head(query, mask), keys, allowed).astype(bf16)
    return from_head(dot_left(probs, values), mask).astype(bf16)


def attend_back(query, keys, values, allowed, mask, grad_mixed):
    queries, grads = by_head(query, mask), by_head(grad_mixed, mask)
    probs = weights_of(queries, keys, allowed)
    grad_probs = dot_right(values, grads)
    inner = jnp.sum(probs * grad_probs, axis=0, keepdims=True)
    grad_scores = (probs * (grad_probs - inner)).astype(bf16)
    scale = HEAD ** (-0.5)
    return (
        (from_head(dot_left(grad_scores, keys), mask) * scale).astype(bf16),
        (dot(grad_scores, queries) * scale).astype(bf16),
        dot(probs.astype(bf16), grads).astype(bf16),
    )


def causal_mask():
    shape = (SEQ, 4 * SEQ)
    query = lax.broadcasted_iota(jnp.int32, shape, 1) % SEQ
    return lax.broadcasted_iota(jnp.int32, shape, 0) <= query


def unpack_vectors(blocks, vec, bias, n_dp, depth, inner_dp):
    for d in range(n_dp):
        row = d * VEC_ROWS
        vec[0:13, d * depth : (d + 1) * depth] = blocks[row : row + 13, 0:depth]
        for j in range(inner_dp // LANES):
            at, col = divmod(d * inner_dp + j * LANES, bias.shape[1])
            bias[at : at + 1, col : col + LANES] = blocks[row + 13 + j : row + 14 + j, :]


def pack_vectors(vec, bias, blocks, n_dp, depth, inner_dp):
    blocks[...] = jnp.zeros_like(blocks)
    for d in range(n_dp):
        row = d * VEC_ROWS
        blocks[row : row + 13, 0:depth] = vec[0:13, d * depth : (d + 1) * depth]
        for j in range(inner_dp // LANES):
            at, col = divmod(d * inner_dp + j * LANES, bias.shape[1])
            blocks[row + 13 + j : row + 14 + j, :] = bias[at : at + 1, col : col + LANES]


class Copies:
    def __init__(self, semaphores):
        self.semaphores, self.used, self.open = semaphores, 0, []

    def start(self, src, dst):
        copy = pltpu.make_async_copy(src, dst, self.semaphores.at[self.used])
        self.used += 1
        copy.start()
        self.open.append(copy)
        return copy

    def wait(self, *copies):
        for copy in copies:
            self.open = [other for other in self.open if other is not copy]
            copy.wait()

    def finish(self):
        self.wait(*self.open)


def kept_shapes(dims):
    n_dp, n_img, caps, depth, width, inner_dp, block_len = dims
    rows, wide, inner = caps * SEQ, MODEL_WIDTH, n_dp * inner_dp
    low, high = ((rows, wide), bf16), ((rows, wide), f32)
    return dict(
        weights=((wide, 6 * wide), bf16),
        normed1=low,
        qkv=((rows, 3 * wide), bf16),
        self_mixed=low,
        first_sum=high,
        normed2=low,
        query=low,
        kv=((n_img, caps, block_len, 2 * wide), bf16),
        mixed=low,
        second_sum=high,
        vec=((16, wide), f32),
        bias=((n_img, inner // n_img), f32),
        images=((n_img, caps, block_len, wide), bf16),
        ckv=((wide, 2 * wide), bf16),
    )


class Forward:
    def __init__(self, dims, counts, raw, tokens, kept):
        self.n_img, self.width = dims[1], dims[4]
        self.counts, self.raw, self.tokens, self.kept = counts, raw, tokens, kept

    def gain(self, k):
        return self.kept.vec[k : k + 1, :]

    def shift(self, k):
        return self.kept.vec[3 + k : 4 + k, :]

    def first_norm(self):
        norm_rows(self.kept.normed1, self.tokens, self.gain(0), self.shift(0))

    def assemble(self, i):
        weights, w, wide = self.kept.weights, self.width, MODEL_WIDTH
        weights[:, i * 3 * w : (i + 1) * 3 * w] = self.raw[i, :, 0 : 3 * w]
        for n in range(3):
            at = (3 + n) * wide + i * w
            weights[:, at : at + w] = self.raw[i, :, (3 + n) * w : (4 + n) * w]

    def image_kv(self, start, stop):
        wide, kv, images = MODEL_WIDTH, self.kept.kv, self.kept.images
        block = images[:, start:stop].reshape(-1, wide)
        for n in range(2):
            value = dot(block, self.kept.ckv[:, n * wide : (n + 1) * wide])
            if n == 1:
                value = value + self.shift(7)
            kv[:, start:stop, :, n * wide : (n + 1) * wide] = value.astype(bf16).reshape(
                images.shape[0], stop - start, images.shape[2], wide
            )

    def project(self):
        wide, qkv = MODEL_WIDTH, self.kept.qkv
        for n, shift in enumerate((3, None, 4)):
            value = dot(self.kept.normed1[...], self.kept.weights[:, n * wide : (n + 1) * wide])
            if shift is not None:
                value = value + self.shift(shift)
            qkv[:, n * wide : (n + 1) * wide] = value.astype(bf16)

    def self_attention(self, start, stop):
        qkv, out, wide = self.kept.qkv, self.kept.self_mixed, MODEL_WIDTH
        allowed, mask = causal_mask(), head_mask()

        def caption(c, carry):
            part = pl.ds(pl.multiple_of(c * SEQ, SEQ), SEQ)
            for t in range(wide // QUAD):
                at = t * QUAD
                out[part, at : at + QUAD] = attend(
                    qkv[part, at : at + QUAD],
                    qkv[part, wide + at : wide + at + QUAD],
                    qkv[part, 2 * wide + at : 2 * wide + at + QUAD],
                    allowed,
                    mask,
                )
            return carry

        lax.fori_loop(start, stop, caption, 0, unroll=True)

    def add_product(self, left, n, shift, base, out):
        wide = MODEL_WIDTH
        out[...] = dot(left[...], self.kept.weights[:, n * wide : (n + 1) * wide])
        row = self.shift(shift)

        def body(part):
            out[part, :] = base[part, :].astype(f32) + (out[part, :] + row)

        for_rows(out.shape[0], 64, body)

    def first_residual(self):
        wide = MODEL_WIDTH
        self.add_product(self.kept.self_mixed, 3, 5, self.tokens, self.kept.first_sum)
        norm_rows(self.kept.normed2, self.kept.first_sum, self.gain(1), self.shift(1))
        value = dot(self.kept.normed2[...], self.kept.weights[:, 4 * wide : 5 * wide])
        self.kept.query[...] = (value + self.shift(6)).astype(bf16)

    def valid_keys(self, c):
        shape = (self.n_img * self.kept.kv.shape[2], 4 * SEQ)
        return lax.broadcasted_iota(jnp.int32, shape, 0) < self.counts[c]

    def cross_attention(self, start, stop):
        query, kv, out, wide = self.kept.query, self.kept.kv, self.kept.mixed, MODEL_WIDTH
        mask = head_mask()
        length = self.n_img * kv.shape[2]

        def caption(c, carry):
            part = pl.ds(pl.multiple_of(c * SEQ, SEQ), SEQ)
            allowed = self.valid_keys(c)
            for t in range(wide // QUAD):
                at = t * QUAD
                out[part, at : at + QUAD] = attend(
                    query[part, at : at + QUAD],
                    kv[:, c, :, at : at + QUAD].reshape(length, QUAD),
                    kv[:, c, :, wide + at : wide + at + QUAD].reshape(length, QUAD),
                    allowed,
                    mask,
                )
            return carry

        lax.fori_loop(start, stop, caption, 0, unroll=True)

    def second_residual(self):
        self.add_product(self.kept.mixed, 5, 8, self.kept.first_sum, self.kept.second_sum)


class Gatherer:
    def __init__(self, here, groups, own, full, send_sem, recv_sem):
        self.here, self.groups, self.own, self.full = here, groups, own, full
        self.send_sem, self.recv_sem = send_sem, recv_sem
        self.sends, self.used = Sends(), [0] * len(groups)

    def forward(self, g, d, i, src, device, when=None):
        self.sends.send(
            src,
            self.groups[g].block(self.full[g], d, i),
            self.send_sem.at[g, self.used[g]],
            self.recv_sem.at[g, d, i],
            device,
            when,
        )
        self.used[g] += 1

    def arrived(self, g, d, i):
        block, here = self.groups[g].block(self.full[g], d, i), self.here
        pltpu.make_async_remote_copy(
            block,
            block,
            self.send_sem.at[g, 0],
            self.recv_sem.at[g, d, i],
            device_id=(here.sib, here.im),
            device_id_type=MESH,
        ).wait_recv()
        return block

    def to_planes(self, g, d, i, block):
        here = self.here
        self.forward(g, d, i, block, (here.first(here.dp), here.im))
        self.forward(g, d, i, block, (here.second(here.dp), here.im))
        self.forward(g, d, i, block, (here.sib, here.im))

    def start(self, g):
        here = self.here
        dp, im = here.dp, here.im
        self.forward(g, dp, im, self.own[g], (dp, im + 1), im < here.n_img - 1)
        self.forward(g, dp, im, self.own[g], (dp, im - 1), im > 0)
        self.to_planes(g, dp, im, self.own[g])

    def line(self, g, k):
        here = self.here
        dp, im, i = here.dp, here.im, here.near(k)
        block = self.arrived(g, dp, i)
        after = im + jnp.where(i < im, 1, -1)
        self.forward(g, dp, i, block, (dp, after), (after >= 0) & (after < here.n_img))
        self.to_planes(g, dp, i, block)

    def first(self, g, k):
        here = self.here
        d, i = here.first(here.dp), here.near(k)
        block = self.arrived(g, d, i)
        self.forward(g, d, i, block, (here.second(here.dp), here.im))
        self.forward(g, d, i, block, (here.sib, here.im))

    def second(self, g, k):
        here = self.here
        i = here.near(k)
        for d in (here.second(here.dp), here.second(here.first(here.dp))):
            block = self.arrived(g, d, i)
            self.forward(g, d, i, block, (here.sib, here.im))

    def complete(self, g):
        for c in range(4):
            for i in range(self.here.n_img):
                self.arrived(g, 2 * c + 1 - self.here.core, i)


X_PARTS = 4
LAGS = (6, 12)
X_EVERY = 4


def entry_groups(dims):
    n_dp, n_img, caps, depth, width, inner_dp, block_len = dims
    wide, inner = MODEL_WIDTH, n_dp * inner_dp
    return [
        Group(VEC_ROWS, LANES, f32, (n_img, n_dp * VEC_ROWS, LANES), stacked_block),
        Group(depth, 2 * width, bf16, (wide, 2 * wide), grid_block),
        Group(depth, 6 * width, bf16, (n_img, wide, 6 * width), stacked_block),
        Group(depth, inner // n_img, bf16, (wide, inner), grid_block),
        Group(width, inner_dp, bf16, (wide, inner), turned_block),
    ]


def entry_kernel(dims, *refs):
    n_dp, n_img, caps, depth, width, inner_dp, block_len = dims
    groups, shapes = entry_groups(dims), kept_shapes(dims)
    count = len(groups)
    counts, own, (x_ref, tokens_hbm) = refs[0], refs[1 : 1 + count], refs[1 + count : 3 + count]
    refs = refs[3 + count :]
    outs, (in_w, out_t) = bag(shapes, refs), refs[len(shapes) : len(shapes) + 2]
    refs = refs[len(shapes) + 2 :]
    kept, refs = bag(shapes, refs), refs[len(shapes) :]
    vec_full, raw, tokens, send_sem, recv_sem, xs_sem, xr_sem, local_sem = refs
    here = Place(n_img)
    dp, im = here.dp, here.im
    copies = Copies(local_sem)
    full = (vec_full, kept.ckv, raw, in_w, out_t)
    gather = Gatherer(here, groups, own, full, send_sem, recv_sem)
    local_blocks = [
        copies.start(own[g], groups[g].block(full[g], dp, im)) for g in range(count)
    ]
    own_images = copies.start(x_ref.at[pl.ds(im * caps, caps)], kept.images.at[im])
    token_load = copies.start(tokens_hbm, tokens)
    here.barrier()
    for g in range(count):
        gather.start(g)
    part_caps = caps // X_PARTS

    def x_copy(k, p, target, source):
        return pltpu.make_async_remote_copy(
            x_ref.at[pl.ds(target * caps + p * part_caps, part_caps)],
            kept.images.at[source, pl.ds(p * part_caps, part_caps)],
            xs_sem.at[k, p],
            xr_sem.at[k, p],
            device_id=(dp, target),
            device_id_type=MESH,
        )

    waiting = [(k, p) for p in range(X_PARTS) for k in range(1, n_img)][::-1]
    ticks = [0]

    def tick():
        ticks[0] += 1
        if ticks[0] % X_EVERY == 0 and waiting:
            k, p = waiting.pop()
            gather.sends.send_copy(x_copy(k, p, (im + k) % n_img, im))

    units = [(g, k) for g in range(count) for k in range(n_img)]

    def exchange(t):
        if t < len(units):
            g, k = units[t]
            if k > 0:
                gather.line(g, k)
                tick()
        if 0 <= t - LAGS[0] < len(units):
            gather.first(*units[t - LAGS[0]])
            tick()
        if 0 <= t - LAGS[1] < len(units):
            gather.second(*units[t - LAGS[1]])
            tick()

    def images_of(p):
        part = pl.ds(p * part_caps, part_caps)
        for k in range(1, n_img):
            source = (im + n_img - k) % n_img
            x_copy(k, p, source, source).wait_recv()
        copies.start(kept.images.at[:, part], outs.images.at[:, part])
        step.image_kv(p * part_caps, (p + 1) * part_caps)
        copies.start(kept.kv.at[:, part], outs.kv.at[:, part])

    step = Forward(dims, counts, raw, tokens, kept)
    done = LAGS[1] + n_img
    for t in range(len(units) + LAGS[1]):
        exchange(t)
        if t == done:
            gather.complete(0)
            copies.wait(local_blocks[0], token_load)
            unpack_vectors(vec_full.at[0], kept.vec, kept.bias, n_dp, depth, inner_dp)
            step.first_norm()
        if t == done + n_img:
            gather.complete(1)
            copies.wait(local_blocks[1], own_images)
            images_of(0)
        if t == done + n_img + 2:
            images_of(1)
        if t == done + 2 * n_img:
            gather.complete(2)
            copies.wait(local_blocks[2])
            for i in range(n_img):
                step.assemble(i)
            step.project()
        if t == done + 2 * n_img + 1:
            step.self_attention(0, caps // 2)
        if t == done + 2 * n_img + 2:
            step.self_attention(caps // 2, caps)
        if t == done + 2 * n_img + 3:
            step.first_residual()
        if t == done + 2 * n_img + 4:
            step.cross_attention(0, part_caps)
        if t == done + 2 * n_img + 5:
            step.cross_attention(part_caps, 2 * part_caps)
    copies.start(kept.vec, outs.vec)
    copies.start(kept.bias, outs.bias)
    copies.start(kept.ckv, outs.ckv)
    copies.start(kept.weights, outs.weights)
    copies.start(kept.normed1, outs.normed1)
    copies.start(kept.qkv, outs.qkv)
    copies.start(kept.self_mixed, outs.self_mixed)
    copies.start(kept.first_sum, outs.first_sum)
    copies.start(kept.normed2, outs.normed2)
    copies.start(kept.query, outs.query)
    for p in range(2, X_PARTS):
        images_of(p)
        step.cross_attention(p * part_caps, (p + 1) * part_caps)
    copies.start(kept.mixed, outs.mixed)
    step.second_residual()
    copies.start(kept.second_sum, outs.second_sum)
    for g in range(3, count):
        gather.complete(g)
    gather.sends.finish()
    copies.finish()


def entry_pass(dims, counts, owns, image_tokens, tokens):
    n_dp, n_img, caps, depth, width, inner_dp, block_len = dims
    groups, shapes = entry_groups(dims), kept_shapes(dims)
    count = len(groups)
    dma = pltpu.SemaphoreType.DMA
    any_spec = pl.BlockSpec(memory_space=pl.ANY)
    outs = pl.pallas_call(
        functools.partial(entry_kernel, dims),
        out_shape=structs_of(shapes) + [jax.ShapeDtypeStruct(g.full, g.dtype) for g in groups[3:]],
        in_specs=[pl.BlockSpec(memory_space=pltpu.SMEM)] + [any_spec] * (count + 2),
        out_specs=[any_spec] * (len(shapes) + 2),
        scratch_shapes=[pltpu.VMEM(*shape) for shape in shapes.values()]
        + [pltpu.VMEM(groups[0].full, f32), pltpu.VMEM(groups[2].full, bf16), pltpu.VMEM(tokens.shape, bf16)]
        + [
            dma((count, 64)),
            dma((count, n_dp, n_img)),
            dma((n_img, X_PARTS)),
            dma((n_img, X_PARTS)),
            dma((48,)),
        ],
        compiler_params=pltpu.CompilerParams(
            collective_id=1, has_side_effects=True, vmem_limit_bytes=62 << 20
        ),
    )(counts, *owns, image_tokens, tokens)
    kept = dict(zip(shapes, outs))
    kept.update(in_w=outs[-2], out_t=outs[-1])
    return kept


class Backward:
    def __init__(self, dims, counts, refs):
        self.dims, self.counts, self.refs = dims, counts, refs

    def __getattr__(self, name):
        return getattr(self.refs, name)

    def gain(self, k):
        return self.vec[k : k + 1, :]

    def weight(self, n):
        return self.weights[n][...]

    def sum_row(self, k, values):
        self.sums[3 + k : 4 + k, :] = jnp.sum(values.astype(f32), axis=0, keepdims=True)

    def begin(self):
        wide = MODEL_WIDTH
        norm_rows(self.normed3, self.second_sum, self.gain(2), self.vec[5:6, :])
        self.sum_row(9, self.cot[...])
        self.turned[0:wide, :] = self.normed3[...].astype(f32).T.astype(bf16)
        self.turned[wide : 2 * wide, :] = self.cot[...].astype(f32).T.astype(bf16)
        row = self.vec[12:13, :]

        def body(part):
            self.result[part, :] = self.second_sum[part, :] + row
            self.grad[part, :] = jnp.zeros((64, wide), f32)

        for_rows(self.result.shape[0], 64, body)

    def feed_forward(self, bias, in_w, out_t):
        rows = self.normed3.shape[0]
        self.hidden[...] = dot(self.normed3[...], in_w[...])
        self.grad_act[...] = dot(self.cot[...], out_t[...])
        self.hidden_sums[...] = jnp.zeros_like(self.hidden_sums)

        def body(part):
            pre = self.hidden[part, :] + bias
            below = 0.5 * (1.0 + lax.erf(pre * 2**-0.5))
            self.activated[part, :] = (pre * below).astype(bf16)
            slope = below + pre * (jnp.exp(-0.5 * pre * pre) * (2 * jnp.pi) ** -0.5)
            grad = (self.grad_act[part, :] * slope).astype(bf16)
            self.grad_hidden[part, :] = grad
            self.hidden_sums[...] += jnp.sum(grad.astype(f32), axis=0, keepdims=True)

        for_rows(rows, 32, body)
        self.result[...] += dot_right(self.activated[...], out_t[...])
        self.grad[...] += dot_right(self.grad_hidden[...], in_w[...])

    def third_norm_back(self):
        norm_rows_back(
            self.grad, self.second_sum, self.gain(2), self.cot, self.grad_sum, self.sums, self.low, 2, 5, 11
        )

    def cross_grad(self):
        self.grad_mixed[...] = dot_right(self.low[...], self.weight(5)).astype(bf16)

    def cross_caption(self, c, kv, grad_kv):
        wide = MODEL_WIDTH
        n_img, block_len = kv.shape[:2]
        length = n_img * block_len
        part = pl.ds(pl.multiple_of(c * SEQ, SEQ), SEQ)
        allowed = lax.broadcasted_iota(jnp.int32, (length, 4 * SEQ), 0) < self.counts[c]
        mask = head_mask()
        for t in range(wide // QUAD):
            own, other = slice(t * QUAD, (t + 1) * QUAD), slice(wide + t * QUAD, wide + (t + 1) * QUAD)
            grad_query, grad_keys, grad_values = attend_back(
                self.query[part, own],
                kv[:, :, own].reshape(length, QUAD),
                kv[:, :, other].reshape(length, QUAD),
                allowed,
                mask,
                self.grad_mixed[part, own],
            )
            self.grad_query[part, own] = grad_query
            grad_kv[:, :, own] = grad_keys.reshape(n_img, block_len, QUAD)
            grad_kv[:, :, other] = grad_values.reshape(n_img, block_len, QUAD)
            self.sums[10:11, own] += jnp.sum(grad_values.astype(f32), axis=0, keepdims=True)

    def second_norm_back(self):
        self.sum_row(6, self.grad_query[...])
        self.grad[...] = dot_right(self.grad_query[...], self.weight(4))
        norm_rows_back(
            self.grad, self.first_sum, self.gain(1), self.grad_sum, self.grad_sum, self.sums, self.low, 1, 4, 8
        )

    def self_grad(self):
        self.grad_mixed[...] = dot_right(self.low[...], self.weight(3)).astype(bf16)

    def self_attention(self, start, stop):
        wide = MODEL_WIDTH
        allowed, mask = causal_mask(), head_mask()

        def caption(c, carry):
            part = pl.ds(pl.multiple_of(c * SEQ, SEQ), SEQ)
            for t in range(wide // QUAD):
                own, other = slice(t * QUAD, (t + 1) * QUAD), slice(wide + t * QUAD, wide + (t + 1) * QUAD)
                grads = attend_back(
                    self.kv[0, c, :, own],
                    self.kv[0, c, :, other],
                    self.kv[1, c, :, own],
                    allowed,
                    mask,
                    self.grad_mixed[part, own],
                )
                self.kv[2, c, :, own] = grads[0]
                self.kv[2, c, :, other] = grads[1]
                self.kv[3, c, :, own] = grads[2]
            return carry

        lax.fori_loop(start, stop, caption, 0, unroll=2)

    def grad_qkv(self, place, start, stop):
        rows = self.kv.shape[1] * SEQ
        return self.kv[2 + place, :, :, start:stop].reshape(rows, stop - start)

    def qkv_grads(self, pair, stage):
        wide, block = MODEL_WIDTH, 3 * MODEL_WIDTH // 4
        unit = self.normed1[...]
        if pair == 0:
            both = dot_left(unit, self.grad_qkv(0, 0, 2 * block)).astype(bf16)
            stage[0, :, 0:block] = both[:, 0:block]
            stage[1, :, 0:block] = both[:, block : 2 * block]
        else:
            keys = dot_left(unit, self.grad_qkv(0, 2 * block, 2 * wide)).astype(bf16)
            values = dot_left(unit, self.grad_qkv(1, 0, wide)).astype(bf16)
            cut = 3 * block - 2 * wide
            stage[0, :, 0 : 2 * wide - 2 * block] = keys
            stage[0, :, 2 * wide - 2 * block : block] = values[:, 0:cut]
            stage[1, :, 0:block] = values[:, cut:]

    def first_norm_back(self, weights):
        wide = MODEL_WIDTH
        parts = [self.grad_qkv(0, 0, wide), self.grad_qkv(0, wide, 2 * wide), self.grad_qkv(1, 0, wide)]
        self.sum_row(3, parts[0])
        self.sum_row(4, parts[2])
        self.grad[...] = dot_right(parts[0], weights[0][...])
        for part, weight in zip(parts[1:], weights[1:]):
            self.grad[...] += dot_right(part, weight[...])
        norm_rows_back(
            self.grad, self.tokens, self.gain(0), self.grad_sum, None, self.sums, self.low, 0, 3, None
        )


class Reducer:
    def __init__(self, here, groups, places, buffers, semaphores, credits):
        self.here, self.groups, self.places, self.n_img = here, groups, places, here.n_img
        self.acc, self.r0, self.r1, self.r2, self.zr = buffers
        (self.load_sem, self.s0, self.r0_sem, self.s1, self.r1_sem, self.s2, self.r2_sem, self.sz, self.rz) = semaphores
        self.credits = credits
        self.sends = Sends()
        self.sent = {}
        dp = here.dp
        self.chip = dp // 2
        self.chip1, self.chip2 = here.first(dp) // 2, here.second(dp) // 2
        self.chip12 = here.second(here.first(dp)) // 2

    @staticmethod
    def leads(n_img):
        return (4, n_img), (4, n_img), (2, n_img), (n_img,), (n_img + 1,)

    @staticmethod
    def semaphores(count, n_img):
        dma = pltpu.SemaphoreType.DMA
        sizes = [(4, n_img)] * 3 + [(2, n_img)] * 2 + [(n_img,)] * 3 + [(n_img + 1,)]
        return [dma((count,) + size) for size in sizes]

    def view(self, buffers, g, *index):
        own, shared, start = self.places[g]
        store = own if buffers is self.acc else shared
        return buffers[store].at[index + (pl.ds(start, self.groups[g].rows), slice(None))]

    def send(self, g, src, dst, send_sem, recv_sem, device, when=None):
        entry = self.sends.send(src, dst, send_sem, recv_sem, device, when)
        self.sent.setdefault(g, []).append(entry)
        return entry

    def settle(self, g):
        self.sends.wait(*self.sent.pop(g))

    def give_each(self, g, c, i, count, own, other):
        return [self.give(g, c, i + n, 1, own.at[pl.ds(n, 1)], other.at[pl.ds(n, 1)]) for n in range(count)]

    def give(self, g, c, i, count, own, other):
        here, part = self.here, pl.ds(i, count)
        copy = pltpu.make_async_copy(own, self.view(self.acc, g, c, part), self.load_sem.at[g, c, i])
        copy.start()
        sent = self.sends.send(
            other,
            self.view(self.r0, g, c, part),
            self.s0.at[g, c, i],
            self.r0_sem.at[g, c, i],
            (here.sib, here.im),
        )
        return copy, sent

    def given(self, pieces):
        for copy, sent in pieces:
            copy.wait()
            self.sends.wait(sent)

    def chips(self):
        return self.chip12, self.chip2, self.chip1, self.chip

    def arrived(self, buffer, semaphore):
        here = self.here
        pltpu.make_async_remote_copy(
            buffer, buffer, self.s0.at[0, 0, 0], semaphore, device_id=(here.sib, here.im), device_id_type=MESH
        ).wait_recv()

    def take(self, block, buffer, semaphore):
        self.arrived(buffer, semaphore)
        add_into(block, buffer)

    def pair(self, g, c, i, count):
        part = pl.ds(i, count)
        block = self.view(self.acc, g, c, part)
        self.take(block, self.view(self.r0, g, c, part), self.r0_sem.at[g, c, i])
        return block

    def second_send(self, g, j, c, i, count, when=None):
        here, part = self.here, pl.ds(i, count)
        self.send(
            g,
            self.view(self.acc, g, c, part),
            self.view(self.r1, g, j, part),
            self.s1.at[g, j, i],
            self.r1_sem.at[g, j, i],
            (here.second(here.dp), here.im),
            when,
        )

    def second(self, g, i, count):
        for j, c in ((1, self.chip12), (0, self.chip2)):
            for n in range(i, i + count):
                self.pair(g, c, n, 1)
                self.second_send(g, j, c, n, 1)

    def second_if(self, g, c):
        far = jnp.where(self.chip12 == c, 1, 0)
        when = (self.chip12 == c) | (self.chip2 == c)

        for i in range(self.n_img):

            @pl.when(when)
            def _():
                self.pair(g, c, i, 1)

            self.second_send(g, far, c, i, 1, when)

    def first(self, g, i, count):
        for n in range(i, i + count):
            self.first_one(g, n, 1)

    def first_one(self, g, i, count):
        here, part = self.here, pl.ds(i, count)
        block = self.pair(g, self.chip1, i, count)
        self.take(block, self.view(self.r1, g, 1, part), self.r1_sem.at[g, 1, i])
        self.send(
            g,
            block,
            self.view(self.r2, g, part),
            self.s2.at[g, i],
            self.r2_sem.at[g, i],
            (here.first(here.dp), here.im),
        )

    def plane(self, g, i, count):
        for n in range(i, i + count):
            self.plane_one(g, n, 1)

    def plane_one(self, g, i, count):
        part = pl.ds(i, count)
        block = self.pair(g, self.chip, i, count)
        self.take(block, self.view(self.r1, g, 0, part), self.r1_sem.at[g, 0, i])
        self.take(block, self.view(self.r2, g, part), self.r2_sem.at[g, i])

    def line(self, g, k):
        here, im, n_img = self.here, self.here.im, self.n_img
        i = here.near(k)
        block = self.view(self.acc, g, self.chip, i)
        down = jnp.where(i < im, 1, 0)

        @pl.when((im > 0) & (im < n_img - 1))
        def _():
            self.take(block, self.view(self.zr, g, i), self.rz.at[g, i])

        target = im + 1 - 2 * down
        slot = jnp.where((down == 1) & (i == target), n_img, i)
        self.send(
            g, block, self.view(self.zr, g, slot), self.sz.at[g, i], self.rz.at[g, slot], (here.dp, target)
        )

    def last(self, g, out):
        im, n_img = self.here.im, self.n_img
        out[...] = self.view(self.acc, g, self.chip, im)[...].astype(f32)
        for slot, has in ((im, im > 0), (n_img, im < n_img - 1)):

            @pl.when(has)
            def _():
                buffer = self.view(self.zr, g, slot)
                self.arrived(buffer, self.rz.at[g, slot])
                out[...] += buffer[...].astype(f32)

    def neighbours(self):
        here = self.here
        im = here.im
        return ((here.dp, im - 1), im > 0, 3), ((here.dp, im + 1), im < self.n_img - 1, 4)

    def free_partner(self, n):
        here = self.here
        partner = (here.sib, here.second(here.dp), here.first(here.dp))[n]
        pl.semaphore_signal(self.credits.at[n], inc=1, device_id=(partner, here.im), device_id_type=MESH)

    def await_partner(self, n):
        pl.semaphore_wait(self.credits.at[n], 1)

    def free_line(self):
        for device, has, n in self.neighbours():
            mine = 7 - n

            @pl.when(has)
            def _():
                pl.semaphore_signal(self.credits.at[mine], inc=1, device_id=device, device_id_type=MESH)

    def await_line(self):
        for device, has, n in self.neighbours():

            @pl.when(has)
            def _():
                pl.semaphore_wait(self.credits.at[n], 1)


def bag(shapes, refs):
    return SimpleNamespace(**dict(zip(shapes, refs)))


def structs_of(shapes):
    return [jax.ShapeDtypeStruct(*shape) for shape in shapes.values()]


def back_inputs(dims):
    n_dp, n_img, caps, depth, width, inner_dp, block_len = dims
    wide, rows, inner = MODEL_WIDTH, caps * SEQ, n_dp * inner_dp
    low, high = ((rows, wide), bf16), ((rows, wide), f32)
    return dict(
        vec=((16, wide), f32),
        bias=((n_img, inner // n_img), f32),
        second_sum=high,
        cot=low,
        mixed=low,
        query=low,
        kv=((n_img, caps, block_len, 2 * wide), bf16),
        images=((n_img, caps, block_len, wide), bf16),
        normed2=low,
        in_w=((wide, inner), bf16),
        out_t=((wide, inner), bf16),
        weights=((wide, 6 * wide), bf16),
        ckv=((wide, 2 * wide), bf16),
        first_sum=high,
        qkv=((caps, SEQ, 3 * wide), bf16),
        self_mixed=low,
        normed1=low,
        tokens=low,
    )


def back_outputs(dims):
    n_dp, n_img, caps, depth, width, inner_dp, block_len = dims
    wide, rows, inner = MODEL_WIDTH, caps * SEQ, n_dp * inner_dp
    return dict(
        layer_out=((rows, wide), bf16),
        token_grads=((rows, wide), bf16),
        image_out=((n_img, caps, block_len, wide), bf16),
        s_out=((width, inner_dp), f32),
        s_in=((depth, inner // n_img), f32),
        s_cross=((depth, 2 * width), f32),
        s_ckv=((depth, 2 * width), f32),
        s_self=((depth, 4 * width), f32),
        s_vec=((VEC_ROWS, LANES), f32),
    )


def back_scratch(dims):
    n_dp, n_img, caps, depth, width, inner_dp, block_len = dims
    wide, rows, inner = MODEL_WIDTH, caps * SEQ, n_dp * inner_dp
    tile = inner // n_img
    low, high = ((rows, wide), bf16), ((rows, wide), f32)
    return dict(
        vec=((16, wide), f32),
        bias=((n_img, tile), f32),
        sums=((16, wide), f32),
        bias_sums=((n_img, tile), f32),
        hidden_sums=((1, tile), f32),
        vectors=((1, n_dp * VEC_ROWS, LANES), f32),
        cot=low,
        second_sum=high,
        normed3=low,
        turned=((2 * wide, rows), bf16),
        result=high,
        grad=high,
        hidden=((rows, tile), f32),
        grad_act=((rows, tile), f32),
        activated=((rows, tile), bf16),
        grad_hidden=((rows, tile), bf16),
        in_tile=((2, wide, tile), bf16),
        out_tile=((2, wide, tile), bf16),
        stage_in=((1, wide, tile), bf16),
        stage_out=((n_img, width, tile), bf16),
        low=low,
        mixed=low,
        query=low,
        normed2=low,
        kv=((n_img, caps, block_len, 2 * wide), bf16),
        images=((n_img, caps, block_len, wide), bf16),
        images_out=((n_img, caps, block_len, wide), bf16),
        stage_cross=((n_img, wide, 2 * width), bf16),
        stage_self=((2, wide, 4 * width), bf16),
    )


OUT, IN, CROSS, CKV, SELF, VEC = range(6)
PLACES = ((0, 0, 0), (1, 1, 0), (2, 0, 0), (2, 0, 1), (1, 1, 0), (3, 2, 0))


def back_groups(dims):
    n_dp, n_img, caps, depth, width, inner_dp, block_len = dims
    wide, inner = MODEL_WIDTH, n_dp * inner_dp
    return [
        Group(width, inner_dp, bf16, (wide, inner), turned_block),
        Group(depth, inner // n_img, bf16, (wide, inner), grid_block),
        Group(depth, 2 * width, bf16, (n_img, wide, 2 * width), stacked_block),
        Group(depth, 2 * width, bf16, (wide, 2 * wide), grid_block),
        Group(depth, 4 * width, bf16, (n_img, wide, 4 * width), stacked_block),
        Group(VEC_ROWS, LANES, f32, (n_dp * VEC_ROWS, LANES), repeated_block),
    ]


def back_buffers(dims):
    groups = back_groups(dims)
    out, inside, vec = [(g.rows, g.cols, g.dtype) for g in (groups[OUT], groups[IN], groups[VEC])]
    stores = [[out, inside, out, vec]] + [[out, inside, vec]] * 4
    return [
        [pltpu.VMEM(lead + store[:2], store[2]) for store in these]
        for lead, these in zip(Reducer.leads(dims[1]), stores)
    ]


def back_kernel(dims, *refs):
    n_dp, n_img, caps, depth, width, inner_dp, block_len = dims
    wide, rows, inner = MODEL_WIDTH, caps * SEQ, n_dp * inner_dp
    tile = inner // n_img
    inputs, outputs, scratch = back_inputs(dims), back_outputs(dims), back_scratch(dims)
    counts, refs = refs[0], refs[1:]
    hbm, refs = bag(inputs, refs), refs[len(inputs) :]
    outs, refs = bag(outputs, refs), refs[len(outputs) :]
    s, refs = bag(scratch, refs), refs[len(scratch) :]
    groups = back_groups(dims)
    buffers = []
    for these in back_buffers(dims):
        buffers.append(refs[: len(these)])
        refs = refs[len(these) :]
    places = [(own, shared, start * depth) for own, shared, start in PLACES]
    here = Place(n_img)
    dp, im, core = here.dp, here.im, here.core
    red = Reducer(here, groups, places, buffers, refs[:9], refs[9])
    copies = Copies(refs[10])
    dx_send, dx_recv = refs[11:]
    every = range(n_img)
    names = list(inputs)

    def load(*wanted):
        return [copies.start(getattr(hbm, name), getattr(s, name)) for name in wanted]

    first_loads = load(*names[:4])

    def load_tile(t):
        cols = pl.ds(t * tile, tile)
        return [
            copies.start(hbm.in_w.at[:, cols], s.in_tile.at[t % 2]),
            copies.start(hbm.out_t.at[:, cols], s.out_tile.at[t % 2]),
        ]

    def load_square(n, dst):
        return copies.start(hbm.weights.at[:, pl.ds(n * wide, wide)], dst)

    tiles = [load_tile(0), load_tile(1)]
    middle_loads = load(*names[4:9])
    here.barrier()
    copies.wait(*first_loads)
    s.sums[...] = jnp.zeros_like(s.sums)
    step = Backward(dims, counts, s)
    step.begin()
    given = []
    own, other = tile_ds(core, inner_dp, LANES), tile_ds(1 - core, inner_dp, LANES)
    for t in every:
        copies.wait(*tiles[t])
        step.feed_forward(s.bias[t : t + 1, :], s.in_tile.at[t % 2], s.out_tile.at[t % 2])
        s.bias_sums[t : t + 1, :] = s.hidden_sums[...]
        if t + 2 < n_img:
            tiles.append(load_tile(t + 2))
        red.given(given)
        s.stage_in[0] = dot(s.turned[0:wide, :], s.grad_hidden[...]).astype(bf16)
        given = [
            red.give(
                IN,
                c,
                t,
                1,
                s.stage_in.at[:, tile_ds(2 * c + core, depth, 16), :],
                s.stage_in.at[:, tile_ds(2 * c + 1 - core, depth, 16), :],
            )
            for c in red.chips()
        ]
        value = dot(s.turned[wide : 2 * wide, :], s.activated[...]).astype(bf16)
        s.stage_out[...] = value.reshape(s.stage_out.shape)
        given.extend(red.give_each(OUT, t, 0, n_img, s.stage_out.at[:, :, own], s.stage_out.at[:, :, other]))
        if t >= 1:
            red.second(IN, t - 1, 1)
            red.second_if(OUT, t - 1)
        if t >= 2:
            red.first(IN, t - 2, 1)
    red.given(given)
    cross_loads = [load_square(4 + n, s.in_tile.at[n]) for n in range(2)]
    cross_loads += [copies.start(hbm.ckv.at[:, pl.ds(n * wide, wide)], s.out_tile.at[n]) for n in range(2)]
    first_sum = copies.start(hbm.first_sum, s.grad_act)
    red.second(IN, n_img - 1, 1)
    red.second_if(OUT, n_img - 1)

    def body(part):
        s.activated[part, :] = s.result[part, :].astype(bf16)

    for_rows(rows, 64, body)
    layer_out = copies.start(s.activated, outs.layer_out)
    s.grad_sum, s.grad_query, s.first_sum = s.hidden, s.grad_hidden, s.grad_act
    step.third_norm_back()
    copies.wait(layer_out, *cross_loads)
    s.grad_mixed, s.weights = s.activated, (None,) * 4 + (s.in_tile.at[0], s.in_tile.at[1])
    step.cross_grad()
    sout_load = load_square(3, s.in_tile.at[1])
    copies.wait(*middle_loads)
    flat = n_img * caps * block_len

    def dx(k, c):
        target, part = (im + k) % n_img, pl.ds(c, 1)
        red.sends.send(
            s.images_out.at[target, part],
            outs.image_out.at[im, part],
            dx_send.at[k, c],
            dx_recv.at[k, c],
            (dp, target),
        )

    def caption(c, carry):
        step.cross_caption(c, s.kv.at[:, c], s.kv.at[:, c])
        return carry

    def captions_back(p):
        lax.fori_loop(2 * p, 2 * p + 2, caption, 0, unroll=True)

    def images_back(p):
        part = slice(2 * p, 2 * p + 2)
        length = n_img * 2 * block_len
        value = dot_right(s.kv[:, part, :, 0:wide].reshape(length, wide), s.out_tile[0])
        value = value + dot_right(s.kv[:, part, :, wide : 2 * wide].reshape(length, wide), s.out_tile[1])
        s.images_out[:, part] = value.astype(bf16).reshape(n_img, 2, block_len, wide)

    def square_grad(values, grads, n):
        for m in range(wide // 256):
            cols = slice(m * 256, (m + 1) * 256)
            s.stage_in[0, :, cols] = dot_left(values[...], grads[:, cols]).astype(bf16)
        if n is not None:
            for i in every:
                s.stage_cross[i, :, n * width : (n + 1) * width] = s.stage_in[0, :, i * width : (i + 1) * width]

    def ckv_grad(n):
        at, col = divmod(n * 256, wide)
        part = s.kv[:, :, :, n * 256 : (n + 1) * 256].reshape(flat, 256)
        s.out_tile[at, :, col : col + 256] = dot_left(s.images[...].reshape(flat, wide), part).astype(bf16)

    def give_ckv():
        pieces = []
        for c in red.chips():
            for i in every:
                at, col = divmod(i * 2 * width, wide)
                half = s.out_tile.at[pl.ds(at, 1), :, pl.ds(col, 2 * width)]
                pieces.append(
                    red.give(
                        CKV,
                        c,
                        i,
                        1,
                        half.at[:, tile_ds(2 * c + core, depth, 16), :],
                        half.at[:, tile_ds(2 * c + 1 - core, depth, 16), :],
                    )
                )
        return pieces

    def give_stacked(g, stage, i):
        count = stage.shape[0]
        return [
            piece
            for c in red.chips()
            for piece in red.give_each(
                g,
                c,
                i,
                count,
                stage.at[:, tile_ds(2 * c + core, depth, 16), :],
                stage.at[:, tile_ds(2 * c + 1 - core, depth, 16), :],
            )
        ]

    def give_vec():
        pack_vectors(s.sums, s.bias_sums, s.vectors.at[0], n_dp, depth, inner_dp)
        pieces = []
        for c in red.chips():
            for i in every:
                own = s.vectors.at[:, tile_ds(2 * c + core, VEC_ROWS, 8), :]
                other = s.vectors.at[:, tile_ds(2 * c + 1 - core, VEC_ROWS, 8), :]
                pieces.append(red.give(VEC, c, i, 1, own, other))
        return pieces

    def self_weights(pair):
        step.qkv_grads(pair, s.stage_self)
        for n in range(2):
            i = 2 * pair + n
            s.stage_self[n, :, 3 * width :] = s.stage_in[0, :, i * width : (i + 1) * width]

    captions_back(0)
    images_back(0)
    dx(2, 0)
    dx(1, 0)
    dx(3, 0)
    dx(2, 1)
    captions_back(1)
    images_back(1)
    for i in (2, 3):
        red.first(IN, i, 1)
    dx(1, 1)
    dx(3, 1)
    dx(2, 2)
    captions_back(2)
    images_back(2)
    dx(1, 2)
    dx(3, 2)
    captions_back(3)
    tokens = copies.start(hbm.tokens, s.query)
    images_back(3)
    red.first(OUT, 0, n_img)
    dx(2, 3)
    dx(1, 3)
    square_grad(s.mixed, s.low, 0)
    self_mixed = copies.start(hbm.self_mixed, s.mixed)
    ckv_grad(0)
    ckv_grad(1)
    ckv_grad(2)
    for i in every:
        red.plane(IN, i, 1)
    ckv_grad(3)
    ckv_grad(4)
    ckv_grad(5)
    qkv_loads = [
        copies.start(hbm.qkv.at[:, :, pl.ds(0, 2 * wide)], s.kv.at[0]),
        copies.start(hbm.qkv.at[:, :, pl.ds(2 * wide, wide)], s.kv.at[1, :, :, pl.ds(0, wide)]),
    ]
    red.line(IN, 3)
    copies.wait(first_sum)
    step.second_norm_back()
    weight_loads = [load_square(2, s.in_tile.at[0])]
    red.plane(OUT, 0, n_img)
    for n in range(3):
        red.free_partner(n)
    red.line(OUT, 3)
    red.await_partner(0)
    ckv_given = give_ckv()
    square_grad(s.normed2, s.grad_query, 1)
    normed1 = copies.start(hbm.normed1, s.normed2)
    cross_given = give_stacked(CROSS, s.stage_cross, 0)
    red.line(IN, 2)
    copies.wait(sout_load)
    s.weights = (None,) * 3 + (s.in_tile.at[1],)
    step.self_grad()
    copies.wait(*qkv_loads)
    red.await_partner(1)
    red.given(ckv_given)
    weight_loads += [load_square(n, s.out_tile.at[n]) for n in range(2)]
    for i in every:
        red.second(CKV, i, 1)
    red.given(cross_given)
    red.second(CROSS, 0, n_img)
    dx(3, 3)
    dx(2, 4)
    step.self_attention(0, 2)
    red.line(OUT, 2)
    red.line(IN, 1)
    dx(1, 4)
    step.self_attention(2, 4)
    red.await_partner(2)
    for i in every:
        red.first(CKV, i, 1)
    red.line(OUT, 1)
    dx(3, 4)
    step.self_attention(4, 6)
    red.first(CROSS, 0, n_img)
    red.last(IN, outs.s_in)
    red.last(OUT, outs.s_out)
    red.free_line()
    dx(2, 5)
    step.self_attention(6, 8)
    dx(1, 5)
    copies.wait(self_mixed, normed1, tokens)
    s.self_mixed, s.normed1, s.tokens = s.mixed, s.normed2, s.query
    square_grad(s.self_mixed, s.low, None)
    self_weights(0)
    red.settle(IN)
    self_given = give_stacked(SELF, s.stage_self, 0)
    red.given(self_given)
    self_weights(1)
    self_given2 = give_stacked(SELF, s.stage_self, 2)
    red.second(SELF, 0, 2)
    for i in every:
        red.plane(CKV, i, 1)
    red.given(self_given2)
    red.second(SELF, 2, 2)
    red.await_line()
    red.line(CKV, 3)
    dx(3, 5)
    dx(2, 6)
    copies.wait(*weight_loads)
    step.first_norm_back((s.out_tile.at[0], s.out_tile.at[1], s.in_tile.at[0]))
    copies.start(s.low, outs.token_grads)
    red.plane(CROSS, 0, n_img)
    red.line(CROSS, 3)
    vec_given = give_vec()
    red.line(CKV, 2)
    red.first(SELF, 0, 2)
    red.given(vec_given)
    for i in every:
        red.second(VEC, i, 1)
    red.first(SELF, 2, 2)
    dx(1, 6)
    dx(3, 6)
    dx(2, 7)
    dx(1, 7)
    dx(3, 7)
    red.line(CROSS, 2)
    red.line(CKV, 1)
    for i in every:
        red.first(VEC, i, 1)
    red.line(CROSS, 1)
    red.plane(SELF, 0, 2)
    red.plane(SELF, 2, 2)
    for i in every:
        red.plane(VEC, i, 1)
    red.line(SELF, 3)
    red.line(VEC, 3)
    red.line(SELF, 2)
    red.line(VEC, 2)
    red.line(SELF, 1)
    red.line(VEC, 1)
    red.last(CKV, outs.s_ckv)
    red.last(CROSS, outs.s_cross)
    red.last(SELF, outs.s_self)
    red.last(VEC, outs.s_vec)
    copies.start(s.images_out.at[im], outs.image_out.at[im])
    for c in range(caps):
        for k in range(1, n_img):
            source = (im + n_img - k) % n_img
            block = outs.image_out.at[source, pl.ds(c, 1)]
            pltpu.make_async_remote_copy(
                block, block, dx_send.at[k, c], dx_recv.at[k, c], device_id=(dp, source), device_id_type=MESH
            ).wait_recv()
    red.sends.finish()
    copies.finish()


def back_pass(dims, counts, values):
    inputs, outputs, scratch = back_inputs(dims), back_outputs(dims), back_scratch(dims)
    n_img, caps = dims[1], dims[2]
    dma = pltpu.SemaphoreType.DMA
    any_spec, vmem_spec = pl.BlockSpec(memory_space=pl.ANY), pl.BlockSpec(memory_space=pltpu.VMEM)
    outs = pl.pallas_call(
        functools.partial(back_kernel, dims),
        out_shape=structs_of(outputs),
        in_specs=[pl.BlockSpec(memory_space=pltpu.SMEM)] + [any_spec] * len(inputs),
        out_specs=[any_spec] * 3 + [vmem_spec] * (len(outputs) - 3),
        scratch_shapes=[pltpu.VMEM(*shape) for shape in scratch.values()]
        + [buffer for these in back_buffers(dims) for buffer in these]
        + Reducer.semaphores(len(back_groups(dims)), n_img)
        + [
            pltpu.SemaphoreType.REGULAR((5,)),
            dma((48,)),
            dma((n_img, caps)),
            dma((n_img, caps)),
        ],
        compiler_params=pltpu.CompilerParams(
            collective_id=2, has_side_effects=True, vmem_limit_bytes=63 << 20
        ),
    )(counts, *[values[name] for name in inputs])
    return dict(zip(outputs, outs))


def exit_kernel(dims, *refs):
    n_dp, n_img, caps, depth, width, inner_dp, block_len = dims
    layer_in, token_in, image_in, s_out, s_in, s_cross, s_ckv, s_self, s_vec = refs[:9]
    layer_out, token_grads, image_out, qkv, sout, cq, ckv, cout, w_in, w_out, gains, shifts, bias = refs[9:22]
    copies = Copies(refs[22])
    copies.start(image_in, image_out)
    copies.start(layer_in, layer_out)
    copies.start(token_in, token_grads)
    qkv[...] = s_self[:, 0 : 3 * width]
    sout[...] = s_self[:, 3 * width :]
    cq[...] = s_cross[:, width:]
    cout[...] = s_cross[:, 0:width]
    ckv[...] = s_ckv[...]
    w_in[...] = s_in[...]
    w_out[...] = s_out[...].T
    gains[...] = s_vec[0:3, 0:depth]
    shifts[...] = s_vec[3:13, 0:depth]
    for j in range(inner_dp // LANES):
        bias[pl.ds(j * LANES, LANES)] = s_vec[13 + j]
    copies.finish()


def exit_pass(dims, values):
    n_dp, n_img, caps, depth, width, inner_dp, block_len = dims
    any_spec, vmem_spec = pl.BlockSpec(memory_space=pl.ANY), pl.BlockSpec(memory_space=pltpu.VMEM)
    outputs = back_outputs(dims)
    square = (depth, width)
    small = ((depth, 3 * width), square, square, (depth, 2 * width), square)
    small += (outputs["s_in"][0], (inner_dp, width), (3, depth), (10, depth), (inner_dp,))
    return pl.pallas_call(
        functools.partial(exit_kernel, dims),
        out_shape=structs_of(outputs)[:3] + [jax.ShapeDtypeStruct(shape, f32) for shape in small],
        in_specs=[any_spec] * 3 + [vmem_spec] * 6,
        out_specs=[any_spec] * 3 + [vmem_spec] * len(small),
        scratch_shapes=[pltpu.SemaphoreType.DMA((3,))],
        compiler_params=pltpu.CompilerParams(vmem_limit_bytes=16 << 20),
    )(*[values[name] for name in outputs])


def layer_norm(values, norm_gain, norm_shift):
    average = jnp.mean(values, axis=-1, keepdims=True)
    centred = values - average
    spread = jnp.mean(centred * centred, axis=-1, keepdims=True)
    return centred * lax.rsqrt(spread + norm_epsilon) * norm_gain + norm_shift


def matmul(left_op, right_op):
    return jnp.dot(left_op, right_op, preferred_element_type=f32)


def matmul_tleft(left_op, right_op):
    return lax.dot_general(
        left_op, right_op, (((0,), (0,)), ((), ())), preferred_element_type=f32
    )


def matmul_tright(left_op, right_op):
    return lax.dot_general(
        left_op, right_op, (((1,), (1,)), ((), ())), preferred_element_type=f32
    )


def column_sums(values):
    return jnp.sum(values.astype(f32), axis=0)


def to_heads(values, captions):
    return values.reshape(captions, -1, HEADS, HEAD)


def probabilities(queries, key_heads, allowed):
    scores = jnp.einsum("cqhd,ckhd->chqk", queries, key_heads, preferred_element_type=f32)
    scores = jnp.where(allowed, scores * HEAD ** (-0.5), masked_value)
    return jax.nn.softmax(scores, axis=-1)


def attention(queries, key_heads, value_heads, allowed):
    probs = probabilities(queries, key_heads, allowed).astype(bf16)
    return jnp.einsum("chqk,ckhd->cqhd", probs, value_heads, preferred_element_type=f32)


def attention_backward(queries, key_heads, value_heads, allowed, grad_mixed):
    probs = probabilities(queries, key_heads, allowed)
    grad_probs = jnp.einsum("cqhd,ckhd->chqk", grad_mixed, value_heads, preferred_element_type=f32)
    inner_term = jnp.sum(probs * grad_probs, axis=-1, keepdims=True)
    grad_scores = (probs * (grad_probs - inner_term)).astype(bf16)
    score_scale = HEAD ** (-0.5)
    grad_queries = (
        jnp.einsum("chqk,ckhd->cqhd", grad_scores, key_heads, preferred_element_type=f32)
        * score_scale
    )
    grad_keys = (
        jnp.einsum("chqk,cqhd->ckhd", grad_scores, queries, preferred_element_type=f32)
        * score_scale
    )
    grad_values = jnp.einsum(
        "chqk,cqhd->ckhd", probs.astype(bf16), grad_mixed, preferred_element_type=f32
    )
    return grad_queries.astype(bf16), grad_keys.astype(bf16), grad_values.astype(bf16)


def local_direct(
    n_dp,
    n_img,
    tokens,
    image_tokens,
    counts,
    mixed,
    cross_kv,
    mlp_in,
    mlp_out,
    norm_gains,
    shifts,
    mlp_bias,
    cotangent,
):
    captions = tokens.shape[0]
    depth = mixed.shape[0]
    width = mlp_out.shape[1]
    inner_dp = mlp_out.shape[0]
    rows_all = captions * SEQ
    dims = (n_dp, n_img, captions, depth, width, inner_dp, image_tokens.shape[1])
    narrow = jnp.pad(jnp.concatenate([norm_gains, shifts]), ((0, 0), (0, LANES - depth)))
    vectors = jnp.concatenate([narrow, mlp_bias.reshape(-1, LANES)])
    token_rows = tokens.reshape(rows_all, MODEL_WIDTH)
    values = entry_pass(
        dims, counts, (vectors, cross_kv, mixed, mlp_in, mlp_out.T), image_tokens, token_rows
    )
    values.update(cot=cotangent.reshape(rows_all, MODEL_WIDTH), tokens=token_rows)
    values.update(qkv=values.pop("qkv").reshape(captions, SEQ, 3 * MODEL_WIDTH))
    results = exit_pass(dims, back_pass(dims, counts, values))
    return tuple(
        value.reshape(like.shape) for value, like in zip(results, (tokens, tokens, image_tokens))
    ) + tuple(results[3:])


def local(
    n_dp,
    n_img,
    tokens,
    image_tokens,
    token_counts,
    self_qkv,
    self_out,
    cross_q,
    cross_kv,
    cross_out,
    mlp_in,
    mlp_out,
    norm_gains,
    shifts,
    mlp_bias,
    cotangent,
):
    captions = tokens.shape[0]
    rows_all = captions * SEQ
    block_len = image_tokens.shape[1]
    width = self_out.shape[1]
    depth = self_out.shape[0]
    inner_dp = mlp_out.shape[0]
    direct = n_dp == 8 and depth % 16 == 0 and captions * n_img == image_tokens.shape[0]
    counts = lax.dynamic_slice_in_dim(token_counts, lax.axis_index("img") * captions, captions)

    mixed = jnp.concatenate([self_qkv, self_out, cross_q, cross_out], axis=1)
    if direct:
        return local_direct(
            n_dp,
            n_img,
            tokens,
            image_tokens,
            counts,
            mixed,
            cross_kv,
            mlp_in,
            mlp_out,
            norm_gains,
            shifts,
            mlp_bias,
            cotangent,
        )
    vectors = jnp.concatenate([norm_gains.reshape(-1), shifts.reshape(-1), mlp_bias])

    def everything(block, first, then, axes):
        return lax.all_gather(
            lax.all_gather(block, first, axis=axes[0], tiled=True), then, axis=axes[1], tiled=True
        )

    mixed_full = lax.all_gather(
        lax.all_gather(mixed, "dp", axis=0, tiled=True), "img", axis=0, tiled=False
    )
    ckv_w = everything(cross_kv, "img", "dp", (1, 0))
    in_w = everything(mlp_in, "img", "dp", (1, 0))
    outm_t = everything(mlp_out, "img", "dp", (1, 0)).T
    vec_full = lax.all_gather(vectors, "dp", axis=0, tiled=False)
    image_own = lax.all_to_all(
        image_tokens.reshape((n_img, captions) + image_tokens.shape[1:]), "img", 0, 0, tiled=True
    )

    def columns(start, size):
        return (
            mixed_full[:, :, start * width : (start + size) * width]
            .transpose(1, 0, 2)
            .reshape(MODEL_WIDTH, size * MODEL_WIDTH)
        )

    qkv_w, sout_w, cq_w, cout_w = columns(0, 3), columns(3, 1), columns(4, 1), columns(5, 1)
    gain_rows = vec_full[:, : 3 * depth].reshape(n_dp, 3, depth).transpose(1, 0, 2).reshape(3, -1)
    shift_rows = (
        vec_full[:, 3 * depth : 13 * depth]
        .reshape(n_dp, 10, depth)
        .transpose(1, 0, 2)
        .reshape(10, -1)
    )
    inner_bias = vec_full[:, 13 * depth :].reshape(-1)

    zero_row = jnp.zeros((MODEL_WIDTH,), f32)
    rows = tokens.reshape(rows_all, MODEL_WIDTH).astype(f32)
    normed1 = layer_norm(rows, gain_rows[0], shift_rows[0]).astype(bf16)
    mixed_qkv = (
        matmul(normed1, qkv_w) + jnp.concatenate([shift_rows[3], zero_row, shift_rows[4]])
    ).astype(bf16)
    self_queries, self_keys, self_values = [
        to_heads(mixed_qkv[:, n * MODEL_WIDTH : (n + 1) * MODEL_WIDTH], captions) for n in range(3)
    ]
    places = jnp.arange(SEQ, dtype=jnp.int32)
    causal = (places[None, :] <= places[:, None])[None, None]
    self_mixed = attention(self_queries, self_keys, self_values, causal)
    self_mixed = self_mixed.reshape(rows_all, MODEL_WIDTH).astype(bf16)
    first_sum = rows + matmul(self_mixed, sout_w) + shift_rows[5]
    normed2 = layer_norm(first_sum, gain_rows[1], shift_rows[1]).astype(bf16)
    cross_query = (matmul(normed2, cq_w) + shift_rows[6]).astype(bf16)
    cross_queries = to_heads(cross_query, captions)

    image_len = n_img * block_len
    image_rows = image_own.reshape(n_img * captions * block_len, MODEL_WIDTH)
    image_kv = (matmul(image_rows, ckv_w) + jnp.concatenate([zero_row, shift_rows[7]])).astype(bf16)

    def by_caption(values):
        return (
            values.reshape(n_img, captions, block_len, HEADS, HEAD)
            .transpose(1, 0, 2, 3, 4)
            .reshape(captions, image_len, HEADS, HEAD)
        )

    def by_place(values):
        return (
            values.reshape(captions, n_img, block_len, MODEL_WIDTH)
            .transpose(1, 0, 2, 3)
            .reshape(-1, MODEL_WIDTH)
        )

    cross_keys = by_caption(image_kv[:, :MODEL_WIDTH])
    cross_values = by_caption(image_kv[:, MODEL_WIDTH:])
    valid = (jnp.arange(image_len, dtype=jnp.int32)[None, :] < counts[:, None])[:, None, None, :]
    cross_mixed = attention(cross_queries, cross_keys, cross_values, valid)
    cross_mixed = cross_mixed.reshape(rows_all, MODEL_WIDTH).astype(bf16)
    second_sum = first_sum + matmul(cross_mixed, cout_w) + shift_rows[8]
    normed3 = layer_norm(second_sum, gain_rows[2], shift_rows[2]).astype(bf16)
    hidden = matmul(normed3, in_w) + inner_bias
    activated = jax.nn.gelu(hidden, approximate=False).astype(bf16)
    result = second_sum + matmul_tright(activated, outm_t) + shift_rows[9]
    layer_out = result.reshape(tokens.shape).astype(bf16)

    grad_low3 = cotangent.reshape(rows_all, MODEL_WIDTH)
    g_outm_t = matmul_tleft(grad_low3, activated)
    g_shift9 = column_sums(grad_low3)
    grad_act = matmul(grad_low3, outm_t)
    _, gelu_pull = jax.vjp(lambda pre_act: jax.nn.gelu(pre_act, approximate=False), hidden)
    grad_hidden = gelu_pull(grad_act)[0].astype(bf16)
    g_in = matmul_tleft(normed3, grad_hidden)
    g_inner_bias = column_sums(grad_hidden)
    grad_normed3 = matmul_tright(grad_hidden, in_w)
    _, norm_pull3 = jax.vjp(layer_norm, second_sum, gain_rows[2], shift_rows[2])
    grad_second_ln, g_gain2, g_shift2 = norm_pull3(grad_normed3)
    grad_second = grad_low3.astype(f32) + grad_second_ln
    grad_low2 = grad_second.astype(bf16)
    g_cout = matmul_tleft(cross_mixed, grad_low2)
    g_shift8 = column_sums(grad_low2)
    grad_cross_mixed = to_heads(matmul_tright(grad_low2, cout_w).astype(bf16), captions)
    grad_query, grad_ckeys, grad_cvalues = attention_backward(
        cross_queries, cross_keys, cross_values, valid, grad_cross_mixed
    )
    grad_query = grad_query.reshape(rows_all, MODEL_WIDTH)
    g_cq = matmul_tleft(normed2, grad_query)
    g_shift6 = column_sums(grad_query)
    grad_normed2 = matmul_tright(grad_query, cq_w)
    grad_value_rows = by_place(grad_cvalues)
    grad_image_kv = jnp.concatenate([by_place(grad_ckeys), grad_value_rows], axis=1)
    g_ckv = matmul_tleft(image_rows, grad_image_kv)
    g_shift7 = column_sums(grad_value_rows)
    image_grads = matmul_tright(grad_image_kv, ckv_w).astype(bf16).reshape(image_own.shape)
    _, norm_pull2 = jax.vjp(layer_norm, first_sum, gain_rows[1], shift_rows[1])
    grad_first_ln, g_gain1, g_shift1 = norm_pull2(grad_normed2)
    grad_first = grad_second + grad_first_ln
    grad_low1 = grad_first.astype(bf16)
    g_sout = matmul_tleft(self_mixed, grad_low1)
    g_shift5 = column_sums(grad_low1)
    grad_self_mixed = to_heads(matmul_tright(grad_low1, sout_w).astype(bf16), captions)
    grad_qkv = jnp.concatenate(
        [
            part.reshape(rows_all, MODEL_WIDTH)
            for part in attention_backward(
                self_queries, self_keys, self_values, causal, grad_self_mixed
            )
        ],
        axis=1,
    )
    g_qkv = matmul_tleft(normed1, grad_qkv)
    qkv_sums = column_sums(grad_qkv)
    g_shift3, g_shift4 = qkv_sums[:MODEL_WIDTH], qkv_sums[2 * MODEL_WIDTH :]
    grad_normed1 = matmul_tright(grad_qkv, qkv_w)
    _, norm_pull1 = jax.vjp(layer_norm, rows, gain_rows[0], shift_rows[0])
    grad_rows_ln, g_gain0, g_shift0 = norm_pull1(grad_normed1)
    token_grads = (grad_first + grad_rows_ln).reshape(tokens.shape).astype(bf16)
    g_vector_rows = jnp.stack(
        [
            g_gain0,
            g_gain1,
            g_gain2,
            g_shift0,
            g_shift1,
            g_shift2,
            g_shift3,
            g_shift4,
            g_shift5,
            g_shift6,
            g_shift7,
            g_shift8,
            g_shift9,
        ]
    )

    def scattered(grad):
        tall = lax.psum_scatter(grad, "dp", scatter_dimension=0, tiled=True)
        return lax.psum_scatter(tall, "img", scatter_dimension=1, tiled=True)

    s_qkv, s_sout, s_cq, s_ckv, s_cout, s_in, s_outm = [
        scattered(g) for g in (g_qkv, g_sout, g_cq, g_ckv, g_cout, g_in, g_outm_t.T)
    ]
    s_rows, s_inner = lax.psum(
        (
            lax.psum_scatter(g_vector_rows, "dp", scatter_dimension=1, tiled=True),
            lax.psum_scatter(g_inner_bias, "dp", scatter_dimension=0, tiled=True),
        ),
        "img",
    )
    image_out = lax.all_to_all(image_grads, "img", 0, 0, tiled=True).reshape(image_tokens.shape)
    return (
        layer_out,
        token_grads,
        image_out,
        s_qkv,
        s_sout,
        s_cq,
        s_ckv,
        s_cout,
        s_in,
        s_outm,
        s_rows[:3],
        s_rows[3:],
        s_inner,
    )


def solution(mesh):
    caption_rows = P(("dp", "img"), None, None)
    weight = P("dp", "img")
    vector = P(None, "dp")
    in_specs = (caption_rows, P("dp", "img", None), P("dp")) + (weight,) * 7
    in_specs += (vector, vector, P("dp"), caption_rows)
    out_specs = (caption_rows, caption_rows, P("dp", "img", None)) + (weight,) * 7
    out_specs += (vector, vector, P("dp"))
    return jax.shard_map(
        functools.partial(local, mesh.shape["dp"], mesh.shape["img"]),
        mesh=mesh,
        in_specs=in_specs,
        out_specs=out_specs,
        check_vma=False,
    )
```

```python
import functools
from types import SimpleNamespace

import jax
import jax.numpy as jnp
from jax import lax
from jax.experimental import pallas as pl
from jax.experimental.pallas import tpu as pltpu
from jax.sharding import PartitionSpec as P

MODEL_WIDTH = 768
HEADS = 12
HEAD = 64
SEQ = 64
VEC_ROWS = 16
LANES = 128
MESH = pl.DeviceIdType.MESH
bf16 = jnp.bfloat16
f32 = jnp.float32

masked_value = -1e30
norm_epsilon = 1e-05


def tile_ds(index, size, unit):
    return pl.ds(pl.multiple_of(index * size, unit), size)


def stacked_block(rows, cols):
    return lambda ref, d, i: ref.at[i, tile_ds(d, rows, 16), :]


def grid_block(rows, cols):
    return lambda ref, d, i: ref.at[tile_ds(d, rows, 16), tile_ds(i, cols, LANES)]


def turned_block(rows, cols):
    return lambda ref, d, i: ref.at[tile_ds(i, rows, 16), tile_ds(d, cols, LANES)]


def repeated_block(rows, cols):
    return lambda ref, d, i: ref.at[tile_ds(d, rows, 8), :]


class Group:
    def __init__(self, rows, cols, dtype, full, block):
        self.rows, self.cols, self.dtype, self.full = rows, cols, dtype, full
        self.block = block(rows, cols)


def flip(d, bit):
    return d + bit * (1 - 2 * ((d // bit) % 2))


class Place:
    def __init__(self, n_img):
        self.n_img = n_img
        self.dp, self.im = lax.axis_index("dp"), lax.axis_index("img")
        self.core = self.dp % 2
        self.sib = flip(self.dp, 1)

    def first(self, d):
        return flip(d, 2) * (1 - self.core) + flip(d, 4) * self.core

    def second(self, d):
        return flip(d, 4) * (1 - self.core) + flip(d, 2) * self.core

    def near(self, k):
        value = jnp.int32(0)
        for at in range(self.n_img):
            order = sorted(range(self.n_img), key=lambda other: (abs(other - at), other))
            value = jnp.where(self.im == at, order[k], value)
        return value

    def barrier(self):
        semaphore = pltpu.get_barrier_semaphore()
        peers = [(self.sib, self.im), (self.first(self.dp), self.im), (self.second(self.dp), self.im)]
        peers += [(self.dp, (self.im + k) % self.n_img) for k in range(1, self.n_img)]
        for peer in peers:
            pl.semaphore_signal(semaphore, inc=1, device_id=peer, device_id_type=MESH)
        pl.semaphore_wait(semaphore, len(peers))


class Sends:
    def __init__(self):
        self.started = []

    def send(self, src, dst, send_sem, recv_sem, device, when=None):
        copy = pltpu.make_async_remote_copy(
            src, dst, send_sem, recv_sem, device_id=device, device_id_type=MESH
        )
        entry = (when, copy)
        self.started.append(entry)
        if when is None:
            copy.start()
        else:
            pl.when(when)(copy.start)
        return entry

    def send_copy(self, copy):
        self.started.append((None, copy))
        copy.start()

    def wait(self, *entries):
        for entry in entries:
            self.started = [other for other in self.started if other is not entry]
            when, copy = entry
            if when is None:
                copy.wait_send()
            else:
                pl.when(when)(copy.wait_send)

    def finish(self):
        self.wait(*self.started)


def dot(left, right):
    return jnp.dot(left, right, preferred_element_type=f32)


def dot_left(left, right):
    return lax.dot_general(left, right, (((0,), (0,)), ((), ())), preferred_element_type=f32)


def dot_right(left, right):
    return lax.dot_general(left, right, (((1,), (1,)), ((), ())), preferred_element_type=f32)


def for_rows(count, size, body):
    def step(r, carry):
        body(pl.ds(pl.multiple_of(r * size, size), size))
        return carry

    lax.fori_loop(0, count // size, step, 0)


def standard(values):
    average = jnp.mean(values, axis=-1, keepdims=True)
    centred = values - average
    spread = jnp.mean(centred * centred, axis=-1, keepdims=True)
    rate = lax.rsqrt(spread + norm_epsilon)
    return centred * rate, rate


def add_into(dst, src):
    dst[...] = (dst[...].astype(f32) + src[...].astype(f32)).astype(dst.dtype)


def norm_rows(out, values, gain, shift):
    def body(part):
        unit, _ = standard(values[part, :].astype(f32))
        out[part, :] = (unit * gain + shift).astype(bf16)

    for_rows(out.shape[0], 64, body)


def norm_rows_back(grad, values, gain, add, out, sums, low, gain_row, shift_row, low_row):
    zero = jnp.zeros((1, MODEL_WIDTH), f32)
    sums[gain_row : gain_row + 1, :] = zero
    sums[shift_row : shift_row + 1, :] = zero
    if low_row is not None:
        sums[low_row : low_row + 1, :] = zero

    def body(part):
        unit, rate = standard(values[part, :].astype(f32))
        grad_part = grad[part, :]
        scaled = grad_part * gain
        inner = jnp.mean(scaled, axis=-1, keepdims=True)
        along = jnp.mean(scaled * unit, axis=-1, keepdims=True)
        total = add[part, :].astype(f32) + rate * (scaled - inner - unit * along)
        rounded = total.astype(bf16)
        if out is not None:
            out[part, :] = total
        low[part, :] = rounded
        sums[gain_row : gain_row + 1, :] += jnp.sum(grad_part * unit, axis=0, keepdims=True)
        sums[shift_row : shift_row + 1, :] += jnp.sum(grad_part, axis=0, keepdims=True)
        if low_row is not None:
            sums[low_row : low_row + 1, :] += jnp.sum(rounded.astype(f32), axis=0, keepdims=True)

    for_rows(grad.shape[0], 64, body)


QUAD = 4 * HEAD


def head_mask():
    lane_head = lax.broadcasted_iota(jnp.int32, (4, SEQ, QUAD), 2) // HEAD
    return lane_head == lax.broadcasted_iota(jnp.int32, (4, SEQ, QUAD), 0)


def by_head(values, mask):
    return jnp.where(mask, values.astype(f32)[None], 0.0).reshape(4 * SEQ, QUAD).astype(bf16)


def from_head(values, mask):
    return jnp.sum(jnp.where(mask, values.reshape(4, SEQ, QUAD), 0.0), axis=0)


def weights_of(queries, keys, allowed):
    scores = jnp.where(allowed, dot_right(keys, queries) * HEAD ** (-0.5), masked_value)
    weights = jnp.exp(scores - jnp.max(scores, axis=0, keepdims=True))
    return weights * (1.0 / jnp.sum(weights, axis=0, keepdims=True))


def attend(query, keys, values, allowed, mask):
    probs = weights_of(by_head(query, mask), keys, allowed).astype(bf16)
    return from_head(dot_left(probs, values), mask).astype(bf16)


def attend_back(query, keys, values, allowed, mask, grad_mixed):
    queries, grads = by_head(query, mask), by_head(grad_mixed, mask)
    probs = weights_of(queries, keys, allowed)
    grad_probs = dot_right(values, grads)
    inner = jnp.sum(probs * grad_probs, axis=0, keepdims=True)
    grad_scores = (probs * (grad_probs - inner)).astype(bf16)
    scale = HEAD ** (-0.5)
    return (
        (from_head(dot_left(grad_scores, keys), mask) * scale).astype(bf16),
        (dot(grad_scores, queries) * scale).astype(bf16),
        dot(probs.astype(bf16), grads).astype(bf16),
    )


def causal_mask():
    shape = (SEQ, 4 * SEQ)
    query = lax.broadcasted_iota(jnp.int32, shape, 1) % SEQ
    return lax.broadcasted_iota(jnp.int32, shape, 0) <= query


def unpack_vectors(blocks, vec, bias, n_dp, depth, inner_dp):
    for d in range(n_dp):
        row = d * VEC_ROWS
        vec[0:13, d * depth : (d + 1) * depth] = blocks[row : row + 13, 0:depth]
        for j in range(inner_dp // LANES):
            at, col = divmod(d * inner_dp + j * LANES, bias.shape[1])
            bias[at : at + 1, col : col + LANES] = blocks[row + 13 + j : row + 14 + j, :]


def pack_vectors(vec, bias, blocks, n_dp, depth, inner_dp):
    blocks[...] = jnp.zeros_like(blocks)
    for d in range(n_dp):
        row = d * VEC_ROWS
        blocks[row : row + 13, 0:depth] = vec[0:13, d * depth : (d + 1) * depth]
        for j in range(inner_dp // LANES):
            at, col = divmod(d * inner_dp + j * LANES, bias.shape[1])
            blocks[row + 13 + j : row + 14 + j, :] = bias[at : at + 1, col : col + LANES]


class Copies:
    def __init__(self, semaphores):
        self.semaphores, self.used, self.open = semaphores, 0, []

    def start(self, src, dst):
        copy = pltpu.make_async_copy(src, dst, self.semaphores.at[self.used])
        self.used += 1
        copy.start()
        self.open.append(copy)
        return copy

    def wait(self, *copies):
        for copy in copies:
            self.open = [other for other in self.open if other is not copy]
            copy.wait()

    def finish(self):
        self.wait(*self.open)


def kept_shapes(dims):
    n_dp, n_img, caps, depth, width, inner_dp, block_len = dims
    rows, wide, inner = caps * SEQ, MODEL_WIDTH, n_dp * inner_dp
    low, high = ((rows, wide), bf16), ((rows, wide), f32)
    return dict(
        weights=((wide, 6 * wide), bf16),
        normed1=low,
        qkv=((rows, 3 * wide), bf16),
        self_mixed=low,
        first_sum=high,
        normed2=low,
        query=low,
        kv=((n_img, caps, block_len, 2 * wide), bf16),
        mixed=low,
        second_sum=high,
        vec=((16, wide), f32),
        bias=((n_img, inner // n_img), f32),
        images=((n_img, caps, block_len, wide), bf16),
        ckv=((wide, 2 * wide), bf16),
    )


class Forward:
    def __init__(self, dims, counts, raw, tokens, kept):
        self.n_img, self.width = dims[1], dims[4]
        self.counts, self.raw, self.tokens, self.kept = counts, raw, tokens, kept

    def gain(self, k):
        return self.kept.vec[k : k + 1, :]

    def shift(self, k):
        return self.kept.vec[3 + k : 4 + k, :]

    def first_norm(self):
        norm_rows(self.kept.normed1, self.tokens, self.gain(0), self.shift(0))

    def assemble(self, i):
        weights, w, wide = self.kept.weights, self.width, MODEL_WIDTH
        weights[:, i * 3 * w : (i + 1) * 3 * w] = self.raw[i, :, 0 : 3 * w]
        for n in range(3):
            at = (3 + n) * wide + i * w
            weights[:, at : at + w] = self.raw[i, :, (3 + n) * w : (4 + n) * w]

    def image_kv(self, start, stop):
        wide, kv, images = MODEL_WIDTH, self.kept.kv, self.kept.images
        block = images[:, start:stop].reshape(-1, wide)
        for n in range(2):
            value = dot(block, self.kept.ckv[:, n * wide : (n + 1) * wide])
            if n == 1:
                value = value + self.shift(7)
            kv[:, start:stop, :, n * wide : (n + 1) * wide] = value.astype(bf16).reshape(
                images.shape[0], stop - start, images.shape[2], wide
            )

    def project(self):
        wide, qkv = MODEL_WIDTH, self.kept.qkv
        for n, shift in enumerate((3, None, 4)):
            value = dot(self.kept.normed1[...], self.kept.weights[:, n * wide : (n + 1) * wide])
            if shift is not None:
                value = value + self.shift(shift)
            qkv[:, n * wide : (n + 1) * wide] = value.astype(bf16)

    def self_attention(self, start, stop):
        qkv, out, wide = self.kept.qkv, self.kept.self_mixed, MODEL_WIDTH
        allowed, mask = causal_mask(), head_mask()

        def caption(c, carry):
            part = pl.ds(pl.multiple_of(c * SEQ, SEQ), SEQ)
            for t in range(wide // QUAD):
                at = t * QUAD
                out[part, at : at + QUAD] = attend(
                    qkv[part, at : at + QUAD],
                    qkv[part, wide + at : wide + at + QUAD],
                    qkv[part, 2 * wide + at : 2 * wide + at + QUAD],
                    allowed,
                    mask,
                )
            return carry

        lax.fori_loop(start, stop, caption, 0, unroll=True)

    def add_product(self, left, n, shift, base, out):
        wide = MODEL_WIDTH
        out[...] = dot(left[...], self.kept.weights[:, n * wide : (n + 1) * wide])
        row = self.shift(shift)

        def body(part):
            out[part, :] = base[part, :].astype(f32) + (out[part, :] + row)

        for_rows(out.shape[0], 64, body)

    def first_residual(self):
        wide = MODEL_WIDTH
        self.add_product(self.kept.self_mixed, 3, 5, self.tokens, self.kept.first_sum)
        norm_rows(self.kept.normed2, self.kept.first_sum, self.gain(1), self.shift(1))
        value = dot(self.kept.normed2[...], self.kept.weights[:, 4 * wide : 5 * wide])
        self.kept.query[...] = (value + self.shift(6)).astype(bf16)

    def valid_keys(self, c):
        shape = (self.n_img * self.kept.kv.shape[2], 4 * SEQ)
        return lax.broadcasted_iota(jnp.int32, shape, 0) < self.counts[c]

    def cross_attention(self, start, stop):
        query, kv, out, wide = self.kept.query, self.kept.kv, self.kept.mixed, MODEL_WIDTH
        mask = head_mask()
        length = self.n_img * kv.shape[2]

        def caption(c, carry):
            part = pl.ds(pl.multiple_of(c * SEQ, SEQ), SEQ)
            allowed = self.valid_keys(c)
            for t in range(wide // QUAD):
                at = t * QUAD
                out[part, at : at + QUAD] = attend(
                    query[part, at : at + QUAD],
                    kv[:, c, :, at : at + QUAD].reshape(length, QUAD),
                    kv[:, c, :, wide + at : wide + at + QUAD].reshape(length, QUAD),
                    allowed,
                    mask,
                )
            return carry

        lax.fori_loop(start, stop, caption, 0, unroll=True)

    def second_residual(self):
        self.add_product(self.kept.mixed, 5, 8, self.kept.first_sum, self.kept.second_sum)


class Gatherer:
    def __init__(self, here, groups, own, full, send_sem, recv_sem):
        self.here, self.groups, self.own, self.full = here, groups, own, full
        self.send_sem, self.recv_sem = send_sem, recv_sem
        self.sends, self.used = Sends(), [0] * len(groups)

    def forward(self, g, d, i, src, device, when=None):
        self.sends.send(
            src,
            self.groups[g].block(self.full[g], d, i),
            self.send_sem.at[g, self.used[g]],
            self.recv_sem.at[g, d, i],
            device,
            when,
        )
        self.used[g] += 1

    def arrived(self, g, d, i):
        block, here = self.groups[g].block(self.full[g], d, i), self.here
        pltpu.make_async_remote_copy(
            block,
            block,
            self.send_sem.at[g, 0],
            self.recv_sem.at[g, d, i],
            device_id=(here.sib, here.im),
            device_id_type=MESH,
        ).wait_recv()
        return block

    def to_planes(self, g, d, i, block):
        here = self.here
        self.forward(g, d, i, block, (here.first(here.dp), here.im))
        self.forward(g, d, i, block, (here.second(here.dp), here.im))
        self.forward(g, d, i, block, (here.sib, here.im))

    def start(self, g):
        here = self.here
        dp, im = here.dp, here.im
        self.forward(g, dp, im, self.own[g], (dp, im + 1), im < here.n_img - 1)
        self.forward(g, dp, im, self.own[g], (dp, im - 1), im > 0)
        self.to_planes(g, dp, im, self.own[g])

    def line(self, g, k):
        here = self.here
        dp, im, i = here.dp, here.im, here.near(k)
        block = self.arrived(g, dp, i)
        after = im + jnp.where(i < im, 1, -1)
        self.forward(g, dp, i, block, (dp, after), (after >= 0) & (after < here.n_img))
        self.to_planes(g, dp, i, block)

    def first(self, g, k):
        here = self.here
        d, i = here.first(here.dp), here.near(k)
        block = self.arrived(g, d, i)
        self.forward(g, d, i, block, (here.second(here.dp), here.im))
        self.forward(g, d, i, block, (here.sib, here.im))

    def second(self, g, k):
        here = self.here
        i = here.near(k)
        for d in (here.second(here.dp), here.second(here.first(here.dp))):
            block = self.arrived(g, d, i)
            self.forward(g, d, i, block, (here.sib, here.im))

    def complete(self, g):
        for c in range(4):
            for i in range(self.here.n_img):
                self.arrived(g, 2 * c + 1 - self.here.core, i)


X_PARTS = 4
LAGS = (6, 12)
X_EVERY = 4


def entry_groups(dims):
    n_dp, n_img, caps, depth, width, inner_dp, block_len = dims
    wide, inner = MODEL_WIDTH, n_dp * inner_dp
    return [
        Group(VEC_ROWS, LANES, f32, (n_img, n_dp * VEC_ROWS, LANES), stacked_block),
        Group(depth, 2 * width, bf16, (wide, 2 * wide), grid_block),
        Group(depth, 6 * width, bf16, (n_img, wide, 6 * width), stacked_block),
        Group(depth, inner // n_img, bf16, (wide, inner), grid_block),
        Group(width, inner_dp, bf16, (wide, inner), turned_block),
    ]


def entry_kernel(dims, *refs):
    n_dp, n_img, caps, depth, width, inner_dp, block_len = dims
    groups, shapes = entry_groups(dims), kept_shapes(dims)
    count = len(groups)
    counts, own, (x_ref, tokens_hbm) = refs[0], refs[1 : 1 + count], refs[1 + count : 3 + count]
    refs = refs[3 + count :]
    outs, (in_w, out_t) = bag(shapes, refs), refs[len(shapes) : len(shapes) + 2]
    refs = refs[len(shapes) + 2 :]
    kept, refs = bag(shapes, refs), refs[len(shapes) :]
    vec_full, raw, tokens, send_sem, recv_sem, xs_sem, xr_sem, local_sem = refs
    here = Place(n_img)
    dp, im = here.dp, here.im
    copies = Copies(local_sem)
    full = (vec_full, kept.ckv, raw, in_w, out_t)
    gather = Gatherer(here, groups, own, full, send_sem, recv_sem)
    local_blocks = [
        copies.start(own[g], groups[g].block(full[g], dp, im)) for g in range(count)
    ]
    own_images = copies.start(x_ref.at[pl.ds(im * caps, caps)], kept.images.at[im])
    token_load = copies.start(tokens_hbm, tokens)
    here.barrier()
    for g in range(count):
        gather.start(g)
    part_caps = caps // X_PARTS

    def x_copy(k, p, target, source):
        return pltpu.make_async_remote_copy(
            x_ref.at[pl.ds(target * caps + p * part_caps, part_caps)],
            kept.images.at[source, pl.ds(p * part_caps, part_caps)],
            xs_sem.at[k, p],
            xr_sem.at[k, p],
            device_id=(dp, target),
            device_id_type=MESH,
        )

    waiting = [(k, p) for p in range(X_PARTS) for k in (*range(2, n_img), 1)][::-1]
    ticks = [0]

    def tick():
        ticks[0] += 1
        if ticks[0] % X_EVERY == 0 and waiting:
            k, p = waiting.pop()
            gather.sends.send_copy(x_copy(k, p, (im + k) % n_img, im))

    units = [(g, k) for g in range(count) for k in range(n_img)]

    def exchange(t):
        if t < len(units):
            g, k = units[t]
            if k > 0:
                gather.line(g, k)
                tick()
        if 0 <= t - LAGS[0] < len(units):
            gather.first(*units[t - LAGS[0]])
            tick()
        if 0 <= t - LAGS[1] < len(units):
            gather.second(*units[t - LAGS[1]])
            tick()

    def images_of(p):
        part = pl.ds(p * part_caps, part_caps)
        for k in range(1, n_img):
            source = (im + n_img - k) % n_img
            x_copy(k, p, source, source).wait_recv()
        copies.start(kept.images.at[:, part], outs.images.at[:, part])
        step.image_kv(p * part_caps, (p + 1) * part_caps)
        copies.start(kept.kv.at[:, part], outs.kv.at[:, part])

    step = Forward(dims, counts, raw, tokens, kept)
    done = LAGS[1] + n_img
    for t in range(len(units) + LAGS[1]):
        exchange(t)
        if t == done:
            gather.complete(0)
            copies.wait(local_blocks[0], token_load)
            unpack_vectors(vec_full.at[0], kept.vec, kept.bias, n_dp, depth, inner_dp)
            step.first_norm()
        if t == done + n_img:
            gather.complete(1)
            copies.wait(local_blocks[1], own_images)
            images_of(0)
        if t == done + n_img + 2:
            images_of(1)
        if t == done + 2 * n_img:
            gather.complete(2)
            copies.wait(local_blocks[2])
            for i in range(n_img):
                step.assemble(i)
            step.project()
        if t == done + 2 * n_img + 1:
            step.self_attention(0, caps // 2)
        if t == done + 2 * n_img + 2:
            step.self_attention(caps // 2, caps)
        if t == done + 2 * n_img + 3:
            step.first_residual()
        if t == done + 2 * n_img + 4:
            step.cross_attention(0, part_caps)
        if t == done + 2 * n_img + 5:
            step.cross_attention(part_caps, 2 * part_caps)
    while waiting:
        k, p = waiting.pop()
        gather.sends.send_copy(x_copy(k, p, (im + k) % n_img, im))
    copies.start(kept.vec, outs.vec)
    copies.start(kept.bias, outs.bias)
    copies.start(kept.ckv, outs.ckv)
    copies.start(kept.weights, outs.weights)
    copies.start(kept.normed1, outs.normed1)
    copies.start(kept.qkv, outs.qkv)
    copies.start(kept.self_mixed, outs.self_mixed)
    copies.start(kept.first_sum, outs.first_sum)
    copies.start(kept.normed2, outs.normed2)
    copies.start(kept.query, outs.query)
    for p in range(2, X_PARTS):
        images_of(p)
        step.cross_attention(p * part_caps, (p + 1) * part_caps)
    copies.start(kept.mixed, outs.mixed)
    step.second_residual()
    copies.start(kept.second_sum, outs.second_sum)
    for g in range(3, count):
        gather.complete(g)
    gather.sends.finish()
    copies.finish()


def entry_pass(dims, counts, owns, image_tokens, tokens):
    n_dp, n_img, caps, depth, width, inner_dp, block_len = dims
    groups, shapes = entry_groups(dims), kept_shapes(dims)
    count = len(groups)
    dma = pltpu.SemaphoreType.DMA
    any_spec = pl.BlockSpec(memory_space=pl.ANY)
    outs = pl.pallas_call(
        functools.partial(entry_kernel, dims),
        out_shape=structs_of(shapes) + [jax.ShapeDtypeStruct(g.full, g.dtype) for g in groups[3:]],
        in_specs=[pl.BlockSpec(memory_space=pltpu.SMEM)] + [any_spec] * (count + 2),
        out_specs=[any_spec] * (len(shapes) + 2),
        scratch_shapes=[pltpu.VMEM(*shape) for shape in shapes.values()]
        + [pltpu.VMEM(groups[0].full, f32), pltpu.VMEM(groups[2].full, bf16), pltpu.VMEM(tokens.shape, bf16)]
        + [
            dma((count, 64)),
            dma((count, n_dp, n_img)),
            dma((n_img, X_PARTS)),
            dma((n_img, X_PARTS)),
            dma((48,)),
        ],
        compiler_params=pltpu.CompilerParams(
            collective_id=1, has_side_effects=True, vmem_limit_bytes=62 << 20
        ),
    )(counts, *owns, image_tokens, tokens)
    kept = dict(zip(shapes, outs))
    kept.update(in_w=outs[-2], out_t=outs[-1])
    return kept


class Backward:
    def __init__(self, dims, counts, refs):
        self.dims, self.counts, self.refs = dims, counts, refs

    def __getattr__(self, name):
        return getattr(self.refs, name)

    def gain(self, k):
        return self.vec[k : k + 1, :]

    def weight(self, n):
        return self.weights[n][...]

    def sum_row(self, k, values):
        self.sums[3 + k : 4 + k, :] = jnp.sum(values.astype(f32), axis=0, keepdims=True)

    def begin(self):
        wide = MODEL_WIDTH
        norm_rows(self.normed3, self.second_sum, self.gain(2), self.vec[5:6, :])
        self.sum_row(9, self.cot[...])
        self.turned[0:wide, :] = self.normed3[...].astype(f32).T.astype(bf16)
        self.turned[wide : 2 * wide, :] = self.cot[...].astype(f32).T.astype(bf16)
        row = self.vec[12:13, :]

        def body(part):
            self.result[part, :] = self.second_sum[part, :] + row
            self.grad[part, :] = jnp.zeros((64, wide), f32)

        for_rows(self.result.shape[0], 64, body)

    def feed_forward(self, bias, in_w, out_t):
        rows = self.normed3.shape[0]
        self.hidden[...] = dot(self.normed3[...], in_w[...])
        self.grad_act[...] = dot(self.cot[...], out_t[...])
        self.hidden_sums[...] = jnp.zeros_like(self.hidden_sums)

        def body(part):
            pre = self.hidden[part, :] + bias
            below = 0.5 * (1.0 + lax.erf(pre * 2**-0.5))
            self.activated[part, :] = (pre * below).astype(bf16)
            slope = below + pre * (jnp.exp(-0.5 * pre * pre) * (2 * jnp.pi) ** -0.5)
            grad = (self.grad_act[part, :] * slope).astype(bf16)
            self.grad_hidden[part, :] = grad
            self.hidden_sums[...] += jnp.sum(grad.astype(f32), axis=0, keepdims=True)

        for_rows(rows, 32, body)
        self.result[...] += dot_right(self.activated[...], out_t[...])
        self.grad[...] += dot_right(self.grad_hidden[...], in_w[...])

    def third_norm_back(self):
        norm_rows_back(
            self.grad, self.second_sum, self.gain(2), self.cot, self.grad_sum, self.sums, self.low, 2, 5, 11
        )

    def cross_grad(self):
        self.grad_mixed[...] = dot_right(self.low[...], self.weight(5)).astype(bf16)

    def cross_caption(self, c, kv, grad_kv):
        wide = MODEL_WIDTH
        n_img, block_len = kv.shape[:2]
        length = n_img * block_len
        part = pl.ds(pl.multiple_of(c * SEQ, SEQ), SEQ)
        allowed = lax.broadcasted_iota(jnp.int32, (length, 4 * SEQ), 0) < self.counts[c]
        mask = head_mask()
        for t in range(wide // QUAD):
            own, other = slice(t * QUAD, (t + 1) * QUAD), slice(wide + t * QUAD, wide + (t + 1) * QUAD)
            grad_query, grad_keys, grad_values = attend_back(
                self.query[part, own],
                kv[:, :, own].reshape(length, QUAD),
                kv[:, :, other].reshape(length, QUAD),
                allowed,
                mask,
                self.grad_mixed[part, own],
            )
            self.grad_query[part, own] = grad_query
            grad_kv[:, :, own] = grad_keys.reshape(n_img, block_len, QUAD)
            grad_kv[:, :, other] = grad_values.reshape(n_img, block_len, QUAD)
            self.sums[10:11, own] += jnp.sum(grad_values.astype(f32), axis=0, keepdims=True)

    def second_norm_back(self):
        self.sum_row(6, self.grad_query[...])
        self.grad[...] = dot_right(self.grad_query[...], self.weight(4))
        norm_rows_back(
            self.grad, self.first_sum, self.gain(1), self.grad_sum, self.grad_sum, self.sums, self.low, 1, 4, 8
        )

    def self_grad(self):
        self.grad_mixed[...] = dot_right(self.low[...], self.weight(3)).astype(bf16)

    def self_attention(self, start, stop):
        wide = MODEL_WIDTH
        allowed, mask = causal_mask(), head_mask()

        def caption(c, carry):
            part = pl.ds(pl.multiple_of(c * SEQ, SEQ), SEQ)
            for t in range(wide // QUAD):
                own, other = slice(t * QUAD, (t + 1) * QUAD), slice(wide + t * QUAD, wide + (t + 1) * QUAD)
                grads = attend_back(
                    self.kv[0, c, :, own],
                    self.kv[0, c, :, other],
                    self.kv[1, c, :, own],
                    allowed,
                    mask,
                    self.grad_mixed[part, own],
                )
                self.kv[2, c, :, own] = grads[0]
                self.kv[2, c, :, other] = grads[1]
                self.kv[3, c, :, own] = grads[2]
            return carry

        lax.fori_loop(start, stop, caption, 0, unroll=2)

    def grad_qkv(self, place, start, stop):
        rows = self.kv.shape[1] * SEQ
        return self.kv[2 + place, :, :, start:stop].reshape(rows, stop - start)

    def qkv_grads(self, pair, stage):
        wide, block = MODEL_WIDTH, 3 * MODEL_WIDTH // 4
        unit = self.normed1[...]
        if pair == 0:
            both = dot_left(unit, self.grad_qkv(0, 0, 2 * block)).astype(bf16)
            stage[0, :, 0:block] = both[:, 0:block]
            stage[1, :, 0:block] = both[:, block : 2 * block]
        else:
            keys = dot_left(unit, self.grad_qkv(0, 2 * block, 2 * wide)).astype(bf16)
            values = dot_left(unit, self.grad_qkv(1, 0, wide)).astype(bf16)
            cut = 3 * block - 2 * wide
            stage[0, :, 0 : 2 * wide - 2 * block] = keys
            stage[0, :, 2 * wide - 2 * block : block] = values[:, 0:cut]
            stage[1, :, 0:block] = values[:, cut:]

    def first_norm_back(self, weights):
        wide = MODEL_WIDTH
        parts = [self.grad_qkv(0, 0, wide), self.grad_qkv(0, wide, 2 * wide), self.grad_qkv(1, 0, wide)]
        self.sum_row(3, parts[0])
        self.sum_row(4, parts[2])
        self.grad[...] = dot_right(parts[0], weights[0][...])
        for part, weight in zip(parts[1:], weights[1:]):
            self.grad[...] += dot_right(part, weight[...])
        norm_rows_back(
            self.grad, self.tokens, self.gain(0), self.grad_sum, None, self.sums, self.low, 0, 3, None
        )


class Reducer:
    def __init__(self, here, groups, places, buffers, semaphores, credits):
        self.here, self.groups, self.places, self.n_img = here, groups, places, here.n_img
        self.acc, self.r0, self.r1, self.r2, self.zr = buffers
        (self.load_sem, self.s0, self.r0_sem, self.s1, self.r1_sem, self.s2, self.r2_sem, self.sz, self.rz) = semaphores
        self.credits = credits
        self.sends = Sends()
        self.sent = {}
        dp = here.dp
        self.chip = dp // 2
        self.chip1, self.chip2 = here.first(dp) // 2, here.second(dp) // 2
        self.chip12 = here.second(here.first(dp)) // 2

    @staticmethod
    def leads(n_img):
        return (4, n_img), (4, n_img), (2, n_img), (n_img,), (n_img + 1,)

    @staticmethod
    def semaphores(count, n_img):
        dma = pltpu.SemaphoreType.DMA
        sizes = [(4, n_img)] * 3 + [(2, n_img)] * 2 + [(n_img,)] * 3 + [(n_img + 1,)]
        return [dma((count,) + size) for size in sizes]

    def view(self, buffers, g, *index):
        own, shared, start = self.places[g]
        store = own if buffers is self.acc else shared
        return buffers[store].at[index + (pl.ds(start, self.groups[g].rows), slice(None))]

    def send(self, g, src, dst, send_sem, recv_sem, device, when=None):
        entry = self.sends.send(src, dst, send_sem, recv_sem, device, when)
        self.sent.setdefault(g, []).append(entry)
        return entry

    def settle(self, g):
        self.sends.wait(*self.sent.pop(g))

    def give_each(self, g, c, i, count, own, other):
        return [self.give(g, c, i + n, 1, own.at[pl.ds(n, 1)], other.at[pl.ds(n, 1)]) for n in range(count)]

    def give(self, g, c, i, count, own, other):
        here, part = self.here, pl.ds(i, count)
        copy = pltpu.make_async_copy(own, self.view(self.acc, g, c, part), self.load_sem.at[g, c, i])
        copy.start()
        sent = self.sends.send(
            other,
            self.view(self.r0, g, c, part),
            self.s0.at[g, c, i],
            self.r0_sem.at[g, c, i],
            (here.sib, here.im),
        )
        return copy, sent

    def given(self, pieces):
        for copy, sent in pieces:
            copy.wait()
            self.sends.wait(sent)

    def chips(self):
        return self.chip12, self.chip2, self.chip1, self.chip

    def arrived(self, buffer, semaphore):
        here = self.here
        pltpu.make_async_remote_copy(
            buffer, buffer, self.s0.at[0, 0, 0], semaphore, device_id=(here.sib, here.im), device_id_type=MESH
        ).wait_recv()

    def take(self, block, buffer, semaphore):
        self.arrived(buffer, semaphore)
        add_into(block, buffer)

    def pair(self, g, c, i, count):
        part = pl.ds(i, count)
        block = self.view(self.acc, g, c, part)
        self.take(block, self.view(self.r0, g, c, part), self.r0_sem.at[g, c, i])
        return block

    def second_send(self, g, j, c, i, count, when=None):
        here, part = self.here, pl.ds(i, count)
        self.send(
            g,
            self.view(self.acc, g, c, part),
            self.view(self.r1, g, j, part),
            self.s1.at[g, j, i],
            self.r1_sem.at[g, j, i],
            (here.second(here.dp), here.im),
            when,
        )

    def second(self, g, i, count):
        for j, c in ((1, self.chip12), (0, self.chip2)):
            for n in range(i, i + count):
                self.pair(g, c, n, 1)
                self.second_send(g, j, c, n, 1)

    def second_if(self, g, c):
        far = jnp.where(self.chip12 == c, 1, 0)
        when = (self.chip12 == c) | (self.chip2 == c)

        for i in range(self.n_img):

            @pl.when(when)
            def _():
                self.pair(g, c, i, 1)

            self.second_send(g, far, c, i, 1, when)

    def first(self, g, i, count):
        for n in range(i, i + count):
            self.first_one(g, n, 1)

    def first_one(self, g, i, count):
        here, part = self.here, pl.ds(i, count)
        block = self.pair(g, self.chip1, i, count)
        self.take(block, self.view(self.r1, g, 1, part), self.r1_sem.at[g, 1, i])
        self.send(
            g,
            block,
            self.view(self.r2, g, part),
            self.s2.at[g, i],
            self.r2_sem.at[g, i],
            (here.first(here.dp), here.im),
        )

    def plane(self, g, i, count):
        for n in range(i, i + count):
            self.plane_one(g, n, 1)

    def plane_one(self, g, i, count):
        part = pl.ds(i, count)
        block = self.pair(g, self.chip, i, count)
        self.take(block, self.view(self.r1, g, 0, part), self.r1_sem.at[g, 0, i])
        self.take(block, self.view(self.r2, g, part), self.r2_sem.at[g, i])

    def line(self, g, k):
        here, im, n_img = self.here, self.here.im, self.n_img
        i = here.near(k)
        block = self.view(self.acc, g, self.chip, i)
        down = jnp.where(i < im, 1, 0)

        @pl.when((im > 0) & (im < n_img - 1))
        def _():
            self.take(block, self.view(self.zr, g, i), self.rz.at[g, i])

        target = im + 1 - 2 * down
        slot = jnp.where((down == 1) & (i == target), n_img, i)
        self.send(
            g, block, self.view(self.zr, g, slot), self.sz.at[g, i], self.rz.at[g, slot], (here.dp, target)
        )

    def last(self, g, out):
        im, n_img = self.here.im, self.n_img
        out[...] = self.view(self.acc, g, self.chip, im)[...].astype(f32)
        for slot, has in ((im, im > 0), (n_img, im < n_img - 1)):

            @pl.when(has)
            def _():
                buffer = self.view(self.zr, g, slot)
                self.arrived(buffer, self.rz.at[g, slot])
                out[...] += buffer[...].astype(f32)

    def neighbours(self):
        here = self.here
        im = here.im
        return ((here.dp, im - 1), im > 0, 3), ((here.dp, im + 1), im < self.n_img - 1, 4)

    def free_partner(self, n):
        here = self.here
        partner = (here.sib, here.second(here.dp), here.first(here.dp))[n]
        pl.semaphore_signal(self.credits.at[n], inc=1, device_id=(partner, here.im), device_id_type=MESH)

    def await_partner(self, n):
        pl.semaphore_wait(self.credits.at[n], 1)

    def free_line(self):
        for device, has, n in self.neighbours():
            mine = 7 - n

            @pl.when(has)
            def _():
                pl.semaphore_signal(self.credits.at[mine], inc=1, device_id=device, device_id_type=MESH)

    def await_line(self):
        for device, has, n in self.neighbours():

            @pl.when(has)
            def _():
                pl.semaphore_wait(self.credits.at[n], 1)


def bag(shapes, refs):
    return SimpleNamespace(**dict(zip(shapes, refs)))


def structs_of(shapes):
    return [jax.ShapeDtypeStruct(*shape) for shape in shapes.values()]


def back_inputs(dims):
    n_dp, n_img, caps, depth, width, inner_dp, block_len = dims
    wide, rows, inner = MODEL_WIDTH, caps * SEQ, n_dp * inner_dp
    low, high = ((rows, wide), bf16), ((rows, wide), f32)
    return dict(
        vec=((16, wide), f32),
        bias=((n_img, inner // n_img), f32),
        second_sum=high,
        cot=low,
        mixed=low,
        query=low,
        kv=((n_img, caps, block_len, 2 * wide), bf16),
        images=((n_img, caps, block_len, wide), bf16),
        normed2=low,
        in_w=((wide, inner), bf16),
        out_t=((wide, inner), bf16),
        weights=((wide, 6 * wide), bf16),
        ckv=((wide, 2 * wide), bf16),
        first_sum=high,
        qkv=((caps, SEQ, 3 * wide), bf16),
        self_mixed=low,
        normed1=low,
        tokens=low,
    )


def back_outputs(dims):
    n_dp, n_img, caps, depth, width, inner_dp, block_len = dims
    wide, rows, inner = MODEL_WIDTH, caps * SEQ, n_dp * inner_dp
    return dict(
        layer_out=((rows, wide), bf16),
        token_grads=((rows, wide), bf16),
        image_out=((n_img, caps, block_len, wide), bf16),
        s_out=((width, inner_dp), f32),
        s_in=((depth, inner // n_img), f32),
        s_cross=((depth, 2 * width), f32),
        s_ckv=((depth, 2 * width), f32),
        s_self=((depth, 4 * width), f32),
        s_vec=((VEC_ROWS, LANES), f32),
    )


def back_scratch(dims):
    n_dp, n_img, caps, depth, width, inner_dp, block_len = dims
    wide, rows, inner = MODEL_WIDTH, caps * SEQ, n_dp * inner_dp
    tile = inner // n_img
    low, high = ((rows, wide), bf16), ((rows, wide), f32)
    return dict(
        vec=((16, wide), f32),
        bias=((n_img, tile), f32),
        sums=((16, wide), f32),
        bias_sums=((n_img, tile), f32),
        hidden_sums=((1, tile), f32),
        vectors=((1, n_dp * VEC_ROWS, LANES), f32),
        cot=low,
        second_sum=high,
        normed3=low,
        turned=((2 * wide, rows), bf16),
        result=high,
        grad=high,
        hidden=((rows, tile), f32),
        grad_act=((rows, tile), f32),
        activated=((rows, tile), bf16),
        grad_hidden=((rows, tile), bf16),
        in_tile=((2, wide, tile), bf16),
        out_tile=((2, wide, tile), bf16),
        stage_in=((1, wide, tile), bf16),
        stage_out=((n_img, width, tile), bf16),
        low=low,
        mixed=low,
        query=low,
        normed2=low,
        kv=((n_img, caps, block_len, 2 * wide), bf16),
        images=((n_img, caps, block_len, wide), bf16),
        images_out=((n_img, caps, block_len, wide), bf16),
        stage_cross=((n_img, wide, 2 * width), bf16),
        stage_self=((2, wide, 4 * width), bf16),
    )


OUT, IN, CROSS, CKV, SELF, VEC = range(6)
PLACES = ((0, 0, 0), (1, 1, 0), (2, 0, 0), (2, 0, 1), (1, 1, 0), (3, 2, 0))


def back_groups(dims):
    n_dp, n_img, caps, depth, width, inner_dp, block_len = dims
    wide, inner = MODEL_WIDTH, n_dp * inner_dp
    return [
        Group(width, inner_dp, bf16, (wide, inner), turned_block),
        Group(depth, inner // n_img, bf16, (wide, inner), grid_block),
        Group(depth, 2 * width, bf16, (n_img, wide, 2 * width), stacked_block),
        Group(depth, 2 * width, bf16, (wide, 2 * wide), grid_block),
        Group(depth, 4 * width, bf16, (n_img, wide, 4 * width), stacked_block),
        Group(VEC_ROWS, LANES, f32, (n_dp * VEC_ROWS, LANES), repeated_block),
    ]


def back_buffers(dims):
    groups = back_groups(dims)
    out, inside, vec = [(g.rows, g.cols, g.dtype) for g in (groups[OUT], groups[IN], groups[VEC])]
    stores = [[out, inside, out, vec]] + [[out, inside, vec]] * 4
    return [
        [pltpu.VMEM(lead + store[:2], store[2]) for store in these]
        for lead, these in zip(Reducer.leads(dims[1]), stores)
    ]


def back_kernel(dims, *refs):
    n_dp, n_img, caps, depth, width, inner_dp, block_len = dims
    wide, rows, inner = MODEL_WIDTH, caps * SEQ, n_dp * inner_dp
    tile = inner // n_img
    inputs, outputs, scratch = back_inputs(dims), back_outputs(dims), back_scratch(dims)
    counts, refs = refs[0], refs[1:]
    hbm, refs = bag(inputs, refs), refs[len(inputs) :]
    outs, refs = bag(outputs, refs), refs[len(outputs) :]
    s, refs = bag(scratch, refs), refs[len(scratch) :]
    groups = back_groups(dims)
    buffers = []
    for these in back_buffers(dims):
        buffers.append(refs[: len(these)])
        refs = refs[len(these) :]
    places = [(own, shared, start * depth) for own, shared, start in PLACES]
    here = Place(n_img)
    dp, im, core = here.dp, here.im, here.core
    red = Reducer(here, groups, places, buffers, refs[:9], refs[9])
    copies = Copies(refs[10])
    dx_send, dx_recv = refs[11:]
    every = range(n_img)
    names = list(inputs)

    def load(*wanted):
        return [copies.start(getattr(hbm, name), getattr(s, name)) for name in wanted]

    first_loads = load(*names[:4])

    def load_tile(t):
        cols = pl.ds(t * tile, tile)
        return [
            copies.start(hbm.in_w.at[:, cols], s.in_tile.at[t % 2]),
            copies.start(hbm.out_t.at[:, cols], s.out_tile.at[t % 2]),
        ]

    def load_square(n, dst):
        return copies.start(hbm.weights.at[:, pl.ds(n * wide, wide)], dst)

    tiles = [load_tile(0), load_tile(1)]
    middle_loads = load(*names[4:9])
    here.barrier()
    copies.wait(*first_loads)
    s.sums[...] = jnp.zeros_like(s.sums)
    step = Backward(dims, counts, s)
    step.begin()
    given = []
    own, other = tile_ds(core, inner_dp, LANES), tile_ds(1 - core, inner_dp, LANES)
    for t in every:
        copies.wait(*tiles[t])
        step.feed_forward(s.bias[t : t + 1, :], s.in_tile.at[t % 2], s.out_tile.at[t % 2])
        s.bias_sums[t : t + 1, :] = s.hidden_sums[...]
        if t + 2 < n_img:
            tiles.append(load_tile(t + 2))
        red.given(given)
        s.stage_in[0] = dot(s.turned[0:wide, :], s.grad_hidden[...]).astype(bf16)
        given = [
            red.give(
                IN,
                c,
                t,
                1,
                s.stage_in.at[:, tile_ds(2 * c + core, depth, 16), :],
                s.stage_in.at[:, tile_ds(2 * c + 1 - core, depth, 16), :],
            )
            for c in red.chips()
        ]
        value = dot(s.turned[wide : 2 * wide, :], s.activated[...]).astype(bf16)
        s.stage_out[...] = value.reshape(s.stage_out.shape)
        given.extend(red.give_each(OUT, t, 0, n_img, s.stage_out.at[:, :, own], s.stage_out.at[:, :, other]))
        if t >= 1:
            red.second(IN, t - 1, 1)
            red.second_if(OUT, t - 1)
        if t >= 2:
            red.first(IN, t - 2, 1)
    red.given(given)
    cross_loads = [load_square(4 + n, s.in_tile.at[n]) for n in range(2)]
    cross_loads += [copies.start(hbm.ckv.at[:, pl.ds(n * wide, wide)], s.out_tile.at[n]) for n in range(2)]
    first_sum = copies.start(hbm.first_sum, s.grad_act)
    red.second(IN, n_img - 1, 1)
    red.second_if(OUT, n_img - 1)

    def body(part):
        s.activated[part, :] = s.result[part, :].astype(bf16)

    for_rows(rows, 64, body)
    layer_out = copies.start(s.activated, outs.layer_out)
    s.grad_sum, s.grad_query, s.first_sum = s.hidden, s.grad_hidden, s.grad_act
    step.third_norm_back()
    copies.wait(layer_out, *cross_loads)
    s.grad_mixed, s.weights = s.activated, (None,) * 4 + (s.in_tile.at[0], s.in_tile.at[1])
    step.cross_grad()
    sout_load = load_square(3, s.in_tile.at[1])
    copies.wait(*middle_loads)
    flat = n_img * caps * block_len

    def dx(k, c):
        target, part = (im + k) % n_img, pl.ds(c, 1)
        red.sends.send(
            s.images_out.at[target, part],
            outs.image_out.at[im, part],
            dx_send.at[k, c],
            dx_recv.at[k, c],
            (dp, target),
        )

    def caption(c, carry):
        step.cross_caption(c, s.kv.at[:, c], s.kv.at[:, c])
        return carry

    def captions_back(p):
        lax.fori_loop(2 * p, 2 * p + 2, caption, 0, unroll=True)

    def images_back(p):
        part = slice(2 * p, 2 * p + 2)
        length = n_img * 2 * block_len
        value = dot_right(s.kv[:, part, :, 0:wide].reshape(length, wide), s.out_tile[0])
        value = value + dot_right(s.kv[:, part, :, wide : 2 * wide].reshape(length, wide), s.out_tile[1])
        s.images_out[:, part] = value.astype(bf16).reshape(n_img, 2, block_len, wide)

    def square_grad(values, grads, n):
        for m in range(wide // 256):
            cols = slice(m * 256, (m + 1) * 256)
            s.stage_in[0, :, cols] = dot_left(values[...], grads[:, cols]).astype(bf16)
        if n is not None:
            for i in every:
                s.stage_cross[i, :, n * width : (n + 1) * width] = s.stage_in[0, :, i * width : (i + 1) * width]

    def ckv_grad(n):
        at, col = divmod(n * 256, wide)
        part = s.kv[:, :, :, n * 256 : (n + 1) * 256].reshape(flat, 256)
        s.out_tile[at, :, col : col + 256] = dot_left(s.images[...].reshape(flat, wide), part).astype(bf16)

    def give_ckv():
        pieces = []
        for c in red.chips():
            for i in every:
                at, col = divmod(i * 2 * width, wide)
                half = s.out_tile.at[pl.ds(at, 1), :, pl.ds(col, 2 * width)]
                pieces.append(
                    red.give(
                        CKV,
                        c,
                        i,
                        1,
                        half.at[:, tile_ds(2 * c + core, depth, 16), :],
                        half.at[:, tile_ds(2 * c + 1 - core, depth, 16), :],
                    )
                )
        return pieces

    def give_stacked(g, stage, i):
        count = stage.shape[0]
        return [
            piece
            for c in red.chips()
            for piece in red.give_each(
                g,
                c,
                i,
                count,
                stage.at[:, tile_ds(2 * c + core, depth, 16), :],
                stage.at[:, tile_ds(2 * c + 1 - core, depth, 16), :],
            )
        ]

    def give_vec():
        pack_vectors(s.sums, s.bias_sums, s.vectors.at[0], n_dp, depth, inner_dp)
        pieces = []
        for c in red.chips():
            for i in every:
                own = s.vectors.at[:, tile_ds(2 * c + core, VEC_ROWS, 8), :]
                other = s.vectors.at[:, tile_ds(2 * c + 1 - core, VEC_ROWS, 8), :]
                pieces.append(red.give(VEC, c, i, 1, own, other))
        return pieces

    def self_weights(pair):
        step.qkv_grads(pair, s.stage_self)
        for n in range(2):
            i = 2 * pair + n
            s.stage_self[n, :, 3 * width :] = s.stage_in[0, :, i * width : (i + 1) * width]

    captions_back(0)
    images_back(0)
    dx(2, 0)
    dx(1, 0)
    dx(3, 0)
    dx(2, 1)
    captions_back(1)
    images_back(1)
    for i in (2, 3):
        red.first(IN, i, 1)
    dx(1, 1)
    dx(3, 1)
    dx(2, 2)
    captions_back(2)
    images_back(2)
    dx(1, 2)
    dx(3, 2)
    captions_back(3)
    tokens = copies.start(hbm.tokens, s.query)
    images_back(3)
    red.first(OUT, 0, n_img)
    dx(2, 3)
    dx(1, 3)
    square_grad(s.mixed, s.low, 0)
    self_mixed = copies.start(hbm.self_mixed, s.mixed)
    ckv_grad(0)
    ckv_grad(1)
    ckv_grad(2)
    for i in every:
        red.plane(IN, i, 1)
    ckv_grad(3)
    ckv_grad(4)
    ckv_grad(5)
    qkv_loads = [
        copies.start(hbm.qkv.at[:, :, pl.ds(0, 2 * wide)], s.kv.at[0]),
        copies.start(hbm.qkv.at[:, :, pl.ds(2 * wide, wide)], s.kv.at[1, :, :, pl.ds(0, wide)]),
    ]
    red.line(IN, 3)
    copies.wait(first_sum)
    step.second_norm_back()
    weight_loads = [load_square(2, s.in_tile.at[0])]
    red.plane(OUT, 0, n_img)
    for n in range(3):
        red.free_partner(n)
    red.line(OUT, 3)
    red.await_partner(0)
    ckv_given = give_ckv()
    square_grad(s.normed2, s.grad_query, 1)
    normed1 = copies.start(hbm.normed1, s.normed2)
    cross_given = give_stacked(CROSS, s.stage_cross, 0)
    red.line(IN, 2)
    copies.wait(sout_load)
    s.weights = (None,) * 3 + (s.in_tile.at[1],)
    step.self_grad()
    copies.wait(*qkv_loads)
    red.await_partner(1)
    red.given(ckv_given)
    weight_loads += [load_square(n, s.out_tile.at[n]) for n in range(2)]
    for i in every:
        red.second(CKV, i, 1)
    red.given(cross_given)
    red.second(CROSS, 0, n_img)
    dx(3, 3)
    dx(2, 4)
    step.self_attention(0, 2)
    red.line(OUT, 2)
    red.line(IN, 1)
    dx(1, 4)
    step.self_attention(2, 4)
    red.await_partner(2)
    for i in every:
        red.first(CKV, i, 1)
    red.line(OUT, 1)
    dx(3, 4)
    step.self_attention(4, 6)
    red.first(CROSS, 0, n_img)
    red.last(IN, outs.s_in)
    red.last(OUT, outs.s_out)
    red.free_line()
    dx(2, 5)
    step.self_attention(6, 8)
    dx(1, 5)
    copies.wait(self_mixed, normed1, tokens)
    s.self_mixed, s.normed1, s.tokens = s.mixed, s.normed2, s.query
    square_grad(s.self_mixed, s.low, None)
    self_weights(0)
    red.settle(IN)
    self_given = give_stacked(SELF, s.stage_self, 0)
    red.given(self_given)
    self_weights(1)
    self_given2 = give_stacked(SELF, s.stage_self, 2)
    red.second(SELF, 0, 2)
    for i in every:
        red.plane(CKV, i, 1)
    red.given(self_given2)
    red.second(SELF, 2, 2)
    red.await_line()
    red.line(CKV, 3)
    dx(3, 5)
    dx(2, 6)
    copies.wait(*weight_loads)
    step.first_norm_back((s.out_tile.at[0], s.out_tile.at[1], s.in_tile.at[0]))
    copies.start(s.low, outs.token_grads)
    red.plane(CROSS, 0, n_img)
    red.line(CROSS, 3)
    vec_given = give_vec()
    red.line(CKV, 2)
    red.first(SELF, 0, 2)
    red.given(vec_given)
    for i in every:
        red.second(VEC, i, 1)
    red.first(SELF, 2, 2)
    dx(1, 6)
    dx(3, 6)
    dx(2, 7)
    dx(1, 7)
    dx(3, 7)
    red.line(CROSS, 2)
    red.line(CKV, 1)
    for i in every:
        red.first(VEC, i, 1)
    red.line(CROSS, 1)
    red.plane(SELF, 0, 2)
    red.plane(SELF, 2, 2)
    for i in every:
        red.plane(VEC, i, 1)
    red.line(SELF, 3)
    red.line(VEC, 3)
    red.line(SELF, 2)
    red.line(VEC, 2)
    red.line(SELF, 1)
    red.line(VEC, 1)
    red.last(CKV, outs.s_ckv)
    red.last(CROSS, outs.s_cross)
    red.last(SELF, outs.s_self)
    red.last(VEC, outs.s_vec)
    copies.start(s.images_out.at[im], outs.image_out.at[im])
    for c in range(caps):
        for k in range(1, n_img):
            source = (im + n_img - k) % n_img
            block = outs.image_out.at[source, pl.ds(c, 1)]
            pltpu.make_async_remote_copy(
                block, block, dx_send.at[k, c], dx_recv.at[k, c], device_id=(dp, source), device_id_type=MESH
            ).wait_recv()
    red.sends.finish()
    copies.finish()


def back_pass(dims, counts, values):
    inputs, outputs, scratch = back_inputs(dims), back_outputs(dims), back_scratch(dims)
    n_img, caps = dims[1], dims[2]
    dma = pltpu.SemaphoreType.DMA
    any_spec, vmem_spec = pl.BlockSpec(memory_space=pl.ANY), pl.BlockSpec(memory_space=pltpu.VMEM)
    outs = pl.pallas_call(
        functools.partial(back_kernel, dims),
        out_shape=structs_of(outputs),
        in_specs=[pl.BlockSpec(memory_space=pltpu.SMEM)] + [any_spec] * len(inputs),
        out_specs=[any_spec] * 3 + [vmem_spec] * (len(outputs) - 3),
        scratch_shapes=[pltpu.VMEM(*shape) for shape in scratch.values()]
        + [buffer for these in back_buffers(dims) for buffer in these]
        + Reducer.semaphores(len(back_groups(dims)), n_img)
        + [
            pltpu.SemaphoreType.REGULAR((5,)),
            dma((48,)),
            dma((n_img, caps)),
            dma((n_img, caps)),
        ],
        compiler_params=pltpu.CompilerParams(
            collective_id=2, has_side_effects=True, vmem_limit_bytes=63 << 20
        ),
    )(counts, *[values[name] for name in inputs])
    return dict(zip(outputs, outs))


def exit_kernel(dims, *refs):
    n_dp, n_img, caps, depth, width, inner_dp, block_len = dims
    layer_in, token_in, image_in, s_out, s_in, s_cross, s_ckv, s_self, s_vec = refs[:9]
    layer_out, token_grads, image_out, qkv, sout, cq, ckv, cout, w_in, w_out, gains, shifts, bias = refs[9:22]
    copies = Copies(refs[22])
    copies.start(image_in, image_out)
    copies.start(layer_in, layer_out)
    copies.start(token_in, token_grads)
    qkv[...] = s_self[:, 0 : 3 * width]
    sout[...] = s_self[:, 3 * width :]
    cq[...] = s_cross[:, width:]
    cout[...] = s_cross[:, 0:width]
    ckv[...] = s_ckv[...]
    w_in[...] = s_in[...]
    w_out[...] = s_out[...].T
    gains[...] = s_vec[0:3, 0:depth]
    shifts[...] = s_vec[3:13, 0:depth]
    for j in range(inner_dp // LANES):
        bias[pl.ds(j * LANES, LANES)] = s_vec[13 + j]
    copies.finish()


def exit_pass(dims, values):
    n_dp, n_img, caps, depth, width, inner_dp, block_len = dims
    any_spec, vmem_spec = pl.BlockSpec(memory_space=pl.ANY), pl.BlockSpec(memory_space=pltpu.VMEM)
    outputs = back_outputs(dims)
    square = (depth, width)
    small = ((depth, 3 * width), square, square, (depth, 2 * width), square)
    small += (outputs["s_in"][0], (inner_dp, width), (3, depth), (10, depth), (inner_dp,))
    return pl.pallas_call(
        functools.partial(exit_kernel, dims),
        out_shape=structs_of(outputs)[:3] + [jax.ShapeDtypeStruct(shape, f32) for shape in small],
        in_specs=[vmem_spec] * 9,
        out_specs=[any_spec] * 3 + [vmem_spec] * len(small),
        scratch_shapes=[pltpu.SemaphoreType.DMA((3,))],
        compiler_params=pltpu.CompilerParams(vmem_limit_bytes=62 << 20),
    )(*[values[name] for name in outputs])


def layer_norm(values, norm_gain, norm_shift):
    average = jnp.mean(values, axis=-1, keepdims=True)
    centred = values - average
    spread = jnp.mean(centred * centred, axis=-1, keepdims=True)
    return centred * lax.rsqrt(spread + norm_epsilon) * norm_gain + norm_shift


def matmul(left_op, right_op):
    return jnp.dot(left_op, right_op, preferred_element_type=f32)


def matmul_tleft(left_op, right_op):
    return lax.dot_general(
        left_op, right_op, (((0,), (0,)), ((), ())), preferred_element_type=f32
    )


def matmul_tright(left_op, right_op):
    return lax.dot_general(
        left_op, right_op, (((1,), (1,)), ((), ())), preferred_element_type=f32
    )


def column_sums(values):
    return jnp.sum(values.astype(f32), axis=0)


def to_heads(values, captions):
    return values.reshape(captions, -1, HEADS, HEAD)


def probabilities(queries, key_heads, allowed):
    scores = jnp.einsum("cqhd,ckhd->chqk", queries, key_heads, preferred_element_type=f32)
    scores = jnp.where(allowed, scores * HEAD ** (-0.5), masked_value)
    return jax.nn.softmax(scores, axis=-1)


def attention(queries, key_heads, value_heads, allowed):
    probs = probabilities(queries, key_heads, allowed).astype(bf16)
    return jnp.einsum("chqk,ckhd->cqhd", probs, value_heads, preferred_element_type=f32)


def attention_backward(queries, key_heads, value_heads, allowed, grad_mixed):
    probs = probabilities(queries, key_heads, allowed)
    grad_probs = jnp.einsum("cqhd,ckhd->chqk", grad_mixed, value_heads, preferred_element_type=f32)
    inner_term = jnp.sum(probs * grad_probs, axis=-1, keepdims=True)
    grad_scores = (probs * (grad_probs - inner_term)).astype(bf16)
    score_scale = HEAD ** (-0.5)
    grad_queries = (
        jnp.einsum("chqk,ckhd->cqhd", grad_scores, key_heads, preferred_element_type=f32)
        * score_scale
    )
    grad_keys = (
        jnp.einsum("chqk,cqhd->ckhd", grad_scores, queries, preferred_element_type=f32)
        * score_scale
    )
    grad_values = jnp.einsum(
        "chqk,cqhd->ckhd", probs.astype(bf16), grad_mixed, preferred_element_type=f32
    )
    return grad_queries.astype(bf16), grad_keys.astype(bf16), grad_values.astype(bf16)


def local_direct(
    n_dp,
    n_img,
    tokens,
    image_tokens,
    counts,
    mixed,
    cross_kv,
    mlp_in,
    mlp_out,
    norm_gains,
    shifts,
    mlp_bias,
    cotangent,
):
    captions = tokens.shape[0]
    depth = mixed.shape[0]
    width = mlp_out.shape[1]
    inner_dp = mlp_out.shape[0]
    rows_all = captions * SEQ
    dims = (n_dp, n_img, captions, depth, width, inner_dp, image_tokens.shape[1])
    narrow = jnp.pad(jnp.concatenate([norm_gains, shifts]), ((0, 0), (0, LANES - depth)))
    vectors = jnp.concatenate([narrow, mlp_bias.reshape(-1, LANES)])
    token_rows = tokens.reshape(rows_all, MODEL_WIDTH)
    values = entry_pass(
        dims, counts, (vectors, cross_kv, mixed, mlp_in, mlp_out.T), image_tokens, token_rows
    )
    values.update(cot=cotangent.reshape(rows_all, MODEL_WIDTH), tokens=token_rows)
    values.update(qkv=values.pop("qkv").reshape(captions, SEQ, 3 * MODEL_WIDTH))
    results = exit_pass(dims, back_pass(dims, counts, values))
    return tuple(
        value.reshape(like.shape) for value, like in zip(results, (tokens, tokens, image_tokens))
    ) + tuple(results[3:])


def local(
    n_dp,
    n_img,
    tokens,
    image_tokens,
    token_counts,
    self_qkv,
    self_out,
    cross_q,
    cross_kv,
    cross_out,
    mlp_in,
    mlp_out,
    norm_gains,
    shifts,
    mlp_bias,
    cotangent,
):
    captions = tokens.shape[0]
    rows_all = captions * SEQ
    block_len = image_tokens.shape[1]
    width = self_out.shape[1]
    depth = self_out.shape[0]
    inner_dp = mlp_out.shape[0]
    direct = n_dp == 8 and depth % 16 == 0 and captions * n_img == image_tokens.shape[0]
    counts = lax.dynamic_slice_in_dim(token_counts, lax.axis_index("img") * captions, captions)

    mixed = jnp.concatenate([self_qkv, self_out, cross_q, cross_out], axis=1)
    if direct:
        return local_direct(
            n_dp,
            n_img,
            tokens,
            image_tokens,
            counts,
            mixed,
            cross_kv,
            mlp_in,
            mlp_out,
            norm_gains,
            shifts,
            mlp_bias,
            cotangent,
        )
    vectors = jnp.concatenate([norm_gains.reshape(-1), shifts.reshape(-1), mlp_bias])

    def everything(block, first, then, axes):
        return lax.all_gather(
            lax.all_gather(block, first, axis=axes[0], tiled=True), then, axis=axes[1], tiled=True
        )

    mixed_full = lax.all_gather(
        lax.all_gather(mixed, "dp", axis=0, tiled=True), "img", axis=0, tiled=False
    )
    ckv_w = everything(cross_kv, "img", "dp", (1, 0))
    in_w = everything(mlp_in, "img", "dp", (1, 0))
    outm_t = everything(mlp_out, "img", "dp", (1, 0)).T
    vec_full = lax.all_gather(vectors, "dp", axis=0, tiled=False)
    image_own = lax.all_to_all(
        image_tokens.reshape((n_img, captions) + image_tokens.shape[1:]), "img", 0, 0, tiled=True
    )

    def columns(start, size):
        return (
            mixed_full[:, :, start * width : (start + size) * width]
            .transpose(1, 0, 2)
            .reshape(MODEL_WIDTH, size * MODEL_WIDTH)
        )

    qkv_w, sout_w, cq_w, cout_w = columns(0, 3), columns(3, 1), columns(4, 1), columns(5, 1)
    gain_rows = vec_full[:, : 3 * depth].reshape(n_dp, 3, depth).transpose(1, 0, 2).reshape(3, -1)
    shift_rows = (
        vec_full[:, 3 * depth : 13 * depth]
        .reshape(n_dp, 10, depth)
        .transpose(1, 0, 2)
        .reshape(10, -1)
    )
    inner_bias = vec_full[:, 13 * depth :].reshape(-1)

    zero_row = jnp.zeros((MODEL_WIDTH,), f32)
    rows = tokens.reshape(rows_all, MODEL_WIDTH).astype(f32)
    normed1 = layer_norm(rows, gain_rows[0], shift_rows[0]).astype(bf16)
    mixed_qkv = (
        matmul(normed1, qkv_w) + jnp.concatenate([shift_rows[3], zero_row, shift_rows[4]])
    ).astype(bf16)
    self_queries, self_keys, self_values = [
        to_heads(mixed_qkv[:, n * MODEL_WIDTH : (n + 1) * MODEL_WIDTH], captions) for n in range(3)
    ]
    places = jnp.arange(SEQ, dtype=jnp.int32)
    causal = (places[None, :] <= places[:, None])[None, None]
    self_mixed = attention(self_queries, self_keys, self_values, causal)
    self_mixed = self_mixed.reshape(rows_all, MODEL_WIDTH).astype(bf16)
    first_sum = rows + matmul(self_mixed, sout_w) + shift_rows[5]
    normed2 = layer_norm(first_sum, gain_rows[1], shift_rows[1]).astype(bf16)
    cross_query = (matmul(normed2, cq_w) + shift_rows[6]).astype(bf16)
    cross_queries = to_heads(cross_query, captions)

    image_len = n_img * block_len
    image_rows = image_own.reshape(n_img * captions * block_len, MODEL_WIDTH)
    image_kv = (matmul(image_rows, ckv_w) + jnp.concatenate([zero_row, shift_rows[7]])).astype(bf16)

    def by_caption(values):
        return (
            values.reshape(n_img, captions, block_len, HEADS, HEAD)
            .transpose(1, 0, 2, 3, 4)
            .reshape(captions, image_len, HEADS, HEAD)
        )

    def by_place(values):
        return (
            values.reshape(captions, n_img, block_len, MODEL_WIDTH)
            .transpose(1, 0, 2, 3)
            .reshape(-1, MODEL_WIDTH)
        )

    cross_keys = by_caption(image_kv[:, :MODEL_WIDTH])
    cross_values = by_caption(image_kv[:, MODEL_WIDTH:])
    valid = (jnp.arange(image_len, dtype=jnp.int32)[None, :] < counts[:, None])[:, None, None, :]
    cross_mixed = attention(cross_queries, cross_keys, cross_values, valid)
    cross_mixed = cross_mixed.reshape(rows_all, MODEL_WIDTH).astype(bf16)
    second_sum = first_sum + matmul(cross_mixed, cout_w) + shift_rows[8]
    normed3 = layer_norm(second_sum, gain_rows[2], shift_rows[2]).astype(bf16)
    hidden = matmul(normed3, in_w) + inner_bias
    activated = jax.nn.gelu(hidden, approximate=False).astype(bf16)
    result = second_sum + matmul_tright(activated, outm_t) + shift_rows[9]
    layer_out = result.reshape(tokens.shape).astype(bf16)

    grad_low3 = cotangent.reshape(rows_all, MODEL_WIDTH)
    g_outm_t = matmul_tleft(grad_low3, activated)
    g_shift9 = column_sums(grad_low3)
    grad_act = matmul(grad_low3, outm_t)
    _, gelu_pull = jax.vjp(lambda pre_act: jax.nn.gelu(pre_act, approximate=False), hidden)
    grad_hidden = gelu_pull(grad_act)[0].astype(bf16)
    g_in = matmul_tleft(normed3, grad_hidden)
    g_inner_bias = column_sums(grad_hidden)
    grad_normed3 = matmul_tright(grad_hidden, in_w)
    _, norm_pull3 = jax.vjp(layer_norm, second_sum, gain_rows[2], shift_rows[2])
    grad_second_ln, g_gain2, g_shift2 = norm_pull3(grad_normed3)
    grad_second = grad_low3.astype(f32) + grad_second_ln
    grad_low2 = grad_second.astype(bf16)
    g_cout = matmul_tleft(cross_mixed, grad_low2)
    g_shift8 = column_sums(grad_low2)
    grad_cross_mixed = to_heads(matmul_tright(grad_low2, cout_w).astype(bf16), captions)
    grad_query, grad_ckeys, grad_cvalues = attention_backward(
        cross_queries, cross_keys, cross_values, valid, grad_cross_mixed
    )
    grad_query = grad_query.reshape(rows_all, MODEL_WIDTH)
    g_cq = matmul_tleft(normed2, grad_query)
    g_shift6 = column_sums(grad_query)
    grad_normed2 = matmul_tright(grad_query, cq_w)
    grad_value_rows = by_place(grad_cvalues)
    grad_image_kv = jnp.concatenate([by_place(grad_ckeys), grad_value_rows], axis=1)
    g_ckv = matmul_tleft(image_rows, grad_image_kv)
    g_shift7 = column_sums(grad_value_rows)
    image_grads = matmul_tright(grad_image_kv, ckv_w).astype(bf16).reshape(image_own.shape)
    _, norm_pull2 = jax.vjp(layer_norm, first_sum, gain_rows[1], shift_rows[1])
    grad_first_ln, g_gain1, g_shift1 = norm_pull2(grad_normed2)
    grad_first = grad_second + grad_first_ln
    grad_low1 = grad_first.astype(bf16)
    g_sout = matmul_tleft(self_mixed, grad_low1)
    g_shift5 = column_sums(grad_low1)
    grad_self_mixed = to_heads(matmul_tright(grad_low1, sout_w).astype(bf16), captions)
    grad_qkv = jnp.concatenate(
        [
            part.reshape(rows_all, MODEL_WIDTH)
            for part in attention_backward(
                self_queries, self_keys, self_values, causal, grad_self_mixed
            )
        ],
        axis=1,
    )
    g_qkv = matmul_tleft(normed1, grad_qkv)
    qkv_sums = column_sums(grad_qkv)
    g_shift3, g_shift4 = qkv_sums[:MODEL_WIDTH], qkv_sums[2 * MODEL_WIDTH :]
    grad_normed1 = matmul_tright(grad_qkv, qkv_w)
    _, norm_pull1 = jax.vjp(layer_norm, rows, gain_rows[0], shift_rows[0])
    grad_rows_ln, g_gain0, g_shift0 = norm_pull1(grad_normed1)
    token_grads = (grad_first + grad_rows_ln).reshape(tokens.shape).astype(bf16)
    g_vector_rows = jnp.stack(
        [
            g_gain0,
            g_gain1,
            g_gain2,
            g_shift0,
            g_shift1,
            g_shift2,
            g_shift3,
            g_shift4,
            g_shift5,
            g_shift6,
            g_shift7,
            g_shift8,
            g_shift9,
        ]
    )

    def scattered(grad):
        tall = lax.psum_scatter(grad, "dp", scatter_dimension=0, tiled=True)
        return lax.psum_scatter(tall, "img", scatter_dimension=1, tiled=True)

    s_qkv, s_sout, s_cq, s_ckv, s_cout, s_in, s_outm = [
        scattered(g) for g in (g_qkv, g_sout, g_cq, g_ckv, g_cout, g_in, g_outm_t.T)
    ]
    s_rows, s_inner = lax.psum(
        (
            lax.psum_scatter(g_vector_rows, "dp", scatter_dimension=1, tiled=True),
            lax.psum_scatter(g_inner_bias, "dp", scatter_dimension=0, tiled=True),
        ),
        "img",
    )
    image_out = lax.all_to_all(image_grads, "img", 0, 0, tiled=True).reshape(image_tokens.shape)
    return (
        layer_out,
        token_grads,
        image_out,
        s_qkv,
        s_sout,
        s_cq,
        s_ckv,
        s_cout,
        s_in,
        s_outm,
        s_rows[:3],
        s_rows[3:],
        s_inner,
    )


def solution(mesh):
    caption_rows = P(("dp", "img"), None, None)
    weight = P("dp", "img")
    vector = P(None, "dp")
    in_specs = (caption_rows, P("dp", "img", None), P("dp")) + (weight,) * 7
    in_specs += (vector, vector, P("dp"), caption_rows)
    out_specs = (caption_rows, caption_rows, P("dp", "img", None)) + (weight,) * 7
    out_specs += (vector, vector, P("dp"))
    return jax.shard_map(
        functools.partial(local, mesh.shape["dp"], mesh.shape["img"]),
        mesh=mesh,
        in_specs=in_specs,
        out_specs=out_specs,
        check_vma=False,
    )
```
